128 devices in a mesh: lat: 16 (over y, z_hi, core), chan: 8 (over z_lo, x).
Axes of the slice: x: 4, y: 4, z: 4 (z_hi: 2, z_lo: 2; z = z_hi * 2 + z_lo), core: 2. Of those that a mesh axis runs over, the one named last changes fastest.
Arguments:
- state: bfloat16 [64, 512, 1024], P('lat', None, 'chan'), may hold values from -15 to 15
- background: bfloat16 [64, 512, 1024], P('lat', None, 'chan'), may hold values from -15.5 to 15.5
- gain: float32 [1024], replicated, may hold values from 0.5 to 2
- w_query: bfloat16 [1024, 1024], P(None, 'chan'), may hold values from -0.2 to 0.2
- w_key: bfloat16 [1024, 1024], P(None, 'chan'), may hold values from -5 to 5
- w_value: bfloat16 [1024, 1024], P(None, 'chan'), may hold values from -0.1875 to 0.1875
- w_out: bfloat16 [1024, 1024], P('chan'), may hold values from -0.75 to 0.75
- decoder: bfloat16 [1024, 69], P('chan'), may hold values from -0.1875 to 0.1875
- interp: bfloat16 [16, 8, 16, 16, 128, 128], P('lat', 'chan'), may hold values from -0.5 to 0.5
- obs_values: bfloat16 [16, 8, 16, 16, 128], P('lat', 'chan'), may hold values from -6 to 6
- tile_index: int32 [16, 8, 16, 16], P('lat', 'chan'), may hold values from 0 to 1103
- block_count: int32 [16, 8, 16], P('lat', 'chan'), may hold values from 1 to 16, as said below
Outputs:
- misfit: float32 [16, 8, 16, 16, 128], P(None, 'chan', 'lat')
- gradient: float32 [64, 512, 1024], P('lat', None, 'chan')
The draws below stay inside these ranges and needn't reach their ends.
Inputs may be any that keep to these rules, and one draw needn't show every extreme that they name: `tile_index`: A tile index n names variable n // 16 and the run n % 16 of 128 tokens of the target band. Live slots are the first block_count ones; every draw has a target band that receives 16 blocks from every owner and channel group.
All inputs are finite; a program needn't handle non-finite values.
Results may differ from the reference program's by a relative error of at most 0.02.
The reference program's roundings to bfloat16 on the way (of `normed`, `mixed_heads`, `updated`, `rounded`, `grad_mixed`, `grad_scores` and `grad_queries`) count: a program that leaves them out, or rounds other values in their place, can miss the bound.
Values may be sent and summed in bfloat16 or wider, within the bound.
A program may use at most 128 MiB of HBM per device.

```python
import math
import jax
import jax.numpy as jnp
from jax import lax

D = 1024
HEADS = 16
HD = 64
VARS = 69
OBS = 128
CELLS = 128
WC = 256
RB = 4
NC = 512
BSLOT = 16
NR = 64
TPB = 16
N_LAT = 16
N_CHAN = 8


def attention_pair(key):
    base = jnp.clip(jax.random.normal(jax.random.fold_in(key, 101), (D, D), jnp.float32), -5.0, 5.0) * D ** (-0.5)
    other = jnp.clip(jax.random.normal(jax.random.fold_in(key, 102), (D, D), jnp.float32), -5.0, 5.0) * D ** (-0.5)
    key_matrix = other
    return (jnp.clip(base, -0.19921875, 0.19921875), jnp.clip(key_matrix, -5.0, 5.0))


def draw_w_query(key, part):
    return attention_pair(key)[0].astype(jnp.bfloat16)


def draw_w_key(key, part):
    return attention_pair(key)[1].astype(jnp.bfloat16)


def state_field(key):
    base = jnp.clip(jax.random.normal(jax.random.fold_in(key, 201), (NR, NC, D), jnp.float32), -5.0, 5.0)
    return base


def draw_state(key, part):
    return state_field(key).astype(jnp.bfloat16)


def draw_background(key, part):
    offset = jnp.clip(jax.random.normal(jax.random.fold_in(key, 211), (NR, NC, D), jnp.float32), -4.0, 4.0) * 0.04
    return jnp.clip(state_field(key) + offset, -15.5, 15.5).astype(jnp.bfloat16)


def draw_block_count(key, part):
    counts = jax.random.randint(jax.random.fold_in(key, 301), (N_LAT, N_CHAN, N_LAT), 1, BSLOT // 2 + 1)
    busiest = jax.random.randint(jax.random.fold_in(key, 302), (), 0, N_LAT)
    chosen = jnp.arange(N_LAT, dtype=jnp.int32)[None, None, :] == busiest
    return jnp.where(chosen, BSLOT, counts).astype(jnp.int32)


def set_ends(result, stream_key, smallest, top_value):
    index_at = [jax.random.randint(jax.random.fold_in(stream_key, axis), (), 0, length) for axis, length in enumerate(result.shape)]
    main_axis = result.shape.index(max(result.shape))
    neighbour = index_at[:main_axis] + [(index_at[main_axis] + 1) % result.shape[main_axis]] + index_at[main_axis + 1:]
    return result.at[tuple(index_at)].set(smallest).at[tuple(neighbour)].set(top_value)


def level_of(stream_key, extent, shards, least, top_value):
    loudness, own = 1.0, jax.random.fold_in(stream_key, 6)
    for axis_at, blocks in shards:
        heights = jnp.exp(jax.random.uniform(jax.random.fold_in(own, axis_at), (blocks,), jnp.float32, least / len(shards), top_value / len(shards)))
        loudness = loudness * jnp.repeat(heights, extent[axis_at] // blocks).reshape([-1 if axis == axis_at else 1 for axis in range(len(extent))])
    return loudness


def noise(stream_key, shape, deviation, most, cuts=(), kind=jnp.bfloat16):
    level = level_of(stream_key, shape, cuts, -0.22, 0.18) if cuts else 1.0
    result = jax.random.normal(stream_key, shape, jnp.float32) * deviation * level
    return jnp.minimum(jnp.maximum(result, -most), most).astype(kind)


def setup_inputs(seed: int = 0) -> dict:
    arg_keys = jax.random.split(jax.random.key(seed), 13)
    state = draw_state(jax.random.fold_in(arg_keys[12], 71), 0)
    background = draw_background(jax.random.fold_in(arg_keys[12], 71), 0)
    gain = jnp.clip(jnp.exp(jax.random.uniform(arg_keys[2], (D,), jnp.float32, math.log(0.5), math.log(2.0))), 0.5, 2.0)
    w_query = draw_w_query(jax.random.fold_in(arg_keys[12], 71), 0)
    w_key = draw_w_key(jax.random.fold_in(arg_keys[12], 71), 0)
    w_value = noise(arg_keys[5], (D, D), D ** -0.5, 0.1875, ((1, 8),))
    w_out = noise(arg_keys[6], (D, D), HD ** -0.5, 0.75, ((0, 8),))
    decoder = noise(arg_keys[7], (D, VARS), D ** -0.5, 0.1875, ((0, 8),))
    interp = noise(arg_keys[8], (N_LAT, N_CHAN, N_LAT, BSLOT, OBS, CELLS), CELLS ** -0.5, 0.5, ((0, 16), (1, 8)))
    obs_values = noise(arg_keys[9], (N_LAT, N_CHAN, N_LAT, BSLOT, OBS), 1.0, 6.0, ((0, 16), (1, 8)))
    tile_index = set_ends(jax.random.randint(arg_keys[10], (N_LAT, N_CHAN, N_LAT, BSLOT), 0, VARS * TPB), jax.random.fold_in(arg_keys[10], 1), 0, (VARS * TPB) - 1).astype(jnp.int32)
    block_count = draw_block_count(jax.random.fold_in(arg_keys[12], 71), 0)
    return dict(state=state, background=background, gain=gain, w_query=w_query, w_key=w_key, w_value=w_value, w_out=w_out, decoder=decoder, interp=interp, obs_values=obs_values, tile_index=tile_index, block_count=block_count)


EPSILON = 1e-05
NEGATIVE = -1e+30

def normalize(state_rows):
    average = lax.optimization_barrier(jnp.mean(state_rows, axis=-1, keepdims=True))
    centred = state_rows - average
    variance = lax.optimization_barrier(jnp.mean(centred * centred, axis=-1, keepdims=True))
    inverse = lax.rsqrt(variance + EPSILON)
    return (centred * inverse, inverse)

def window_keys(padded, rows_band):
    stacked = jnp.stack([padded[0:rows_band], padded[1:rows_band + 1], padded[2:rows_band + 2]], axis=1)
    shaped = stacked.reshape(rows_band, 3, NC // WC, WC, stacked.shape[3], stacked.shape[4])
    shaped = jnp.transpose(shaped, (0, 2, 1, 3, 4, 5))
    return shaped.reshape(rows_band, NC // WC, 3 * WC, stacked.shape[3], stacked.shape[4])

def key_mask(valid_rows):
    rows_band = valid_rows.shape[0] - 2
    triple = jnp.stack([valid_rows[0:rows_band], valid_rows[1:rows_band + 1], valid_rows[2:rows_band + 2]], axis=1)
    spread = jnp.repeat(triple, WC, axis=1)
    return spread[:, None, None, None, :]

def attend_forward(queries, keys_win, values_win, key_valid):
    scores = jnp.einsum('rwihd,rwjhd->rwhij', queries.astype(jnp.float32), keys_win.astype(jnp.float32)) * HD ** (-0.5)
    scores = jnp.where(key_valid, scores, NEGATIVE)
    highest = lax.optimization_barrier(jnp.max(scores, axis=-1, keepdims=True))
    exponent = jnp.exp(scores - highest)
    attention = exponent / lax.optimization_barrier(jnp.sum(exponent, axis=-1, keepdims=True))
    attention_low = attention.astype(jnp.bfloat16)
    mixed_heads = jnp.einsum('rwhij,rwjhd->rwihd', attention_low.astype(jnp.float32), values_win.astype(jnp.float32)).astype(jnp.bfloat16)
    return (attention, attention_low, mixed_heads)

def attend_backward(queries, keys_win, values_win, attention, attention_low, grad_mixed):
    grad_probs = jnp.einsum('rwihd,rwjhd->rwhij', grad_mixed.astype(jnp.float32), values_win.astype(jnp.float32))
    row_delta = lax.optimization_barrier(jnp.sum(attention * grad_probs, axis=-1, keepdims=True))
    grad_scores = (attention * (grad_probs - row_delta) * HD ** (-0.5)).astype(jnp.bfloat16)
    grad_queries = jnp.einsum('rwhij,rwjhd->rwihd', grad_scores.astype(jnp.float32), keys_win.astype(jnp.float32)).astype(jnp.bfloat16)
    grad_keys = jnp.einsum('rwhij,rwihd->rwjhd', grad_scores.astype(jnp.float32), queries.astype(jnp.float32))
    grad_values = jnp.einsum('rwhij,rwihd->rwjhd', attention_low.astype(jnp.float32), grad_mixed.astype(jnp.float32))
    return (grad_queries, grad_keys, grad_values)

def unwindow(windowed, rows_band):
    width_heads = windowed.shape[3] * windowed.shape[4]
    shaped = windowed.reshape(rows_band, NC // WC, 3, WC, width_heads)
    shaped = jnp.transpose(shaped, (0, 2, 1, 3, 4)).reshape(rows_band, 3, NC, width_heads)
    summed = jnp.zeros((rows_band + 2, NC, width_heads), shaped.dtype)
    for offset in range(3):
        summed = summed.at[offset:offset + rows_band].add(shaped[:, offset])
    return summed

def settle(band_parts, tokens_all):
    main_rows = band_parts[:, 1:RB + 1]
    above_rows = band_parts[:, 0]
    below_rows = band_parts[:, RB + 1]
    zero_row = jnp.zeros_like(above_rows[:1])
    main_rows = main_rows.at[:, RB - 1].add(jnp.concatenate([above_rows[1:], zero_row], axis=0))
    main_rows = main_rows.at[:, 0].add(jnp.concatenate([zero_row, below_rows[:-1]], axis=0))
    return main_rows.reshape(tokens_all, D).astype(jnp.bfloat16)

def round_trip(values_f):
    return lax.optimization_barrier(values_f.astype(jnp.bfloat16)).astype(jnp.float32)

def reference(state, background, gain, w_query, w_key, w_value, w_out, decoder, interp, obs_values, tile_index, block_count):
    tokens_all = NR * NC
    state_wide = state.astype(jnp.float32).reshape(tokens_all, D)
    hat_rows, inverse = normalize(state_wide)
    normed = (hat_rows * gain).astype(jnp.bfloat16)
    queries = jnp.dot(normed, w_query, preferred_element_type=jnp.float32).astype(jnp.bfloat16)
    keys_all = jnp.dot(normed, w_key, preferred_element_type=jnp.float32).astype(jnp.bfloat16)
    values_all = jnp.dot(normed, w_value, preferred_element_type=jnp.float32).astype(jnp.bfloat16)
    pad_rows = ((1, 1), (0, 0), (0, 0), (0, 0))
    key_pad = jnp.pad(keys_all.reshape(NR, NC, HEADS, HD), pad_rows)
    value_pad = jnp.pad(values_all.reshape(NR, NC, HEADS, HD), pad_rows)
    row_ids = jnp.arange(NR + 2, dtype=jnp.int32)
    valid_rows = (row_ids >= 1) & (row_ids <= NR)
    query_bands = queries.reshape(N_LAT, RB, NC // WC, WC, HEADS, HD)

    def band_setup(band_id):
        first_row = (band_id * RB).astype(jnp.int32)
        keys_win = window_keys(lax.dynamic_slice_in_dim(key_pad, first_row, RB + 2, 0), RB)
        values_win = window_keys(lax.dynamic_slice_in_dim(value_pad, first_row, RB + 2, 0), RB)
        band_valid = key_mask(lax.dynamic_slice_in_dim(valid_rows, first_row, RB + 2, 0))
        return (keys_win, values_win, band_valid)

    def band_forward(band_id):
        keys_win, values_win, band_valid = band_setup(band_id)
        return attend_forward(query_bands[band_id], keys_win, values_win, band_valid)[2]
    band_ids_all = jnp.arange(N_LAT, dtype=jnp.int32)
    mixed_heads = lax.map(band_forward, band_ids_all).reshape(tokens_all, D)
    group_width = D // N_CHAN
    attn_sum = jnp.zeros((tokens_all, D), jnp.float32)
    for member in range(N_CHAN):
        group_cols = slice(member * group_width, (member + 1) * group_width)
        attn_sum = attn_sum + round_trip(jnp.dot(mixed_heads[:, group_cols], w_out[group_cols], preferred_element_type=jnp.float32))
    updated = (state_wide + attn_sum).astype(jnp.bfloat16)
    fields = lax.dot_general(decoder, updated, (((0,), (1,)), ((), ())), preferred_element_type=jnp.float32)
    rounded = fields.astype(jnp.bfloat16)
    tiles_band = jnp.transpose(rounded.reshape(VARS, N_LAT, RB * NC), (1, 0, 2)).reshape(N_LAT, VARS * TPB, CELLS)
    band_ids = jnp.arange(N_LAT, dtype=jnp.int32)[None, :, None]

    def owner_step(grad_tiles, owner_id):
        weights = interp[owner_id].astype(jnp.float32)
        owner_tiles = tile_index[owner_id]
        picked = tiles_band[band_ids, owner_tiles].astype(jnp.float32)
        predicted = jnp.einsum('gbsok,gbsk->gbso', weights, picked)
        live_slot = jnp.arange(BSLOT, dtype=jnp.int32)[None, None, :] < block_count[owner_id][..., None]
        misfit = jnp.where(live_slot[..., None], predicted - obs_values[owner_id].astype(jnp.float32), 0.0)
        adjoint = jnp.einsum('gbsok,gbso->gbsk', weights, round_trip(misfit))
        flat_ids = (band_ids * (VARS * TPB) + owner_tiles).reshape(-1)
        grad_tiles = grad_tiles.at[flat_ids].add(adjoint.reshape(-1, CELLS))
        return (grad_tiles, misfit)
    grad_tiles, misfit = lax.scan(owner_step, jnp.zeros((N_LAT * VARS * TPB, CELLS), jnp.float32), band_ids_all)
    grad_field = jnp.transpose(grad_tiles.reshape(N_LAT, VARS, RB * NC), (1, 0, 2)).reshape(VARS, tokens_all)
    grad_update = lax.dot_general(grad_field, decoder.astype(jnp.float32), (((0,), (1,)), ((), ())), precision=lax.Precision.HIGHEST)
    grad_low = grad_update.astype(jnp.bfloat16)
    grad_mixed = jnp.dot(grad_low, w_out.T, preferred_element_type=jnp.float32).astype(jnp.bfloat16)
    grad_mixed_bands = grad_mixed.reshape(N_LAT, RB, NC // WC, WC, HEADS, HD)

    def band_backward(band_id):
        keys_win, values_win, band_valid = band_setup(band_id)
        attention, attention_low, mixed_band = attend_forward(query_bands[band_id], keys_win, values_win, band_valid)
        grad_queries, grad_keys, grad_values = attend_backward(query_bands[band_id], keys_win, values_win, attention, attention_low, grad_mixed_bands[band_id])
        return (grad_queries, unwindow(grad_keys, RB), unwindow(grad_values, RB))
    grad_queries, key_parts, value_parts = lax.map(band_backward, band_ids_all)
    grad_queries = grad_queries.reshape(tokens_all, D)
    grad_keys = settle(key_parts, tokens_all)
    grad_values = settle(value_parts, tokens_all)
    grad_normed = jnp.zeros((tokens_all, D), jnp.float32)
    for member in range(N_CHAN):
        group_cols = slice(member * group_width, (member + 1) * group_width)
        group_part = jnp.dot(grad_queries[:, group_cols], w_query[:, group_cols].T, preferred_element_type=jnp.float32)
        group_part = group_part + jnp.dot(grad_keys[:, group_cols], w_key[:, group_cols].T, preferred_element_type=jnp.float32)
        group_part = group_part + jnp.dot(grad_values[:, group_cols], w_value[:, group_cols].T, preferred_element_type=jnp.float32)
        grad_normed = grad_normed + round_trip(group_part)
    grad_hat = grad_normed * gain
    grad_norm = (grad_hat - lax.optimization_barrier(jnp.mean(grad_hat, axis=-1, keepdims=True)) - hat_rows * lax.optimization_barrier(jnp.mean(grad_hat * hat_rows, axis=-1, keepdims=True))) * inverse
    gradient = state_wide - background.astype(jnp.float32).reshape(tokens_all, D) + grad_update + grad_norm
    return (misfit, gradient.reshape(NR, NC, D))
```

```python
import functools

import jax
import jax.numpy as jnp
from jax import lax
from jax.experimental import pallas as pl
from jax.experimental.pallas import tpu as pltpu
from jax.sharding import PartitionSpec as P

D = 1024
HD = 64
VARS = 69
EPSILON = 1e-05
VP = 80
T = 256
G = 8
L = 16
BIG = 1e30
MESH = pl.DeviceIdType.MESH
BF = jnp.bfloat16
F32 = jnp.float32
VMEM_LIMIT = 62 * 1024 * 1024


def nn(a, b):
    return lax.dot_general(a, b, (((1,), (0,)), ((), ())), preferred_element_type=F32)


def nt(a, b):
    return lax.dot_general(a, b, (((1,), (1,)), ((), ())), preferred_element_type=F32)


def place():
    b = lax.axis_index("lat")
    c = lax.axis_index("chan")
    k = b % 2
    x = c % 4
    r = x + k * (3 - 2 * x)
    return b, c, r, c // 4, k


def row_of(c, k):
    x = c % 4
    return x + k * (3 - 2 * x)


def neighbours():
    b, c, r, w, k = place()
    inner_up = (r > 0).astype(jnp.int32)
    inner_down = (r < 3).astype(jnp.int32)
    up = (b - 1 + inner_up, c + inner_up * (2 * k - 1))
    down = (b + 1 - inner_down, c + inner_down * (1 - 2 * k))
    row = b * 4 + r
    return up, down, row > 0, row < 4 * L - 1


def chan_peer(i):
    b, c, _, _, _ = place()
    return (b, (c + i) % G)


def lat_peer(i):
    b, c, _, _, _ = place()
    return ((b + i) % L, c)


def greet(chan=True, lat=False, rows=False):
    barrier = pltpu.get_barrier_semaphore()
    count = 0
    if chan:
        for i in range(1, G):
            pl.semaphore_signal(barrier, inc=1, device_id=chan_peer(i), device_id_type=MESH)
            count += 1
    if lat:
        for i in range(1, L):
            pl.semaphore_signal(barrier, inc=1, device_id=lat_peer(i), device_id_type=MESH)
            count += 1
    pl.semaphore_wait(barrier, count)


def remote(src, dst, ss, rs, dev):
    return pltpu.make_async_remote_copy(
        src_ref=src, dst_ref=dst, send_sem=ss, recv_sem=rs, device_id=dev, device_id_type=MESH
    )


def call(kernel, out_shape, in_specs, out_specs, scratch, cid, name, args):
    return pl.pallas_call(
        kernel,
        out_shape=out_shape,
        in_specs=in_specs,
        out_specs=out_specs,
        scratch_shapes=scratch,
        compiler_params=pltpu.CompilerParams(
            collective_id=cid, has_side_effects=cid is not None, vmem_limit_bytes=VMEM_LIMIT
        ),
        name=name,
    )(*args)


VM = pl.BlockSpec(memory_space=pltpu.VMEM)
ANY = pl.BlockSpec(memory_space=pl.ANY)
DMA = pltpu.SemaphoreType.DMA


def sds(shape, dtype):
    return jax.ShapeDtypeStruct(shape, dtype)


def gather_kernel(
    state, w3, wo, dec, idx, zero, x_out, w_out, o_out, d_out, i_out,
    s_state, r_state, s_w, r_w, s_o, r_o, s_d, r_d, s_i, r_i, s_h, r_h, f_w, g_w, f_o, g_o, loc,
):
    b, c, r, w, k = place()
    up, down, has_up, has_down = neighbours()
    greet(chan=True, lat=True)
    partner = (b + 1 - 2 * k, c)

    local = [
        pltpu.make_async_copy(state.at[r, pl.ds(w * T, T)], x_out.at[1, c], loc.at[0]),
        pltpu.make_async_copy(w3, w_out.at[c], loc.at[1]),
        pltpu.make_async_copy(wo, o_out.at[c], loc.at[2]),
        pltpu.make_async_copy(dec, d_out.at[c], loc.at[3]),
        pltpu.make_async_copy(idx.at[b], i_out.at[b], loc.at[4]),
    ]
    for copy in local:
        copy.start()

    @pl.when(jnp.logical_not(has_up))
    def _():
        copy = pltpu.make_async_copy(zero, x_out.at[0], loc.at[5])
        copy.start()
        copy.wait()

    @pl.when(jnp.logical_not(has_down))
    def _():
        copy = pltpu.make_async_copy(zero, x_out.at[2], loc.at[5])
        copy.start()
        copy.wait()

    send = []
    states, weights, outs = {}, {}, {}
    for i in range(1, G):
        _, pc = chan_peer(i)
        pr = row_of(pc, k)
        copy = remote(state.at[pr, pl.ds((pc // 4) * T, T)], x_out.at[1, c], s_state.at[i], r_state.at[i], (b, pc))
        copy.start()
        states[i] = copy
    half = pl.ds(k * 512, 512)
    ohalf = pl.ds(k * 64, 64)
    for i in range(1, G):
        copy = remote(w3.at[half], w_out.at[c, half], s_w.at[i], r_w.at[i], chan_peer(i))
        copy.start()
        weights[i] = copy
    for i in range(1, L):
        dev = lat_peer(i)
        copy = remote(idx.at[dev[0]], i_out.at[b], s_i.at[i], r_i.at[i], dev)
        copy.start()
        send.append(copy)
    for i in range(1, G):
        copy = remote(wo.at[ohalf], o_out.at[c, ohalf], s_o.at[i], r_o.at[i], chan_peer(i))
        copy.start()
        outs[i] = copy
        copy = remote(dec, d_out.at[c], s_d.at[i], r_d.at[i], chan_peer(i))
        copy.start()
        send.append(copy)

    def halo(g, sem, start):
        @pl.when(has_up)
        def _():
            copy = remote(x_out.at[1, g], x_out.at[2, g], s_h.at[0, sem], r_h.at[0, sem], up)
            copy.start() if start else copy.wait_send()

        @pl.when(has_down)
        def _():
            copy = remote(x_out.at[1, g], x_out.at[0, g], s_h.at[1, sem], r_h.at[1, sem], down)
            copy.start() if start else copy.wait_send()

    local[0].wait()
    halo(c, 0, True)
    for i in range(1, G):
        states[i].wait_recv()
        halo((c + G - i) % G, i, True)
    forward = []
    for i in range(1, G):
        g = (c + G - i) % G
        weights[i].wait_recv()
        copy = remote(w_out.at[g, half], w_out.at[g, half], f_w.at[i], g_w.at[i], partner)
        copy.start()
        forward.append(copy)
    for i in range(1, G):
        g = (c + G - i) % G
        outs[i].wait_recv()
        copy = remote(o_out.at[g, ohalf], o_out.at[g, ohalf], f_o.at[i], g_o.at[i], partner)
        copy.start()
        forward.append(copy)
    for copy in forward:
        copy.wait()
    for copy in send:
        copy.wait()
    for i in range(1, G):
        states[i].wait_send()
        weights[i].wait_send()
        outs[i].wait_send()
    for i in range(G):
        halo((c + G - i) % G, i, False)

        @pl.when(has_down)
        def _():
            remote(x_out.at[1, 0], x_out.at[2, 0], s_h.at[0, i], r_h.at[0, i], up).wait_recv()

        @pl.when(has_up)
        def _():
            remote(x_out.at[1, 0], x_out.at[0, 0], s_h.at[1, i], r_h.at[1, i], down).wait_recv()

    for copy in local[1:]:
        copy.wait()


def gather(state, w3, wo, dec, idx):
    zero = jnp.zeros((G, T, 128), BF)
    shapes = (
        sds((3, G, T, 128), BF),
        sds((G, D, 384), BF),
        sds((G, 128, D), BF),
        sds((G, VP, 128), BF),
        sds((L, 16, 128), jnp.int32),
    )
    seven, fifteen = DMA((G,)), DMA((L,))
    scratch = [seven, seven, seven, seven, seven, seven, seven, seven, fifteen, fifteen, DMA((2, G)), DMA((2, G)), seven, seven, seven, seven, DMA((6,))]
    return call(gather_kernel, shapes, [ANY] * 6, [ANY] * 5, scratch, 0, "gather", (state, w3, wo, dec, idx, zero))


def wide(ref, h):
    return jnp.concatenate([ref[h, g] for g in range(G)], axis=1)


def moments(x):
    mean = jnp.sum(x, axis=-1, keepdims=True) * (1.0 / D)
    centred = x - mean
    var = jnp.sum(centred * centred, axis=-1, keepdims=True) * (1.0 / D)
    inv = lax.rsqrt(var + EPSILON)
    return centred * inv, inv


def halves(shape):
    lane = lax.broadcasted_iota(jnp.int32, shape, 1)
    return lane < HD


def only(value, hh):
    first = halves(value.shape)
    keep = first if hh == 0 else jnp.logical_not(first)
    return jnp.where(keep, value, jnp.zeros_like(value))


def row_bias():
    _, _, has_up, has_down = neighbours()
    return (
        jnp.where(has_up, 0.0, -BIG).astype(F32),
        jnp.where(has_down, 0.0, -BIG).astype(F32),
    )


def forward_kernel(x_ref, gain, w_ref, wo_ref, dec_ref, q_ref, kv_ref, t_ref, ml_ref, f_ref, n_ref, acc):
    up_bias, down_bias = row_bias()
    for h in range(3):
        hat, _ = moments(wide(x_ref, h).astype(F32))
        n_ref[pl.ds(h * T, T), :] = (hat * gain[...]).astype(BF)

    def project(g, carry):
        res = nn(n_ref[...], w_ref[g])
        q_ref[g] = res[:, :128].astype(BF)
        kv_ref[0, g] = res[:, 128:256].astype(BF)
        kv_ref[1, g] = res[:, 256:].astype(BF)
        t_ref[0, g] = jnp.transpose(res[:, 128:256]).astype(BF)
        t_ref[1, g] = jnp.transpose(res[:, 256:]).astype(BF)
        return carry

    lax.fori_loop(0, G, project, 0)
    acc[...] = jnp.zeros_like(acc)

    def attend(g, carry):
        query = q_ref[g, pl.ds(T, T), :] * jnp.asarray(0.125, BF)
        parts = []
        for hh in range(2):
            q = only(query, hh)
            s = nt(kv_ref[0, g], q)
            m0 = jnp.max(s[:T], axis=0, keepdims=True) + up_bias
            m1 = jnp.max(s[T : 2 * T], axis=0, keepdims=True)
            m2 = jnp.max(s[2 * T :], axis=0, keepdims=True) + down_bias
            m = jnp.maximum(jnp.maximum(m0, m1), m2)
            e0 = jnp.exp(s[:T] - (m - up_bias))
            e1 = jnp.exp(s[T : 2 * T] - m)
            e2 = jnp.exp(s[2 * T :] - (m - down_bias))
            l = jnp.sum(e0, axis=0, keepdims=True) + jnp.sum(e1, axis=0, keepdims=True) + jnp.sum(e2, axis=0, keepdims=True)
            inv = 1.0 / l
            p = jnp.concatenate([(e0 * inv).astype(BF), (e1 * inv).astype(BF), (e2 * inv).astype(BF)], axis=0)
            parts.append(nn(t_ref[1, g, pl.ds(hh * HD, HD), :], p))
            ml_ref[0, 2 * g + hh] = m
            ml_ref[1, 2 * g + hh] = inv
        mixed = jnp.transpose(jnp.concatenate(parts, axis=0)).astype(BF)
        acc[...] += nn(mixed, wo_ref[g]).astype(BF).astype(F32)
        return carry

    lax.fori_loop(0, G, attend, 0)
    updated = (wide(x_ref, 1).astype(F32) + acc[...]).astype(BF)
    dec = jnp.concatenate([dec_ref[g] for g in range(G)], axis=1)
    f_ref[...] = nt(dec, updated).astype(BF)


def forward(x, gain, w, wo, dec):
    shapes = (
        sds((G, 3 * T, 128), BF),
        sds((2, G, 3 * T, 128), BF),
        sds((2, G, 128, 3 * T), BF),
        sds((2, 16, 1, T), F32),
        sds((VP, T), BF),
    )
    scratch = [pltpu.VMEM((3 * T, D), BF), pltpu.VMEM((T, D), F32)]
    return call(forward_kernel, shapes, [VM] * 5, [VM] * 5, scratch, None, "forward", (x, gain, w, wo, dec))


def swap_rows(src, above, below, ss, rs):
    up, down, has_up, has_down = neighbours()
    to_up = remote(src, below, ss.at[0], rs.at[0], up)
    to_down = remote(src, above, ss.at[1], rs.at[1], down)

    def start():
        pl.when(has_up)(lambda: to_up.start())
        pl.when(has_down)(lambda: to_down.start())

    def wait():
        @pl.when(has_up)
        def _():
            to_up.wait_send()
            to_down.wait_recv()

        @pl.when(has_down)
        def _():
            to_down.wait_send()
            to_up.wait_recv()

    return start, wait


def run_of(c, half, k):
    return row_of(c, k) * 4 + (c // 4) * 2 + half


def pick_kernel(f_ref, ml_ref, idx_ref, mlh_ref, picked, fields, mine, s_f, r_f, s_p, r_p, s_m, r_m):
    b, c, r, w, k = place()
    _, _, has_up, has_down = neighbours()
    mlh_ref[:, 0] = jnp.full((2, 16, 1, T), BIG, F32)
    mlh_ref[:, 1] = jnp.zeros((2, 16, 1, T), F32)
    greet(chan=True, lat=True)
    copies = []
    for i in range(1, G):
        copy = remote(f_ref, fields.at[c, pl.ds(0, VP)], s_f.at[i], r_f.at[i], chan_peer(i))
        copy.start()
        copies.append(copy)
    start, wait = swap_rows(ml_ref, mlh_ref.at[0], mlh_ref.at[1], s_m, r_m)
    start()
    fields[c, pl.ds(0, VP), :] = f_ref[...]
    index = idx_ref[...].reshape(16 * L, 128)
    sixteen = lax.broadcasted_iota(jnp.int32, (16 * L, 128), 1) * 16

    def one(g, total):
        for half in range(2):
            hot = (index == sixteen + run_of(g, half, k)).astype(F32).astype(BF)
            total = total + nn(hot[:, :VP], fields[g, :, pl.ds(half * 128, 128)])
        return total

    total = one(c, jnp.zeros((16 * L, 128), F32))
    for i in range(1, G):
        copies[i - 1].wait_recv()
        total = one((c + G - i) % G, total)
    mine[...] = total.astype(BF).reshape(L, 16, 128)
    sends = []
    for i in range(1, L):
        dev = lat_peer(i)
        copy = remote(mine.at[dev[0]], picked.at[b], s_p.at[i], r_p.at[i], dev)
        copy.start()
        sends.append(copy)
    picked[b] = mine[b]
    for copy in sends:
        copy.wait()
    for copy in copies:
        copy.wait_send()
    wait()


def pick(f, ml, idx):
    shapes = (sds((2, 2, 16, 1, T), F32), sds((L, 16, 128), BF))
    scratch = [pltpu.VMEM((G, VP, T), BF), pltpu.VMEM((L, 16, 128), BF), DMA((G,)), DMA((G,)), DMA((L,)), DMA((L,)), DMA((2,)), DMA((2,))]
    return call(pick_kernel, shapes, [VM] * 3, [VM] * 2, scratch, 1, "pick", (f, ml, idx))


def observe_kernel(count, picked, interp, obs, out, pred, adj):
    b = pl.program_id(0)
    live = count[b]
    pred[...] = jnp.zeros_like(pred)
    adj[...] = jnp.zeros_like(adj)
    row = lax.broadcasted_iota(jnp.int32, (16, 128), 0)

    def predict(s, carry):
        pred[...] = jnp.where(row == s, nt(picked[0], interp[0, s]), pred[...])
        return carry

    lax.fori_loop(0, live, predict, 0)
    misfit = jnp.where(row < live, pred[...] - obs[0].astype(F32), 0.0)
    low = misfit.astype(BF)

    def back(s, carry):
        adj[...] = jnp.where(row == s, nn(low, interp[0, s]), adj[...])
        return carry

    lax.fori_loop(0, live, back, 0)
    out[0, :16, :] = adj[...].astype(BF)
    out[0, 16:, :] = low


def observe(count, picked, interp, obs):
    return pl.pallas_call(
        observe_kernel,
        out_shape=sds((L, 32, 128), BF),
        grid_spec=pltpu.PrefetchScalarGridSpec(
            num_scalar_prefetch=1,
            grid=(L,),
            in_specs=[
                pl.BlockSpec((1, 16, 128), lambda i, n: (i, 0, 0)),
                pl.BlockSpec((1, 16, 128, 128), lambda i, n: (i, 0, 0, 0)),
                pl.BlockSpec((1, 16, 128), lambda i, n: (i, 0, 0)),
            ],
            out_specs=pl.BlockSpec((1, 32, 128), lambda i, n: (i, 0, 0)),
            scratch_shapes=[pltpu.VMEM((16, 128), F32), pltpu.VMEM((16, 128), F32)],
        ),
        name="observe",
    )(count, picked, interp, obs)


def settle_kernel(am, idx_ref, misfit, gf, came, parts, got, s_a, r_a, s_g, r_g, s_h, r_h):
    b, c, r, w, k = place()
    gf[...] = jnp.zeros_like(gf)
    greet(chan=True, lat=True)
    copies = []
    for i in range(1, L):
        dev = lat_peer(i)
        copy = remote(am.at[dev[0]], came.at[b], s_a.at[i], r_a.at[i], dev)
        copy.start()
        copies.append(copy)
    came[b] = am[b]
    index = jnp.transpose(idx_ref[...].reshape(16 * L, 128).astype(F32))
    sixteen = lax.broadcasted_iota(jnp.int32, (VP, 16 * L), 0) * 16
    index = index[:VP].astype(jnp.int32)
    for copy in copies:
        copy.wait()
    all_in = came[...]
    misfit[...] = all_in[:, 16:, :].astype(F32)
    adjoint = all_in[:, :16, :].reshape(16 * L, 128)
    sends = []
    for i in list(range(1, G)) + [0]:
        g = (c + i) % G
        for half in range(2):
            hot = (index == sixteen + run_of(g, half, k)).astype(F32).astype(BF)
            parts[g, :, pl.ds(half * 128, 128)] = nn(hot, adjoint).astype(BF)
        if i:
            copy = remote(parts.at[g], got.at[c], s_g.at[i], r_g.at[i], (b, g))
            copy.start()
            sends.append(copy)
    total = parts[c].astype(F32)
    for i in range(1, G):
        sends[i - 1].wait_recv()
        total = total + got[(c + G - i) % G].astype(F32)
    gf[1] = total
    start, wait = swap_rows(gf.at[1], gf.at[0], gf.at[2], s_h, r_h)
    start()
    for copy in sends:
        copy.wait_send()
    wait()


def settle(am, idx):
    shapes = (sds((L, 16, 128), F32), sds((3, VP, T), F32))
    scratch = [pltpu.VMEM((L, 32, 128), BF), pltpu.VMEM((G, VP, T), BF), pltpu.VMEM((G, VP, T), BF), DMA((L,)), DMA((L,)), DMA((G,)), DMA((G,)), DMA((2,)), DMA((2,))]
    return call(settle_kernel, shapes, [VM] * 2, [VM] * 2, scratch, 2, "settle", (am, idx))


def backward_kernel(
    x_ref, gain, w_ref, wo_ref, dec_ref, q_ref, kv_ref, t_ref, ml_ref, mlh_ref, gf_ref,
    back, gu, low, do, dq, dkv, delta, delta_h, gn, outgo, s_d, r_d, s_y, r_y,
):
    b, c, r, w, k = place()
    up_bias, down_bias = row_bias()
    delta_h[...] = jnp.zeros_like(delta_h)
    greet(chan=True, lat=True)
    dec = jnp.concatenate([dec_ref[g] for g in range(G)], axis=1)
    dec = jnp.concatenate([dec, jnp.zeros((128 - VP, D), BF)], axis=0)
    dec3 = jnp.concatenate([dec, dec, dec], axis=0)
    for h in range(3):
        field = jnp.transpose(jnp.concatenate([gf_ref[h], jnp.zeros((128 - VP, T), F32)], axis=0))
        hi = field.astype(BF)
        rest = field - hi.astype(F32)
        mid = rest.astype(BF)
        lo = (rest - mid.astype(F32)).astype(BF)
        update = nn(jnp.concatenate([hi, mid, lo], axis=1), dec3)
        if h == 1:
            gu[...] = update
        low[pl.ds(h * T, T), :] = update.astype(BF)

    def mixed(g, carry):
        do[g] = nt(low[...], wo_ref[g]).astype(BF)
        return carry

    lax.fori_loop(0, G, mixed, 0)
    mid_rows = pl.ds(T, T)

    def own(g, carry):
        query = q_ref[g, mid_rows, :] * jnp.asarray(0.125, BF)
        parts = []
        dk = jnp.zeros((T, 128), F32)
        dv = jnp.zeros((T, 128), F32)
        for hh in range(2):
            n = 2 * g + hh
            q = only(query, hh)
            d = only(do[g, mid_rows, :], hh)
            m, inv = ml_ref[0, n], ml_ref[1, n]
            s = nt(kv_ref[0, g], q)
            dp = nt(kv_ref[1, g], d)
            p0 = jnp.exp(s[:T] - (m - up_bias)) * inv
            p1 = jnp.exp(s[T : 2 * T] - m) * inv
            p2 = jnp.exp(s[2 * T :] - (m - down_bias)) * inv
            p = jnp.concatenate([p0, p1, p2], axis=0)
            row = jnp.sum(p * dp, axis=0, keepdims=True)
            delta[n] = row
            ds = (p * (dp - row)).astype(BF)
            parts.append(nn(t_ref[0, g, pl.ds(hh * HD, HD), :], ds) * 0.125)
            dk = dk + nn(ds[T : 2 * T], q)
            dv = dv + nn(p1.astype(BF), d)
        dq[g] = jnp.transpose(jnp.concatenate(parts, axis=0)).astype(BF)
        dkv[0, g] = dk
        dkv[1, g] = dv
        return carry

    lax.fori_loop(0, G, own, 0)
    start, wait = swap_rows(delta, delta_h.at[0], delta_h.at[1], s_d, r_d)
    start()
    wait()
    gn[...] = jnp.zeros_like(gn)

    def other(g, carry):
        dk = dkv[0, g]
        dv = dkv[1, g]
        for side in range(2):
            rows = pl.ds(side * 2 * T, T)
            query = q_ref[g, rows, :] * jnp.asarray(0.125, BF)
            for hh in range(2):
                n = 2 * g + hh
                q = only(query, hh)
                d = only(do[g, rows, :], hh)
                s = nt(kv_ref[0, g, mid_rows, :], q)
                dp = nt(kv_ref[1, g, mid_rows, :], d)
                p = jnp.exp(s - mlh_ref[side, 0, n]) * mlh_ref[side, 1, n]
                ds = (p * (dp - delta_h[side, n])).astype(BF)
                dk = dk + nn(ds, q)
                dv = dv + nn(p.astype(BF), d)
        three = jnp.concatenate([dq[g], dk.astype(BF), dv.astype(BF)], axis=1)
        gn[...] += nt(three, w_ref[g]).astype(BF).astype(F32)
        return carry

    lax.fori_loop(0, G, other, 0)
    hat, inv = moments(wide(x_ref, 1).astype(F32))
    grad_hat = gn[...] * gain[...]
    mean = jnp.sum(grad_hat, axis=-1, keepdims=True) * (1.0 / D)
    cross = jnp.sum(grad_hat * hat, axis=-1, keepdims=True) * (1.0 / D)
    total = (gu[...] + (grad_hat - mean - hat * cross) * inv).astype(BF)
    for g in range(G):
        outgo[g] = total[:, g * 128 : (g + 1) * 128]
    here = (r, pl.ds(w * T, T))
    sends = []
    for i in range(1, G):
        dev = chan_peer(i)
        copy = remote(outgo.at[dev[1]], back.at[here[0], here[1]], s_y.at[i], r_y.at[i], dev)
        copy.start()
        sends.append(copy)
    back[here[0], here[1], :] = outgo[c]
    for copy in sends:
        copy.wait()


def backward(x, gain, w, wo, dec, q, kv, t, ml, mlh, gf):
    scratch = [
        pltpu.VMEM((T, D), F32),
        pltpu.VMEM((3 * T, D), BF),
        pltpu.VMEM((G, 3 * T, 128), BF),
        pltpu.VMEM((G, T, 128), BF),
        pltpu.VMEM((2, G, T, 128), F32),
        pltpu.VMEM((16, 1, T), F32),
        pltpu.VMEM((2, 16, 1, T), F32),
        pltpu.VMEM((T, D), F32),
        pltpu.VMEM((G, T, 128), BF),
        DMA((2,)), DMA((2,)), DMA((G,)), DMA((G,)),
    ]
    return call(
        backward_kernel, sds((4, 512, 128), BF), [VM] * 11, VM, scratch, 3, "backward",
        (x, gain, w, wo, dec, q, kv, t, ml, mlh, gf),
    )


def body(state, background, gain, w_query, w_key, w_value, w_out, decoder, interp, obs_values, tile_index, block_count):
    w3 = jnp.concatenate([w_query, w_key, w_value], axis=1)
    dec = jnp.pad(jnp.transpose(decoder), ((0, VP - VARS), (0, 0)))
    idx = jnp.broadcast_to(tile_index.reshape(L, 16, 1), (L, 16, 128))
    x, w, wo, dec, idx = gather(state, w3, w_out, dec, idx)
    gain = gain.reshape(1, D)
    q, kv, t, ml, f = forward(x, gain, w, wo, dec)
    mlh, picked = pick(f, ml, idx)
    am = observe(block_count.reshape(L), picked, interp.reshape(L, 16, 128, 128), obs_values.reshape(L, 16, 128))
    misfit, gf = settle(am, idx)
    back = backward(x, gain, w, wo, dec, q, kv, t, ml, mlh, gf)
    gradient = state.astype(F32) - background.astype(F32) + back.astype(F32)
    return misfit.reshape(L, 1, 1, 16, 128), gradient


def solution(mesh):
    return jax.shard_map(
        body,
        mesh=mesh,
        in_specs=(
            P("lat", None, "chan"),
            P("lat", None, "chan"),
            P(),
            P(None, "chan"),
            P(None, "chan"),
            P(None, "chan"),
            P("chan", None),
            P("chan", None),
            P("lat", "chan", None, None, None, None),
            P("lat", "chan", None, None, None),
            P("lat", "chan", None, None),
            P("lat", "chan", None),
        ),
        out_specs=(P(None, "chan", "lat", None, None), P("lat", None, "chan")),
        check_vma=False,
    )
```

```python
import functools

import jax
import jax.numpy as jnp
from jax import lax
from jax.experimental import pallas as pl
from jax.experimental.pallas import tpu as pltpu
from jax.sharding import PartitionSpec as P

D = 1024
HD = 64
VARS = 69
EPSILON = 1e-05
VP = 80
T = 256
G = 8
L = 16
BIG = 1e30
MESH = pl.DeviceIdType.MESH
BF = jnp.bfloat16
F32 = jnp.float32
VMEM_LIMIT = 62 * 1024 * 1024


def nn(a, b):
    return lax.dot_general(a, b, (((1,), (0,)), ((), ())), preferred_element_type=F32)


def nt(a, b):
    return lax.dot_general(a, b, (((1,), (1,)), ((), ())), preferred_element_type=F32)


def place():
    b = lax.axis_index("lat")
    c = lax.axis_index("chan")
    k = b % 2
    x = c % 4
    r = x + k * (3 - 2 * x)
    return b, c, r, c // 4, k


def row_of(c, k):
    x = c % 4
    return x + k * (3 - 2 * x)


def neighbours():
    b, c, r, w, k = place()
    inner_up = (r > 0).astype(jnp.int32)
    inner_down = (r < 3).astype(jnp.int32)
    up = (b - 1 + inner_up, c + inner_up * (2 * k - 1))
    down = (b + 1 - inner_down, c + inner_down * (1 - 2 * k))
    row = b * 4 + r
    return up, down, row > 0, row < 4 * L - 1


def chan_peer(i):
    b, c, _, _, _ = place()
    return (b, (c + i) % G)


def lat_peer(i):
    b, c, _, _, _ = place()
    return ((b + i) % L, c)


def greet(chan=True, lat=False, rows=False):
    barrier = pltpu.get_barrier_semaphore()
    count = 0
    if chan:
        for i in range(1, G):
            pl.semaphore_signal(barrier, inc=1, device_id=chan_peer(i), device_id_type=MESH)
            count += 1
    if lat:
        for i in range(1, L):
            pl.semaphore_signal(barrier, inc=1, device_id=lat_peer(i), device_id_type=MESH)
            count += 1
    pl.semaphore_wait(barrier, count)


def remote(src, dst, ss, rs, dev):
    return pltpu.make_async_remote_copy(
        src_ref=src, dst_ref=dst, send_sem=ss, recv_sem=rs, device_id=dev, device_id_type=MESH
    )


def call(kernel, out_shape, in_specs, out_specs, scratch, cid, name, args):
    return pl.pallas_call(
        kernel,
        out_shape=out_shape,
        in_specs=in_specs,
        out_specs=out_specs,
        scratch_shapes=scratch,
        compiler_params=pltpu.CompilerParams(
            collective_id=cid, has_side_effects=cid is not None, vmem_limit_bytes=VMEM_LIMIT
        ),
        name=name,
    )(*args)


VM = pl.BlockSpec(memory_space=pltpu.VMEM)
ANY = pl.BlockSpec(memory_space=pl.ANY)
DMA = pltpu.SemaphoreType.DMA


def sds(shape, dtype):
    return jax.ShapeDtypeStruct(shape, dtype)


class Spread:
    def __init__(self, view, size, sems):
        self.view, self.size = view, size
        self.s1, self.r1, self.s2, self.s3, self.r3, self.s4, self.r4, self.s5, self.r5 = sems
        b, c, _, z, k = place()
        x, y = c % 4, b // 4
        p = y % 2
        self.b, self.c, self.x, self.z = b, c, x, z
        self.start = (p * 2 + k) * size
        self.across = ((1 - p) * 2 + k) * size
        self.core = (b + 1 - 2 * k, c)
        self.ups = [((b + 4) % L, c), ((b + 12) % L, c)]
        self.flip = (b, (c + 4) % G)
        self.sent = []

    def send(self, g, start, size, ss, rs, dev):
        ref = self.view(g, start, size)
        copy = remote(ref, ref, ss, rs, dev)
        copy.start()
        self.sent.append(copy)

    def wait(self, g, start, size, rs):
        ref = self.view(g, start, size)
        remote(ref, ref, self.s1.at[0], rs, self.core).wait_recv()

    def from_x(self, i):
        return self.z * 4 + (self.x + 4 - i) % 4

    def from_z(self, i):
        return (1 - self.z) * 4 + (self.x + 4 - i) % 4

    def others(self):
        return [self.from_x(i) for i in (1, 3, 2)] + [self.from_z(i) for i in (0, 1, 3, 2)]

    def first(self):
        c = self.c
        self.send(c, self.start, self.size, self.s1.at[0], self.r1.at[c], self.flip)
        for i in (1, 3, 2):
            dev = (self.b, self.z * 4 + (self.x + i) % 4)
            self.send(c, self.start, self.size, self.s1.at[i], self.r1.at[c], dev)

    def fan(self, g):
        half = self.size // 2
        for h in range(2):
            self.send(g, self.start + h * half, half, self.s4.at[h, g], self.r4.at[h, g], self.ups[h])
        self.send(g, self.start, self.size, self.s3.at[g], self.r3.at[g], self.core)

    def relay_x(self):
        for i in (1, 3, 2):
            g = self.from_x(i)
            self.wait(g, self.start, self.size, self.r1.at[g])
            self.send(g, self.start, self.size, self.s2.at[i], self.r1.at[g], self.flip)
            self.fan(g)

    def relay_z(self):
        for i in (0, 1, 3, 2):
            g = self.from_z(i)
            self.wait(g, self.start, self.size, self.r1.at[g])
            self.fan(g)

    def relay_y(self):
        half = self.size // 2
        for g in self.others():
            for h in range(2):
                start = self.across + h * half
                self.wait(g, start, half, self.r4.at[h, g])
                self.send(g, start, half, self.s5.at[h, g], self.r5.at[h, g], self.core)

    def ready(self):
        half = self.size // 2
        _, _, _, _, k = place()
        turn = (1 - 2 * k) * self.size
        for g in self.others():
            self.wait(g, self.start + turn, self.size, self.r3.at[g])
            for h in range(2):
                self.wait(g, self.across + turn + h * half, half, self.r5.at[h, g])

    def finish(self):
        for copy in self.sent:
            copy.wait_send()


def wide(ref, h):
    return jnp.concatenate([ref[h, g] for g in range(G)], axis=1)


def moments(x):
    mean = jnp.sum(x, axis=-1, keepdims=True) * (1.0 / D)
    centred = x - mean
    var = jnp.sum(centred * centred, axis=-1, keepdims=True) * (1.0 / D)
    inv = lax.rsqrt(var + EPSILON)
    return centred * inv, inv


def only(value, hh):
    first = lax.broadcasted_iota(jnp.int32, value.shape, 1) < HD
    keep = first if hh == 0 else jnp.logical_not(first)
    return jnp.where(keep, value, jnp.zeros_like(value))


def swap_rows(src, above, below, ss, rs):
    up, down, has_up, has_down = neighbours()
    to_up = remote(src, below, ss.at[0], rs.at[0], up)
    to_down = remote(src, above, ss.at[1], rs.at[1], down)

    def start():
        pl.when(has_up)(lambda: to_up.start())
        pl.when(has_down)(lambda: to_down.start())

    def wait():
        @pl.when(has_up)
        def _():
            to_up.wait_send()
            to_down.wait_recv()

        @pl.when(has_down)
        def _():
            to_down.wait_send()
            to_up.wait_recv()

    return start, wait


def run_of(c, half, k):
    return row_of(c, k) * 4 + (c // 4) * 2 + half


def loop(n, step):
    def wrapped(i, carry):
        step(i)
        return carry

    lax.fori_loop(0, n, wrapped, 0)


SCRATCH = dict(
    x_v=pltpu.VMEM((3, G, T, 128), BF),
    w_v=pltpu.VMEM((G, 3, D, 128), BF),
    o_v=pltpu.VMEM((G, 128, D), BF),
    d_v=pltpu.VMEM((G, VP, 128), BF),
    i_v=pltpu.VMEM((L, 16, 128), jnp.int32),
    itp=pltpu.VMEM((L, 16, 128, 128), BF),
    n_v=pltpu.VMEM((3 * T, D), BF),
    qkv=pltpu.VMEM((3, G, 3 * T, 128), BF),
    kt=pltpu.VMEM((G, 128, 3 * T), BF),
    mix=pltpu.VMEM((G, T, 128), BF),
    acc=pltpu.VMEM((T, D), F32),
    ml=pltpu.VMEM((2, 16, 1, T), F32),
    mlh=pltpu.VMEM((2, 2, 16, 1, T), F32),
    fields=pltpu.VMEM((G, VP, T), BF),
    mine=pltpu.VMEM((L, 16, 128), BF),
    picked=pltpu.VMEM((L, 16, 128), BF),
    am=pltpu.VMEM((L, 32, 128), BF),
    came=pltpu.VMEM((L, 32, 128), BF),
    parts=pltpu.VMEM((G, VP, T), BF),
    got=pltpu.VMEM((G, VP, T), BF),
    gf=pltpu.VMEM((3, VP, T), F32),
    gu=pltpu.VMEM((T, D), F32),
    low=pltpu.VMEM((3 * T, D), BF),
    do=pltpu.VMEM((G, 3 * T, 128), BF),
    dq=pltpu.VMEM((G, T, 128), BF),
    dkv=pltpu.VMEM((2, G, T, 128), F32),
    delta=pltpu.VMEM((16, 1, T), F32),
    delta_h=pltpu.VMEM((2, 16, 1, T), F32),
    outgo=pltpu.VMEM((G, T, 128), BF),
    loc=DMA((8,)),
    s_state=DMA((G,)), r_state=DMA((G,)),
    s_d=DMA((G,)), r_d=DMA((G,)),
    s_i=DMA((L,)), r_i=DMA((L,)),
    s_h=DMA((2, G)), r_h=DMA((2, G)),
    s_f=DMA((G,)), r_f=DMA((G,)),
    s_p=DMA((L,)), r_p=DMA((L,)),
    s_a=DMA((L,)), r_a=DMA((L,)),
    s_g=DMA((G,)), r_g=DMA((G,)),
    s_y=DMA((G,)), r_y=DMA((G,)),
    s_m=DMA((2,)), r_m=DMA((2,)),
    s_gh=DMA((2,)), r_gh=DMA((2,)),
    s_dl=DMA((2, 2)), r_dl=DMA((2, 2)),
    w1=DMA((4,)), w2=DMA((G,)), w3=DMA((4,)), w4=DMA((G,)), w5=DMA((G,)), w6=DMA((2, G)), w7=DMA((2, G)), w8=DMA((2, G)), w9=DMA((2, G)),
    o1=DMA((4,)), o2=DMA((G,)), o3=DMA((4,)), o4=DMA((G,)), o5=DMA((G,)), o6=DMA((2, G)), o7=DMA((2, G)), o8=DMA((2, G)), o9=DMA((2, G)),
)


class Refs:
    pass


def kernel(state, wq, wk, wv, wo, dec, idx, gain, interp, obs, count, misfit, back, *scratch):
    s = Refs()
    for name, ref in zip(SCRATCH, scratch):
        setattr(s, name, ref)
    b, c, r, w, k = place()
    up, down, has_up, has_down = neighbours()
    up_bias = jnp.where(has_up, 0.0, -BIG).astype(F32)
    down_bias = jnp.where(has_down, 0.0, -BIG).astype(F32)
    mid_rows = pl.ds(T, T)
    eighth = jnp.asarray(0.125, BF)

    local = [
        pltpu.make_async_copy(state.at[r, pl.ds(w * T, T)], s.x_v.at[1, c], s.loc.at[0]),
        pltpu.make_async_copy(wq, s.w_v.at[c, 0], s.loc.at[1]),
        pltpu.make_async_copy(wk, s.w_v.at[c, 1], s.loc.at[2]),
        pltpu.make_async_copy(wv, s.w_v.at[c, 2], s.loc.at[3]),
        pltpu.make_async_copy(wo, s.o_v.at[c], s.loc.at[4]),
        pltpu.make_async_copy(dec, s.d_v.at[c], s.loc.at[5]),
        pltpu.make_async_copy(idx.at[b], s.i_v.at[b], s.loc.at[6]),
        pltpu.make_async_copy(interp, s.itp, s.loc.at[7]),
    ]
    for copy in local:
        copy.start()

    @pl.when(jnp.logical_not(has_up))
    def _():
        s.x_v[0] = jnp.zeros((G, T, 128), BF)

    @pl.when(jnp.logical_not(has_down))
    def _():
        s.x_v[2] = jnp.zeros((G, T, 128), BF)

    s.mlh[:, 0] = jnp.full((2, 16, 1, T), BIG, F32)
    s.mlh[:, 1] = jnp.zeros((2, 16, 1, T), F32)
    s.delta_h[...] = jnp.zeros_like(s.delta_h)
    s.gf[...] = jnp.zeros_like(s.gf)
    greet(chan=True, lat=True)

    sends = []
    states = {}
    for i in (1, 3, 4, 5, 7, 2, 6):
        _, pc = chan_peer(i)
        pr = row_of(pc, k)
        copy = remote(state.at[pr, pl.ds((pc // 4) * T, T)], s.x_v.at[1, c], s.s_state.at[i], s.r_state.at[i], (b, pc))
        copy.start()
        sends.append(copy)
        states[i] = copy
    weights = Spread(
        lambda g, at, n: s.w_v.at[g, :, pl.ds(at, n)], 256, (s.w1, s.w2, s.w3, s.w4, s.w5, s.w6, s.w7, s.w8, s.w9)
    )
    outs = Spread(
        lambda g, at, n: s.o_v.at[g, pl.ds(at, n)], 32, (s.o1, s.o2, s.o3, s.o4, s.o5, s.o6, s.o7, s.o8, s.o9)
    )
    for copy in local[1:4]:
        copy.wait()
    weights.first()
    for i in range(1, L):
        dev = lat_peer(i)
        copy = remote(idx.at[dev[0]], s.i_v.at[b], s.s_i.at[i], s.r_i.at[i], dev)
        copy.start()
        sends.append(copy)

    def halo(g, sem):
        to_up = remote(s.x_v.at[1, g], s.x_v.at[2, g], s.s_h.at[0, sem], s.r_h.at[0, sem], up)
        to_down = remote(s.x_v.at[1, g], s.x_v.at[0, g], s.s_h.at[1, sem], s.r_h.at[1, sem], down)
        return to_up, to_down

    def start_halo(g, sem):
        to_up, to_down = halo(g, sem)
        pl.when(has_up)(lambda: to_up.start())
        pl.when(has_down)(lambda: to_down.start())

    local[0].wait()
    start_halo(c, 0)
    for i in (1, 3, 4, 5, 7, 2, 6):
        states[i].wait_recv()
        start_halo((c + G - i) % G, i)
    weights.relay_x()
    local[4].wait()
    outs.first()
    for i in range(1, G):
        copy = remote(dec, s.d_v.at[c], s.s_d.at[i], s.r_d.at[i], chan_peer(i))
        copy.start()
        sends.append(copy)

    def norm(h):
        hat, _ = moments(wide(s.x_v, h).astype(F32))
        s.n_v[pl.ds(h * T, T), :] = (hat * gain[...]).astype(BF)

    norm(1)
    weights.relay_z()
    weights.relay_y()
    for i in range(G):
        to_up, to_down = halo((c + G - i) % G, i)
        pl.when(has_down)(lambda: to_up.wait_recv())
        pl.when(has_up)(lambda: to_down.wait_recv())
    norm(0)
    norm(2)
    weights.ready()

    def project(g):
        res = nn(s.n_v[...], jnp.concatenate([s.w_v[g, 0], s.w_v[g, 1], s.w_v[g, 2]], axis=1))
        for i in range(3):
            s.qkv[i, g] = res[:, i * 128 : (i + 1) * 128].astype(BF)
        s.kt[g] = jnp.transpose(res[:, 128:256]).astype(BF)

    loop(G, project)

    def attend(g):
        query = s.qkv[0, g, mid_rows, :] * eighth
        vt = jnp.transpose(s.qkv[2, g].astype(F32)).astype(BF)
        parts = []
        for hh in range(2):
            q = only(query, hh)
            sc = nt(s.qkv[1, g], q)
            m0 = jnp.max(sc[:T], axis=0, keepdims=True) + up_bias
            m1 = jnp.max(sc[T : 2 * T], axis=0, keepdims=True)
            m2 = jnp.max(sc[2 * T :], axis=0, keepdims=True) + down_bias
            m = jnp.maximum(jnp.maximum(m0, m1), m2)
            e0 = jnp.exp(sc[:T] - (m - up_bias))
            e1 = jnp.exp(sc[T : 2 * T] - m)
            e2 = jnp.exp(sc[2 * T :] - (m - down_bias))
            l = jnp.sum(e0, axis=0, keepdims=True) + jnp.sum(e1, axis=0, keepdims=True) + jnp.sum(e2, axis=0, keepdims=True)
            inv = 1.0 / l
            p = jnp.concatenate([(e0 * inv).astype(BF), (e1 * inv).astype(BF), (e2 * inv).astype(BF)], axis=0)
            parts.append(nn(vt[hh * HD : (hh + 1) * HD], p))
            s.ml[0, 2 * g + hh] = m
            s.ml[1, 2 * g + hh] = inv
        s.mix[g] = jnp.transpose(jnp.concatenate(parts, axis=0)).astype(BF)

    loop(2, attend)
    outs.relay_x()
    loop(2, lambda g: attend(g + 2))
    outs.relay_z()
    loop(2, lambda g: attend(g + 4))
    outs.relay_y()
    loop(2, lambda g: attend(g + 6))
    start_ml, wait_ml = swap_rows(s.ml, s.mlh.at[0], s.mlh.at[1], s.s_m, s.r_m)
    start_ml()
    outs.ready()
    local[5].wait()
    for i in range(1, G):
        remote(dec, s.d_v.at[0], s.s_d.at[i], s.r_d.at[i], chan_peer(i)).wait_recv()
    s.acc[...] = wide(s.x_v, 1).astype(F32) * 0.0

    def out(g):
        s.acc[...] += nn(s.mix[g], s.o_v[g]).astype(BF).astype(F32)

    loop(G, out)
    updated = (wide(s.x_v, 1).astype(F32) + s.acc[...]).astype(BF)
    dec_all = jnp.concatenate([s.d_v[g] for g in range(G)], axis=1)
    s.fields[c] = nt(dec_all, updated).astype(BF)

    copies = []
    for i in range(1, G):
        copy = remote(s.fields.at[c], s.fields.at[c], s.s_f.at[i], s.r_f.at[i], chan_peer(i))
        copy.start()
        copies.append(copy)
        sends.append(copy)
    local[6].wait()
    for i in range(1, L):
        remote(idx.at[0], s.i_v.at[0], s.s_i.at[i], s.r_i.at[i], lat_peer(i)).wait_recv()
    index = s.i_v[...].reshape(16 * L, 128)
    lanes = lax.broadcasted_iota(jnp.int32, (16 * L, 128), 1) * 16

    def one(g, total):
        for half in range(2):
            hot = (index == lanes + run_of(g, half, k)).astype(F32).astype(BF)
            total = total + nn(hot[:, :VP], s.fields[g, :, pl.ds(half * 128, 128)])
        return total

    total = one(c, jnp.zeros((16 * L, 128), F32))
    for i in range(1, G):
        copies[i - 1].wait_recv()
        total = one((c + G - i) % G, total)
    s.mine[...] = total.astype(BF).reshape(L, 16, 128)
    for i in range(1, L):
        dev = lat_peer(i)
        copy = remote(s.mine.at[dev[0]], s.picked.at[b], s.s_p.at[i], s.r_p.at[i], dev)
        copy.start()
        sends.append(copy)
    s.picked[b] = s.mine[b]

    local[7].wait()
    row = lax.broadcasted_iota(jnp.int32, (16, 128), 0)

    def observe(i):
        band = (b + L - i) % L

        @pl.when(i > 0)
        def _():
            remote(s.mine.at[b], s.picked.at[b], s.s_p.at[i], s.r_p.at[i], (band, c)).wait_recv()

        flat = s.itp[band].reshape(2048, 128)
        big = nt(s.picked[band], flat)
        pred = jnp.zeros((16, 128), F32)
        for n in range(16):
            pred = jnp.where(row == n, big[:, n * 128 : (n + 1) * 128], pred)
        mis = jnp.where(row < count[band], pred - obs[band].astype(F32), 0.0).astype(BF)
        lhs = jnp.concatenate([jnp.where(row == n, mis, jnp.zeros_like(mis)) for n in range(16)], axis=1)
        s.am[band, :16, :] = nn(lhs, flat).astype(BF)
        s.am[band, 16:, :] = mis

        @pl.when(i > 0)
        def _():
            remote(s.am.at[band], s.came.at[b], s.s_a.at[i], s.r_a.at[i], (band, c)).start()

    loop(L, observe)
    s.came[b] = s.am[b]

    index_t = jnp.transpose(index.astype(F32))[:VP].astype(jnp.int32)
    sub = lax.broadcasted_iota(jnp.int32, (VP, 16 * L), 0) * 16

    def arrived(i):
        band = (b + i) % L

        @pl.when(i > 0)
        def _():
            remote(s.am.at[b], s.came.at[b], s.s_a.at[i], s.r_a.at[i], (band, c)).wait()

    loop(L, arrived)
    misfit[...] = s.came[:, 16:, :].astype(F32)
    adjoint = s.came[:, :16, :].reshape(16 * L, 128)
    reduce = []
    for i in list(range(1, G)) + [0]:
        g = (c + i) % G
        for half in range(2):
            hot = (index_t == sub + run_of(g, half, k)).astype(F32).astype(BF)
            s.parts[g, :, pl.ds(half * 128, 128)] = nn(hot, adjoint).astype(BF)
        if i:
            copy = remote(s.parts.at[g], s.got.at[c], s.s_g.at[i], s.r_g.at[i], (b, g))
            copy.start()
            reduce.append(copy)
            sends.append(copy)
    total = s.parts[c].astype(F32)
    for i in range(1, G):
        reduce[i - 1].wait_recv()
        total = total + s.got[(c + G - i) % G].astype(F32)
    s.gf[1] = total
    start_gf, wait_gf = swap_rows(s.gf.at[1], s.gf.at[0], s.gf.at[2], s.s_gh, s.r_gh)
    start_gf()
    wait_ml()

    dec_all = jnp.concatenate([dec_all, jnp.zeros((128 - VP, D), BF)], axis=0)
    dec3 = jnp.concatenate([dec_all, dec_all, dec_all], axis=0)

    def update_of(h):
        field = jnp.transpose(jnp.concatenate([s.gf[h], jnp.zeros((128 - VP, T), F32)], axis=0))
        hi = field.astype(BF)
        rest = field - hi.astype(F32)
        mid = rest.astype(BF)
        lo = (rest - mid.astype(F32)).astype(BF)
        update = nn(jnp.concatenate([hi, mid, lo], axis=1), dec3)
        s.low[pl.ds(h * T, T), :] = update.astype(BF)
        return update

    s.gu[...] = update_of(1)
    wait_gf()
    update_of(0)
    update_of(2)

    def mixed(g):
        s.do[g] = nt(s.low[...], s.o_v[g]).astype(BF)

    loop(G, mixed)

    def own(g):
        query = s.qkv[0, g, mid_rows, :] * eighth
        parts = []
        dk = jnp.zeros((T, 128), F32)
        dv = jnp.zeros((T, 128), F32)
        for hh in range(2):
            n = 2 * g + hh
            q = only(query, hh)
            d = only(s.do[g, mid_rows, :], hh)
            m, inv = s.ml[0, n], s.ml[1, n]
            sc = nt(s.qkv[1, g], q)
            dp = nt(s.qkv[2, g], d)
            p0 = jnp.exp(sc[:T] - (m - up_bias)) * inv
            p1 = jnp.exp(sc[T : 2 * T] - m) * inv
            p2 = jnp.exp(sc[2 * T :] - (m - down_bias)) * inv
            p = jnp.concatenate([p0, p1, p2], axis=0)
            along = jnp.sum(p * dp, axis=0, keepdims=True)
            s.delta[n] = along
            ds = (p * (dp - along)).astype(BF)
            parts.append(nn(s.kt[g, pl.ds(hh * HD, HD), :], ds) * 0.125)
            dk = dk + nn(ds[T : 2 * T], q)
            dv = dv + nn(p1.astype(BF), d)
        s.dq[g] = jnp.transpose(jnp.concatenate(parts, axis=0)).astype(BF)
        s.dkv[0, g] = dk
        s.dkv[1, g] = dv

    def other(g):
        dk = s.dkv[0, g]
        dv = s.dkv[1, g]
        for side in range(2):
            rows = pl.ds(side * 2 * T, T)
            query = s.qkv[0, g, rows, :] * eighth
            for hh in range(2):
                n = 2 * g + hh
                q = only(query, hh)
                d = only(s.do[g, rows, :], hh)
                sc = nt(s.qkv[1, g, mid_rows, :], q)
                dp = nt(s.qkv[2, g, mid_rows, :], d)
                p = jnp.exp(sc - s.mlh[side, 0, n]) * s.mlh[side, 1, n]
                ds = (p * (dp - s.delta_h[side, n])).astype(BF)
                dk = dk + nn(ds, q)
                dv = dv + nn(p.astype(BF), d)
        three = jnp.concatenate([s.dq[g], dk.astype(BF), dv.astype(BF)], axis=1)
        wide_w = jnp.concatenate([s.w_v[g, 0], s.w_v[g, 1], s.w_v[g, 2]], axis=1)
        s.acc[...] += nt(three, wide_w).astype(BF).astype(F32)

    swaps = []
    for n in range(2):
        loop(4, lambda g: own(g + 4 * n))
        heads = pl.ds(8 * n, 8)
        start, wait = swap_rows(
            s.delta.at[heads], s.delta_h.at[0, heads], s.delta_h.at[1, heads], s.s_dl.at[n], s.r_dl.at[n]
        )
        start()
        swaps.append(wait)
    s.acc[...] = jnp.zeros_like(s.acc)
    for n in range(2):
        swaps[n]()
        loop(4, lambda g: other(g + 4 * n))

    hat, inv = moments(wide(s.x_v, 1).astype(F32))
    grad_hat = s.acc[...] * gain[...]
    mean = jnp.sum(grad_hat, axis=-1, keepdims=True) * (1.0 / D)
    cross = jnp.sum(grad_hat * hat, axis=-1, keepdims=True) * (1.0 / D)
    total = (s.gu[...] + (grad_hat - mean - hat * cross) * inv).astype(BF)
    for g in range(G):
        s.outgo[g] = total[:, g * 128 : (g + 1) * 128]
    here = pl.ds(w * T, T)
    final = []
    for i in range(1, G):
        dev = chan_peer(i)
        copy = remote(s.outgo.at[dev[1]], back.at[r, here], s.s_y.at[i], s.r_y.at[i], dev)
        copy.start()
        final.append(copy)
    back[r, here, :] = s.outgo[c]

    weights.finish()
    outs.finish()
    for copy in sends:
        copy.wait_send()
    for i in range(G):
        to_up, to_down = halo((c + G - i) % G, i)
        pl.when(has_up)(lambda: to_up.wait_send())
        pl.when(has_down)(lambda: to_down.wait_send())
    for copy in final:
        copy.wait()


def body(state, background, gain, w_query, w_key, w_value, w_out, decoder, interp, obs_values, tile_index, block_count):
    dec = jnp.pad(jnp.transpose(decoder), ((0, VP - VARS), (0, 0)))
    idx = jnp.broadcast_to(tile_index.reshape(L, 16, 1), (L, 16, 128))
    smem = pl.BlockSpec(memory_space=pltpu.SMEM)
    misfit, back = call(
        kernel,
        (sds((L, 16, 128), F32), sds((4, 512, 128), BF)),
        [ANY] * 7 + [VM, ANY, VM, smem],
        [VM] * 2,
        list(SCRATCH.values()),
        0,
        "whole",
        (
            state, w_query, w_key, w_value, w_out, dec, idx, gain.reshape(1, D),
            interp.reshape(L, 16, 128, 128), obs_values.reshape(L, 16, 128), block_count.reshape(L),
        ),
    )
    gradient = state.astype(F32) - background.astype(F32) + back.astype(F32)
    return misfit.reshape(L, 1, 1, 16, 128), gradient


def solution(mesh):
    return jax.shard_map(
        body,
        mesh=mesh,
        in_specs=(
            P("lat", None, "chan"),
            P("lat", None, "chan"),
            P(),
            P(None, "chan"),
            P(None, "chan"),
            P(None, "chan"),
            P("chan", None),
            P("chan", None),
            P("lat", "chan", None, None, None, None),
            P("lat", "chan", None, None, None),
            P("lat", "chan", None, None),
            P("lat", "chan", None),
        ),
        out_specs=(P(None, "chan", "lat", None, None), P("lat", None, "chan")),
        check_vma=False,
    )
```

```python
import functools

import jax
import jax.numpy as jnp
from jax import lax
from jax.experimental import pallas as pl
from jax.experimental.pallas import tpu as pltpu
from jax.sharding import PartitionSpec as P

D = 1024
HD = 64
VARS = 69
EPSILON = 1e-05
VP = 80
T = 256
G = 8
L = 16
BIG = 1e30
MESH = pl.DeviceIdType.MESH
BF = jnp.bfloat16
F32 = jnp.float32
VMEM_LIMIT = 62 * 1024 * 1024


def nn(a, b):
    return lax.dot_general(a, b, (((1,), (0,)), ((), ())), preferred_element_type=F32)


def nt(a, b):
    return lax.dot_general(a, b, (((1,), (1,)), ((), ())), preferred_element_type=F32)


def place():
    b = lax.axis_index("lat")
    c = lax.axis_index("chan")
    k = b % 2
    big = b // 2
    q = 2 * (c % 4) + k
    row = q + (big % 2) * (7 - 2 * q)
    return b, c, k, big, row, c // 4


def holder(big, row, w):
    q = row + (big % 2) * (7 - 2 * row)
    return big * 2 + q % 2, w * 4 + q // 2


def neighbours():
    b, c, k, big, row, w = place()
    q = 2 * (c % 4) + k
    step = 1 - 2 * (big % 2)
    inner_up = (row > 0).astype(jnp.int32)
    inner_down = (row < 7).astype(jnp.int32)
    q_up, q_down = q - step * inner_up, q + step * inner_down
    up = ((big - 1 + inner_up) * 2 + q_up % 2, w * 4 + q_up // 2)
    down = ((big + 1 - inner_down) * 2 + q_down % 2, w * 4 + q_down // 2)
    return up, down, big * 8 + row > 0, big * 8 + row < 4 * L - 1


def lat_peer(i):
    b, c = lax.axis_index("lat"), lax.axis_index("chan")
    return ((b + i) % L, c)


def far_flip():
    b, c = lax.axis_index("lat"), lax.axis_index("chan")
    return (b + 2 - 4 * ((b // 2) % 2), (c + 4) % G)


def greet():
    b, c, k, big, _, _ = place()
    barrier = pltpu.get_barrier_semaphore()
    peers = [(b, (c + i) % G) for i in range(1, G)]
    peers += [(b + 1 - 2 * k, (c + i) % G) for i in range(G)]
    peers += [(2 * ((big + i) % 8) + j, c) for i in range(1, 8) for j in range(2)]
    peers.append(far_flip())
    for dev in peers:
        pl.semaphore_signal(barrier, inc=1, device_id=dev, device_id_type=MESH)
    pl.semaphore_wait(barrier, len(peers))


def remote(src, dst, ss, rs, dev):
    return pltpu.make_async_remote_copy(
        src_ref=src, dst_ref=dst, send_sem=ss, recv_sem=rs, device_id=dev, device_id_type=MESH
    )


def call(kernel, out_shape, in_specs, out_specs, scratch, cid, name, args):
    return pl.pallas_call(
        kernel,
        out_shape=out_shape,
        in_specs=in_specs,
        out_specs=out_specs,
        scratch_shapes=scratch,
        compiler_params=pltpu.CompilerParams(
            collective_id=cid, has_side_effects=cid is not None, vmem_limit_bytes=VMEM_LIMIT
        ),
        name=name,
    )(*args)


VM = pl.BlockSpec(memory_space=pltpu.VMEM)
ANY = pl.BlockSpec(memory_space=pl.ANY)
DMA = pltpu.SemaphoreType.DMA


def sds(shape, dtype):
    return jax.ShapeDtypeStruct(shape, dtype)


class Spread:
    def __init__(self, view, size, sems):
        self.view, self.half = view, size // 2
        self.s1, self.r1, self.s2, self.r2, self.s3, self.r3, self.s4, self.r4, self.s5, self.r5 = sems
        b, c, k, _, _, z = place()
        x, y = c % 4, b // 4
        p = y % 2
        self.b, self.c, self.x, self.z = b, c, x, z
        self.start = (p * 2 + k) * size
        self.across = ((1 - p) * 2 + k) * size
        self.turn = (1 - 2 * k) * size
        self.core = (b + 1 - 2 * k, c)
        self.ups = [((b + 4) % L, c), ((b + 12) % L, c)]
        self.flips = [(b, (c + 4) % G), far_flip()]
        self.sent = []

    def send(self, g, start, size, ss, rs, dev):
        ref = self.view(g, start, size)
        copy = remote(ref, ref, ss, rs, dev)
        copy.start()
        self.sent.append(copy)

    def wait(self, g, start, size, rs):
        ref = self.view(g, start, size)
        remote(ref, ref, self.s1.at[0], rs, self.core).wait_recv()

    def from_x(self, i):
        return self.z * 4 + (self.x + 4 - i) % 4

    def from_z(self, i):
        return (1 - self.z) * 4 + (self.x + 4 - i) % 4

    def others(self):
        return [self.from_x(i) for i in (1, 3, 2)] + [self.from_z(i) for i in (0, 1, 3, 2)]

    def along_z(self, g):
        for h in range(2):
            at = self.start + h * self.half
            self.send(g, at, self.half, self.s2.at[h, g], self.r2.at[h, g], self.flips[h])

    def first(self):
        for i in (1, 3, 2):
            dev = (self.b, self.z * 4 + (self.x + i) % 4)
            self.send(self.c, self.start, 2 * self.half, self.s1.at[i], self.r1.at[self.c], dev)
        self.along_z(self.c)

    def fan(self, g, h):
        at = self.start + h * self.half
        self.send(g, at, self.half, self.s4.at[h, g], self.r4.at[h, g], self.ups[h])
        self.send(g, at, self.half, self.s3.at[h, g], self.r3.at[h, g], self.core)

    def relay_x(self):
        for i in (1, 3, 2):
            g = self.from_x(i)
            self.wait(g, self.start, 2 * self.half, self.r1.at[g])
            self.along_z(g)
            self.fan(g, 0)
            self.fan(g, 1)

    def relay_z(self):
        for i in (0, 1, 3, 2):
            g = self.from_z(i)
            for h in range(2):
                self.wait(g, self.start + h * self.half, self.half, self.r2.at[h, g])
                self.fan(g, h)

    def relay_y(self):
        for g in self.others():
            for h in range(2):
                at = self.across + h * self.half
                self.wait(g, at, self.half, self.r4.at[h, g])
                self.send(g, at, self.half, self.s5.at[h, g], self.r5.at[h, g], self.core)

    def ready(self):
        for g in self.others():
            for h in range(2):
                self.wait(g, self.start + self.turn + h * self.half, self.half, self.r3.at[h, g])
                self.wait(g, self.across + self.turn + h * self.half, self.half, self.r5.at[h, g])

    def finish(self):
        for copy in self.sent:
            copy.wait_send()


def wide(ref, h):
    return jnp.concatenate([ref[h, g] for g in range(G)], axis=1)


def moments(x):
    mean = jnp.sum(x, axis=-1, keepdims=True) * (1.0 / D)
    centred = x - mean
    var = jnp.sum(centred * centred, axis=-1, keepdims=True) * (1.0 / D)
    inv = lax.rsqrt(var + EPSILON)
    return centred * inv, inv


def only(value, hh):
    first = lax.broadcasted_iota(jnp.int32, value.shape, 1) < HD
    keep = first if hh == 0 else jnp.logical_not(first)
    return jnp.where(keep, value, jnp.zeros_like(value))


def swap_rows(src, above, below, ss, rs):
    up, down, has_up, has_down = neighbours()
    to_up = remote(src, below, ss.at[0], rs.at[0], up)
    to_down = remote(src, above, ss.at[1], rs.at[1], down)

    def start():
        pl.when(has_up)(lambda: to_up.start())
        pl.when(has_down)(lambda: to_down.start())

    def wait():
        @pl.when(has_up)
        def _():
            to_up.wait_send()
            to_down.wait_recv()

        @pl.when(has_down)
        def _():
            to_down.wait_send()
            to_up.wait_recv()

    return start, wait


def loop(n, step):
    def wrapped(i, carry):
        step(i)
        return carry

    lax.fori_loop(0, n, wrapped, 0)


SCRATCH = dict(
    x_v=pltpu.VMEM((3, G, T, 128), BF),
    w_v=pltpu.VMEM((G, 3, D, 128), BF),
    o_v=pltpu.VMEM((G, 128, D), BF),
    d_v=pltpu.VMEM((G, VP, 128), BF),
    i_v=pltpu.VMEM((L, 16, 128), jnp.int32),
    itp=pltpu.VMEM((L, 16, 128, 128), BF),
    n_v=pltpu.VMEM((3 * T, D), BF),
    qkv=pltpu.VMEM((3, G, 3 * T, 128), BF),
    kt=pltpu.VMEM((G, 128, 3 * T), BF),
    mix=pltpu.VMEM((G, T, 128), BF),
    acc=pltpu.VMEM((T, D), F32),
    ml=pltpu.VMEM((2, 16, 1, T), F32),
    mlh=pltpu.VMEM((2, 2, 16, 1, T), F32),
    fields=pltpu.VMEM((G, VP, T), BF),
    mine=pltpu.VMEM((L, 16, 128), BF),
    picked=pltpu.VMEM((L, 16, 128), BF),
    am=pltpu.VMEM((L, 32, 128), BF),
    came=pltpu.VMEM((L, 32, 128), BF),
    parts=pltpu.VMEM((G, VP, T), BF),
    got=pltpu.VMEM((G, VP, T), BF),
    gf=pltpu.VMEM((3, VP, T), F32),
    gu=pltpu.VMEM((T, D), F32),
    low=pltpu.VMEM((3 * T, D), BF),
    do=pltpu.VMEM((G, 3 * T, 128), BF),
    dq=pltpu.VMEM((G, T, 128), BF),
    dkv=pltpu.VMEM((2, G, T, 128), F32),
    delta=pltpu.VMEM((16, 1, T), F32),
    delta_h=pltpu.VMEM((2, 16, 1, T), F32),
    outgo=pltpu.VMEM((G, T, 128), BF),
    f_own=pltpu.VMEM((VP, T), BF),
    i_own=pltpu.VMEM((L, 16, 128), jnp.int32),
    loc=DMA((8,)),
    s_state=DMA((G,)), r_state=DMA((G,)),
    s_d=DMA((G,)), r_d=DMA((G,)),
    s_i=DMA((L,)), r_i=DMA((L,)),
    s_h=DMA((2, G)), r_h=DMA((2, G)),
    s_f=DMA((G,)), r_f=DMA((G,)),
    s_p=DMA((L,)), r_p=DMA((L,)),
    s_a=DMA((L,)), r_a=DMA((L,)),
    s_g=DMA((G,)), r_g=DMA((G,)),
    s_y=DMA((G,)), r_y=DMA((G,)),
    s_m=DMA((2,)), r_m=DMA((2,)),
    s_gh=DMA((2,)), r_gh=DMA((2,)),
    s_dl=DMA((2, 2)), r_dl=DMA((2, 2)),
    w1=DMA((4,)), w2=DMA((G,)), w3=DMA((2, G)), w4=DMA((2, G)), w5=DMA((2, G)), w6=DMA((2, G)), w7=DMA((2, G)), w8=DMA((2, G)), w9=DMA((2, G)), w10=DMA((2, G)),
    o1=DMA((4,)), o2=DMA((G,)), o3=DMA((2, G)), o4=DMA((2, G)), o5=DMA((2, G)), o6=DMA((2, G)), o7=DMA((2, G)), o8=DMA((2, G)), o9=DMA((2, G)), o10=DMA((2, G)),
)


class Refs:
    pass


def kernel(state, wq, wk, wv, wo, dec, idx, gain, interp, obs, count, misfit, back, *scratch):
    s = Refs()
    for name, ref in zip(SCRATCH, scratch):
        setattr(s, name, ref)
    b, c, k, big, row8, w = place()
    r = row8 % 4
    band = 2 * big + row8 // 4
    j_own = r * 2 + w
    home = band == b
    up, down, has_up, has_down = neighbours()
    up_bias = jnp.where(has_up, 0.0, -BIG).astype(F32)
    down_bias = jnp.where(has_down, 0.0, -BIG).astype(F32)
    own_rows = pl.ds(0, T)
    eighth = jnp.asarray(0.125, BF)
    away = jnp.logical_not(home)
    windows = [holder(big, 4 * k + j // 2, j % 2) for j in range(G)]
    mine_at = [jnp.logical_and(home, j_own == j) for j in range(G)]
    members = [(band, (c + i) % G) for i in range(G)]

    local = [
        pltpu.make_async_copy(wq, s.w_v.at[c, 0], s.loc.at[0]),
        pltpu.make_async_copy(wk, s.w_v.at[c, 1], s.loc.at[1]),
        pltpu.make_async_copy(wv, s.w_v.at[c, 2], s.loc.at[2]),
        pltpu.make_async_copy(wo, s.o_v.at[c], s.loc.at[3]),
    ]
    for copy in local:
        copy.start()

    @pl.when(jnp.logical_not(has_up))
    def _():
        s.x_v[0] = jnp.zeros((G, T, 128), BF)

    @pl.when(jnp.logical_not(has_down))
    def _():
        s.x_v[2] = jnp.zeros((G, T, 128), BF)

    s.mlh[:, 0] = jnp.full((2, 16, 1, T), BIG, F32)
    s.mlh[:, 1] = jnp.zeros((2, 16, 1, T), F32)
    s.delta_h[...] = jnp.zeros_like(s.delta_h)
    s.gf[...] = jnp.zeros_like(s.gf)
    eye = lax.broadcasted_iota(jnp.int32, (VP, VARS), 0) == lax.broadcasted_iota(jnp.int32, (VP, VARS), 1)
    s.d_v[c] = nt(eye.astype(F32).astype(BF), dec[...]).astype(BF)
    for n in range(16):
        s.i_own[:, n, :] = jnp.broadcast_to(idx[:, n : n + 1], (L, 128))
    s.i_v[b] = s.i_own[b]
    greet()

    sends = []

    def send_state(j, act):
        src = state.at[j // 2, pl.ds((j % 2) * T, T)]

        @pl.when(jnp.logical_not(mine_at[j]))
        def _():
            copy = remote(src, s.x_v.at[1, c], s.s_state.at[j], s.r_state.at[c], windows[j])
            copy.start() if act else copy.wait_send()

        if act:
            @pl.when(mine_at[j])
            def _():
                pltpu.make_async_copy(src, s.x_v.at[1, c], s.loc.at[4]).start()

    for j in range(G):
        send_state(j, True)
    weights = Spread(
        lambda g, at, n: s.w_v.at[g, :, pl.ds(at, n)], 256, (s.w1, s.w2, s.w3, s.w4, s.w5, s.w6, s.w7, s.w8, s.w9, s.w10)
    )
    outs = Spread(
        lambda g, at, n: s.o_v.at[g, pl.ds(at, n)], 32, (s.o1, s.o2, s.o3, s.o4, s.o5, s.o6, s.o7, s.o8, s.o9, s.o10)
    )
    for copy in local[:3]:
        copy.wait()
    weights.first()
    fetch = pltpu.make_async_copy(interp, s.itp, s.loc.at[5])
    fetch.start()
    for i in range(1, L):
        dev = lat_peer(i)
        copy = remote(s.i_own.at[dev[0]], s.i_v.at[b], s.s_i.at[i], s.r_i.at[i], dev)
        copy.start()
        sends.append(copy)

    def halo(g, sem):
        to_up = remote(s.x_v.at[1, g], s.x_v.at[2, g], s.s_h.at[0, sem], s.r_h.at[0, sem], up)
        to_down = remote(s.x_v.at[1, g], s.x_v.at[0, g], s.s_h.at[1, sem], s.r_h.at[1, sem], down)
        return to_up, to_down

    def start_halo(g, sem):
        to_up, to_down = halo(g, sem)
        pl.when(has_up)(lambda: to_up.start())
        pl.when(has_down)(lambda: to_down.start())

    def got_state(g):
        piece = s.x_v.at[1, g]
        remote(piece, piece, s.s_state.at[0], s.r_state.at[g], members[1]).wait_recv()

    @pl.when(home)
    def _():
        pltpu.make_async_copy(state.at[0, pl.ds(0, T)], s.x_v.at[1, c], s.loc.at[4]).wait()

    pl.when(away)(lambda: got_state(c))
    start_halo(c, 0)
    for i in (1, 3, 4, 5, 7, 2, 6):
        g = (c + i) % G
        got_state(g)
        start_halo(g, i)
    weights.relay_x()
    local[3].wait()
    outs.first()
    for i in range(1, G):
        copy = remote(s.d_v.at[c], s.d_v.at[c], s.s_d.at[i], s.r_d.at[i], (b, (c + i) % G))
        copy.start()
        sends.append(copy)

    def norm(h, at):
        hat, _ = moments(wide(s.x_v, h).astype(F32))
        s.n_v[pl.ds(at * T, T), :] = (hat * gain[...]).astype(BF)

    norm(1, 0)
    weights.relay_z()
    weights.relay_y()

    def project(rows, n):
        def step(m):
            both = [s.w_v[2 * m + e, i] for e in range(2) for i in range(3)]
            res = nn(s.n_v[pl.ds(rows, n), :], jnp.concatenate(both, axis=1))
            for e in range(2):
                for i in range(3):
                    s.qkv[i, 2 * m + e, pl.ds(rows, n), :] = res[:, (3 * e + i) * 128 : (3 * e + i + 1) * 128].astype(BF)

        return step

    weights.ready()
    loop(G // 2, project(0, T))
    for i in range(G):
        to_up, to_down = halo((c + i) % G, i)
        pl.when(has_down)(lambda: to_up.wait_recv())
        pl.when(has_up)(lambda: to_down.wait_recv())
    norm(0, 1)
    norm(2, 2)
    loop(G // 2, project(T, 2 * T))

    def attend(g):
        query = s.qkv[0, g, own_rows, :] * eighth
        s.kt[g] = jnp.transpose(s.qkv[1, g].astype(F32)).astype(BF)
        vt = jnp.transpose(s.qkv[2, g].astype(F32)).astype(BF)
        parts = []
        for hh in range(2):
            q = only(query, hh)
            sc = nt(s.qkv[1, g], q)
            m0 = jnp.max(sc[:T], axis=0, keepdims=True)
            m1 = jnp.max(sc[T : 2 * T], axis=0, keepdims=True) + up_bias
            m2 = jnp.max(sc[2 * T :], axis=0, keepdims=True) + down_bias
            m = jnp.maximum(jnp.maximum(m0, m1), m2)
            e0 = jnp.exp(sc[:T] - m)
            e1 = jnp.exp(sc[T : 2 * T] - (m - up_bias))
            e2 = jnp.exp(sc[2 * T :] - (m - down_bias))
            l = jnp.sum(e0, axis=0, keepdims=True) + jnp.sum(e1, axis=0, keepdims=True) + jnp.sum(e2, axis=0, keepdims=True)
            inv = 1.0 / l
            p = jnp.concatenate([(e0 * inv).astype(BF), (e1 * inv).astype(BF), (e2 * inv).astype(BF)], axis=0)
            parts.append(nn(vt[hh * HD : (hh + 1) * HD], p))
            s.ml[0, 2 * g + hh] = m
            s.ml[1, 2 * g + hh] = inv
        s.mix[g] = jnp.transpose(jnp.concatenate(parts, axis=0)).astype(BF)

    loop(2, attend)
    outs.relay_x()
    loop(2, lambda g: attend(g + 2))
    outs.relay_z()
    loop(2, lambda g: attend(g + 4))
    outs.relay_y()
    loop(2, lambda g: attend(g + 6))
    start_ml, wait_ml = swap_rows(s.ml, s.mlh.at[0], s.mlh.at[1], s.s_m, s.r_m)
    start_ml()
    outs.ready()
    for i in range(1, G):
        remote(s.d_v.at[c], s.d_v.at[c], s.s_d.at[i], s.r_d.at[i], members[i]).wait_recv()
    s.acc[...] = jnp.zeros_like(s.acc)

    def out(g):
        s.acc[...] += nn(s.mix[g], s.o_v[g]).astype(BF).astype(F32)

    loop(G, out)
    updated = (wide(s.x_v, 1).astype(F32) + s.acc[...]).astype(BF)
    dec_all = jnp.concatenate([s.d_v[g] for g in range(G)], axis=1)
    s.f_own[...] = nt(dec_all, updated).astype(BF)

    def send_fields(i, act):
        copy = remote(s.f_own, s.fields.at[j_own], s.s_f.at[i], s.r_f.at[j_own], members[i])
        copy.start() if act else copy.wait_send()

    for i in range(1, G):
        send_fields(i, True)
    pl.when(away)(lambda: send_fields(0, True))

    @pl.when(home)
    def _():
        s.fields[j_own] = s.f_own[...]

    for i in range(1, L):
        remote(s.i_own.at[b], s.i_v.at[b], s.s_i.at[i], s.r_i.at[i], lat_peer(i)).wait_recv()
    index = s.i_v[...].reshape(16 * L, 128)
    lanes = lax.broadcasted_iota(jnp.int32, (16 * L, 128), 1) * 16

    total = jnp.zeros((16 * L, 128), F32)
    for j in range(G):
        @pl.when(jnp.logical_not(mine_at[j]))
        def _():
            remote(s.f_own, s.fields.at[j], s.s_f.at[0], s.r_f.at[j], windows[j]).wait_recv()

        for half in range(2):
            hot = (index == lanes + (2 * j + half)).astype(F32).astype(BF)
            total = total + nn(hot[:, :VP], s.fields[j, :, pl.ds(half * 128, 128)])
    s.mine[...] = total.astype(BF).reshape(L, 16, 128)
    for i in range(1, L):
        dev = lat_peer(i)
        copy = remote(s.mine.at[dev[0]], s.picked.at[b], s.s_p.at[i], s.r_p.at[i], dev)
        copy.start()
        sends.append(copy)
    s.picked[b] = s.mine[b]

    fetch.wait()
    row = lax.broadcasted_iota(jnp.int32, (16, 128), 0)

    def observe(i):
        other_b = (b + L - i) % L

        @pl.when(i > 0)
        def _():
            remote(s.mine.at[b], s.picked.at[b], s.s_p.at[i], s.r_p.at[i], (other_b, c)).wait_recv()

        flat = s.itp[other_b].reshape(2048, 128)
        big = nt(s.picked[other_b], flat)
        pred = jnp.zeros((16, 128), F32)
        for n in range(16):
            pred = jnp.where(row == n, big[:, n * 128 : (n + 1) * 128], pred)
        mis = jnp.where(row < count[other_b], pred - obs[other_b].astype(F32), 0.0).astype(BF)
        lhs = jnp.concatenate([jnp.where(row == n, mis, jnp.zeros_like(mis)) for n in range(16)], axis=1)
        s.am[other_b, :16, :] = nn(lhs, flat).astype(BF)
        s.am[other_b, 16:, :] = mis

        @pl.when(i > 0)
        def _():
            remote(s.am.at[other_b], s.came.at[b], s.s_a.at[i], s.r_a.at[i], (other_b, c)).start()

    loop(L, observe)
    s.came[b] = s.am[b]

    index_t = jnp.transpose(index.astype(F32))[:VP].astype(jnp.int32)
    sub = lax.broadcasted_iota(jnp.int32, (VP, 16 * L), 0) * 16

    def arrived(i):
        other_b = (b + i) % L

        @pl.when(i > 0)
        def _():
            remote(s.am.at[b], s.came.at[b], s.s_a.at[i], s.r_a.at[i], (other_b, c)).wait()

    loop(L, arrived)
    misfit[...] = s.came[:, 16:, :].astype(F32)
    adjoint = s.came[:, :16, :].reshape(16 * L, 128)
    for j in range(G):
        for half in range(2):
            hot = (index_t == sub + (2 * j + half)).astype(F32).astype(BF)
            s.parts[j, :, pl.ds(half * 128, 128)] = nn(hot, adjoint).astype(BF)

        @pl.when(jnp.logical_not(mine_at[j]))
        def _():
            remote(s.parts.at[j], s.got.at[c], s.s_g.at[j], s.r_g.at[c], windows[j]).start()

        @pl.when(mine_at[j])
        def _():
            s.got[c] = s.parts[j]

    def got_part(g):
        remote(s.parts.at[0], s.got.at[g], s.s_g.at[0], s.r_g.at[g], members[1]).wait_recv()

    pl.when(away)(lambda: got_part(c))
    total = s.got[c].astype(F32)
    for i in range(1, G):
        got_part((c + i) % G)
        total = total + s.got[(c + i) % G].astype(F32)
    s.gf[0] = total
    start_gf, wait_gf = swap_rows(s.gf.at[0], s.gf.at[1], s.gf.at[2], s.s_gh, s.r_gh)
    start_gf()
    wait_ml()

    dec_all = jnp.concatenate([dec_all, jnp.zeros((128 - VP, D), BF)], axis=0)
    dec3 = jnp.concatenate([dec_all, dec_all, dec_all], axis=0)

    def update_of(h):
        field = jnp.transpose(jnp.concatenate([s.gf[h], jnp.zeros((128 - VP, T), F32)], axis=0))
        hi = field.astype(BF)
        rest = field - hi.astype(F32)
        mid = rest.astype(BF)
        lo = (rest - mid.astype(F32)).astype(BF)
        update = nn(jnp.concatenate([hi, mid, lo], axis=1), dec3)
        s.low[pl.ds(h * T, T), :] = update.astype(BF)
        return update

    s.gu[...] = update_of(0)
    wait_gf()
    update_of(1)
    update_of(2)

    def mixed(m):
        res = nt(s.low[...], jnp.concatenate([s.o_v[2 * m], s.o_v[2 * m + 1]], axis=0)).astype(BF)
        s.do[2 * m] = res[:, :128]
        s.do[2 * m + 1] = res[:, 128:]

    loop(G // 2, mixed)

    def own(g):
        query = s.qkv[0, g, own_rows, :] * eighth
        parts = []
        dk = jnp.zeros((T, 128), F32)
        dv = jnp.zeros((T, 128), F32)
        for hh in range(2):
            n = 2 * g + hh
            q = only(query, hh)
            d = only(s.do[g, own_rows, :], hh)
            m, inv = s.ml[0, n], s.ml[1, n]
            sc = nt(s.qkv[1, g], q)
            dp = nt(s.qkv[2, g], d)
            p0 = jnp.exp(sc[:T] - m) * inv
            p1 = jnp.exp(sc[T : 2 * T] - (m - up_bias)) * inv
            p2 = jnp.exp(sc[2 * T :] - (m - down_bias)) * inv
            p = jnp.concatenate([p0, p1, p2], axis=0)
            along = jnp.sum(p * dp, axis=0, keepdims=True)
            s.delta[n] = along
            ds = (p * (dp - along)).astype(BF)
            parts.append(nn(s.kt[g, pl.ds(hh * HD, HD), :], ds) * 0.125)
            dk = dk + nn(ds[:T], q)
            dv = dv + nn(p0.astype(BF), d)
        s.dq[g] = jnp.transpose(jnp.concatenate(parts, axis=0)).astype(BF)
        s.dkv[0, g] = dk
        s.dkv[1, g] = dv

    def other(g):
        dk = s.dkv[0, g]
        dv = s.dkv[1, g]
        for side in range(2):
            rows = pl.ds((1 + side) * T, T)
            query = s.qkv[0, g, rows, :] * eighth
            for hh in range(2):
                n = 2 * g + hh
                q = only(query, hh)
                d = only(s.do[g, rows, :], hh)
                sc = nt(s.qkv[1, g, own_rows, :], q)
                dp = nt(s.qkv[2, g, own_rows, :], d)
                p = jnp.exp(sc - s.mlh[side, 0, n]) * s.mlh[side, 1, n]
                ds = (p * (dp - s.delta_h[side, n])).astype(BF)
                dk = dk + nn(ds, q)
                dv = dv + nn(p.astype(BF), d)
        three = jnp.concatenate([s.dq[g], dk.astype(BF), dv.astype(BF)], axis=1)
        wide_w = jnp.concatenate([s.w_v[g, 0], s.w_v[g, 1], s.w_v[g, 2]], axis=1)
        s.acc[...] += nt(three, wide_w).astype(BF).astype(F32)

    swaps = []
    for n in range(2):
        loop(4, lambda g: own(g + 4 * n))
        heads = pl.ds(8 * n, 8)
        start, wait = swap_rows(
            s.delta.at[heads], s.delta_h.at[0, heads], s.delta_h.at[1, heads], s.s_dl.at[n], s.r_dl.at[n]
        )
        start()
        swaps.append(wait)
    s.acc[...] = jnp.zeros_like(s.acc)
    for n in range(2):
        swaps[n]()
        loop(4, lambda g: other(g + 4 * n))

    hat, inv = moments(wide(s.x_v, 1).astype(F32))
    grad_hat = s.acc[...] * gain[...]
    mean = jnp.sum(grad_hat, axis=-1, keepdims=True) * (1.0 / D)
    cross = jnp.sum(grad_hat * hat, axis=-1, keepdims=True) * (1.0 / D)
    total = (s.gu[...] + (grad_hat - mean - hat * cross) * inv).astype(BF)
    for g in range(G):
        s.outgo[g] = total[:, g * 128 : (g + 1) * 128]
    def send_back(i, act):
        dev = members[i]
        copy = remote(s.outgo.at[dev[1]], back.at[r, pl.ds(w * T, T)], s.s_y.at[i], s.r_y.at[j_own], dev)
        copy.start() if act else copy.wait_send()

    for i in range(1, G):
        send_back(i, True)
    pl.when(away)(lambda: send_back(0, True))

    @pl.when(home)
    def _():
        back[r, pl.ds(w * T, T), :] = s.outgo[c]

    weights.finish()
    outs.finish()
    for copy in sends:
        copy.wait_send()
    for i in range(G):
        to_up, to_down = halo((c + i) % G, i)
        pl.when(has_up)(lambda: to_up.wait_send())
        pl.when(has_down)(lambda: to_down.wait_send())
    for i in range(1, G):
        send_fields(i, False)
        send_back(i, False)

    @pl.when(away)
    def _():
        send_fields(0, False)
        send_back(0, False)

    for j in range(G):
        send_state(j, False)

        @pl.when(jnp.logical_not(mine_at[j]))
        def _():
            remote(s.parts.at[j], s.got.at[c], s.s_g.at[j], s.r_g.at[c], windows[j]).wait_send()
            piece = back.at[j // 2, pl.ds((j % 2) * T, T)]
            remote(s.outgo.at[0], piece, s.s_y.at[0], s.r_y.at[j], windows[j]).wait_recv()


def body(state, background, gain, w_query, w_key, w_value, w_out, decoder, interp, obs_values, tile_index, block_count):
    smem = pl.BlockSpec(memory_space=pltpu.SMEM)
    misfit, back = call(
        kernel,
        (sds((L, 16, 128), F32), sds((4, 512, 128), BF)),
        [ANY] * 5 + [VM, VM, VM, ANY, VM, smem],
        [VM] * 2,
        list(SCRATCH.values()),
        0,
        "whole",
        (
            state, w_query, w_key, w_value, w_out, decoder, tile_index.reshape(L, 16), gain.reshape(1, D),
            interp.reshape(L, 16, 128, 128), obs_values.reshape(L, 16, 128), block_count.reshape(L),
        ),
    )
    gradient = state.astype(F32) - background.astype(F32) + back.astype(F32)
    return misfit.reshape(L, 1, 1, 16, 128), gradient


def solution(mesh):
    return jax.shard_map(
        body,
        mesh=mesh,
        in_specs=(
            P("lat", None, "chan"),
            P("lat", None, "chan"),
            P(),
            P(None, "chan"),
            P(None, "chan"),
            P(None, "chan"),
            P("chan", None),
            P("chan", None),
            P("lat", "chan", None, None, None, None),
            P("lat", "chan", None, None, None),
            P("lat", "chan", None, None),
            P("lat", "chan", None),
        ),
        out_specs=(P(None, "chan", "lat", None, None), P("lat", None, "chan")),
        check_vma=False,
    )
```

```python
import functools

import jax
import jax.numpy as jnp
from jax import lax
from jax.experimental import pallas as pl
from jax.experimental.pallas import tpu as pltpu
from jax.sharding import PartitionSpec as P

D = 1024
HD = 64
VARS = 69
EPSILON = 1e-05
VP = 80
T = 256
G = 8
L = 16
BIG = 1e30
MESH = pl.DeviceIdType.MESH
BF = jnp.bfloat16
F32 = jnp.float32
VMEM_LIMIT = 62 * 1024 * 1024


def nn(a, b):
    return lax.dot_general(a, b, (((1,), (0,)), ((), ())), preferred_element_type=F32)


def nt(a, b):
    return lax.dot_general(a, b, (((1,), (1,)), ((), ())), preferred_element_type=F32)


def place():
    b = lax.axis_index("lat")
    c = lax.axis_index("chan")
    k = b % 2
    big = b // 2
    q = 2 * (c % 4) + k
    row = q + (big % 2) * (7 - 2 * q)
    return b, c, k, big, row, c // 4


def holder(big, row, w):
    q = row + (big % 2) * (7 - 2 * row)
    return big * 2 + q % 2, w * 4 + q // 2


def neighbours():
    b, c, k, big, row, w = place()
    q = 2 * (c % 4) + k
    step = 1 - 2 * (big % 2)
    inner_up = (row > 0).astype(jnp.int32)
    inner_down = (row < 7).astype(jnp.int32)
    q_up, q_down = q - step * inner_up, q + step * inner_down
    up = ((big - 1 + inner_up) * 2 + q_up % 2, w * 4 + q_up // 2)
    down = ((big + 1 - inner_down) * 2 + q_down % 2, w * 4 + q_down // 2)
    return up, down, big * 8 + row > 0, big * 8 + row < 4 * L - 1


def lat_peer(i):
    b, c = lax.axis_index("lat"), lax.axis_index("chan")
    return ((b + i) % L, c)


def far_flip():
    b, c = lax.axis_index("lat"), lax.axis_index("chan")
    return (b + 2 - 4 * ((b // 2) % 2), (c + 4) % G)


def greet():
    b, c, k, big, _, _ = place()
    barrier = pltpu.get_barrier_semaphore()
    peers = [(b, (c + i) % G) for i in range(1, G)]
    peers += [(b + 1 - 2 * k, (c + i) % G) for i in range(G)]
    peers += [(2 * ((big + i) % 8) + j, c) for i in range(1, 8) for j in range(2)]
    peers.append(far_flip())
    for dev in peers:
        pl.semaphore_signal(barrier, inc=1, device_id=dev, device_id_type=MESH)
    pl.semaphore_wait(barrier, len(peers))


def remote(src, dst, ss, rs, dev):
    return pltpu.make_async_remote_copy(
        src_ref=src, dst_ref=dst, send_sem=ss, recv_sem=rs, device_id=dev, device_id_type=MESH
    )


def call(kernel, out_shape, in_specs, out_specs, scratch, cid, name, args):
    return pl.pallas_call(
        kernel,
        out_shape=out_shape,
        in_specs=in_specs,
        out_specs=out_specs,
        scratch_shapes=scratch,
        compiler_params=pltpu.CompilerParams(
            collective_id=cid, has_side_effects=cid is not None, vmem_limit_bytes=VMEM_LIMIT
        ),
        name=name,
    )(*args)


VM = pl.BlockSpec(memory_space=pltpu.VMEM)
ANY = pl.BlockSpec(memory_space=pl.ANY)
DMA = pltpu.SemaphoreType.DMA


def sds(shape, dtype):
    return jax.ShapeDtypeStruct(shape, dtype)


class Spread:
    def __init__(self, view, size, sems):
        self.view, self.half = view, size // 2
        self.s1, self.r1, self.s2, self.r2, self.s3, self.r3, self.s4, self.r4, self.s5, self.r5 = sems
        b, c, k, _, _, z = place()
        x, y = c % 4, b // 4
        p = y % 2
        self.b, self.c, self.x, self.z = b, c, x, z
        self.start = (p * 2 + k) * size
        self.across = ((1 - p) * 2 + k) * size
        self.turn = (1 - 2 * k) * size
        self.core = (b + 1 - 2 * k, c)
        self.ups = [((b + 4) % L, c), ((b + 12) % L, c)]
        self.flips = [(b, (c + 4) % G), far_flip()]

    def send(self, g, start, size, ss, rs, dev):
        ref = self.view(g, start, size)
        copy = remote(ref, ref, ss, rs, dev)
        copy.start()

    def wait(self, g, start, size, rs):
        ref = self.view(g, start, size)
        remote(ref, ref, self.s1.at[0], rs, self.core).wait_recv()

    def from_x(self, i):
        return self.z * 4 + (self.x + 4 - i) % 4

    def from_z(self, i):
        return (1 - self.z) * 4 + (self.x + 4 - i) % 4

    def along_z(self, g):
        for h in range(2):
            at = self.start + h * self.half
            self.send(g, at, self.half, self.s2.at[h, g], self.r2.at[h, g], self.flips[h])

    def first(self):
        for i in (1, 3, 2):
            dev = (self.b, self.z * 4 + (self.x + i) % 4)
            self.send(self.c, self.start, 2 * self.half, self.s1.at[i], self.r1.at[self.c], dev)
        self.along_z(self.c)

    def fan(self, g, h):
        at = self.start + h * self.half
        self.send(g, at, self.half, self.s4.at[h, g], self.r4.at[h, g], self.ups[h])
        self.send(g, at, self.half, self.s3.at[h, g], self.r3.at[h, g], self.core)

    def relay_x(self, i):
        g = self.from_x(i)
        self.wait(g, self.start, 2 * self.half, self.r1.at[g])
        self.along_z(g)
        self.fan(g, 0)
        self.fan(g, 1)

    def relay_z(self, i):
        g = self.from_z(i)
        for h in range(2):
            self.wait(g, self.start + h * self.half, self.half, self.r2.at[h, g])
            self.fan(g, h)

    def relay_y(self, g):
        for h in range(2):
            at = self.across + h * self.half
            self.wait(g, at, self.half, self.r4.at[h, g])
            self.send(g, at, self.half, self.s5.at[h, g], self.r5.at[h, g], self.core)

    def ready(self, g):
        for h in range(2):
            self.wait(g, self.start + self.turn + h * self.half, self.half, self.r3.at[h, g])
            self.wait(g, self.across + self.turn + h * self.half, self.half, self.r5.at[h, g])

    def finish(self):
        def sent(g, start, size, sem):
            ref = self.view(g, start, size)
            remote(ref, ref, sem, self.r1.at[0], self.core).wait_send()

        half = self.half
        for i in (1, 3, 2):
            sent(self.c, self.start, 2 * half, self.s1.at[i])
        for i in range(4):
            row = self.from_x(i)
            for h in range(2):
                at = self.start + h * half
                sent(row, at, half, self.s2.at[h, row])
                for g in ([row] if i else []) + [self.from_z(i)]:
                    sent(g, at, half, self.s3.at[h, g])
                    sent(g, at, half, self.s4.at[h, g])
                    sent(g, self.across + h * half, half, self.s5.at[h, g])


def wide(ref, h):
    return jnp.concatenate([ref[h, g] for g in range(G)], axis=1)


def moments(x):
    mean = jnp.sum(x, axis=-1, keepdims=True) * (1.0 / D)
    centred = x - mean
    var = jnp.sum(centred * centred, axis=-1, keepdims=True) * (1.0 / D)
    inv = lax.rsqrt(var + EPSILON)
    return centred * inv, inv


def only(value, hh):
    first = lax.broadcasted_iota(jnp.int32, value.shape, 1) < HD
    keep = first if hh == 0 else jnp.logical_not(first)
    return jnp.where(keep, value, jnp.zeros_like(value))


def swap_rows(src, above, below, ss, rs):
    up, down, has_up, has_down = neighbours()
    to_up = remote(src, below, ss.at[0], rs.at[0], up)
    to_down = remote(src, above, ss.at[1], rs.at[1], down)

    def start():
        pl.when(has_up)(lambda: to_up.start())
        pl.when(has_down)(lambda: to_down.start())

    def wait():
        @pl.when(has_up)
        def _():
            to_up.wait_send()
            to_down.wait_recv()

        @pl.when(has_down)
        def _():
            to_down.wait_send()
            to_up.wait_recv()

    return start, wait


def loop(n, step):
    def wrapped(i, carry):
        step(i)
        return carry

    lax.fori_loop(0, n, wrapped, 0)


SCRATCH = dict(
    x_v=pltpu.VMEM((3, G, T, 128), BF),
    w_v=pltpu.VMEM((G, 3, D, 128), BF),
    o_v=pltpu.VMEM((G, 128, D), BF),
    d_v=pltpu.VMEM((G, VP, 128), BF),
    i_v=pltpu.VMEM((L, 16, 128), jnp.int32),
    itp=pltpu.VMEM((L, 16, 128, 128), BF),
    n_v=pltpu.VMEM((3 * T, D), BF),
    qkv=pltpu.VMEM((3, G, 3 * T, 128), BF),
    kt=pltpu.VMEM((G, 128, 3 * T), BF),
    mix=pltpu.VMEM((G, T, 128), BF),
    acc=pltpu.VMEM((T, D), F32),
    ml=pltpu.VMEM((2, 16, 1, T), F32),
    mlh=pltpu.VMEM((2, 2, 16, 1, T), F32),
    fields=pltpu.VMEM((G, VP, T), BF),
    mine=pltpu.VMEM((L, 16, 128), BF),
    picked=pltpu.VMEM((L, 16, 128), BF),
    am=pltpu.VMEM((L, 32, 128), BF),
    came=pltpu.VMEM((L, 32, 128), BF),
    parts=pltpu.VMEM((G, VP, T), BF),
    got=pltpu.VMEM((G, VP, T), BF),
    gf=pltpu.VMEM((3, VP, T), F32),
    gu=pltpu.VMEM((T, D), F32),
    do=pltpu.VMEM((G, 3 * T, 128), BF),
    dq=pltpu.VMEM((G, T, 128), BF),
    dso=pltpu.VMEM((G, T, 2 * T), BF),
    p_own=pltpu.VMEM((16, 3 * T, T), F32),
    p_nb=pltpu.VMEM((2, 16, T, T), F32),
    delta=pltpu.VMEM((16, 1, T), F32),
    delta_h=pltpu.VMEM((2, 16, 1, T), F32),
    f_own=pltpu.VMEM((VP, T), BF),
    i_own=pltpu.VMEM((L, 16, 128), jnp.int32),
    loc=DMA((8,)),
    s_state=DMA((G,)), r_state=DMA((G,)),
    s_d=DMA((G,)), r_d=DMA((G,)),
    s_i=DMA((L,)), r_i=DMA((L,)),
    s_h=DMA((2, G)), r_h=DMA((2, G)),
    s_f=DMA((G,)), r_f=DMA((G,)),
    s_p=DMA((L,)), r_p=DMA((L,)),
    s_a=DMA((L,)), r_a=DMA((L,)),
    s_g=DMA((G,)), r_g=DMA((G,)),
    s_y=DMA((G,)), r_y=DMA((G,)),
    s_m=DMA((2,)), r_m=DMA((2,)),
    s_gh=DMA((2,)), r_gh=DMA((2,)),
    s_dl=DMA((2, 2)), r_dl=DMA((2, 2)),
    w1=DMA((4,)), w2=DMA((G,)), w3=DMA((2, G)), w4=DMA((2, G)), w5=DMA((2, G)), w6=DMA((2, G)), w7=DMA((2, G)), w8=DMA((2, G)), w9=DMA((2, G)), w10=DMA((2, G)),
    o1=DMA((4,)), o2=DMA((G,)), o3=DMA((2, G)), o4=DMA((2, G)), o5=DMA((2, G)), o6=DMA((2, G)), o7=DMA((2, G)), o8=DMA((2, G)), o9=DMA((2, G)), o10=DMA((2, G)),
)


class Refs:
    pass


def kernel(state, wq, wk, wv, wo, dec, idx, gain, interp, obs, count, misfit, back, *scratch):
    s = Refs()
    for name, ref in zip(SCRATCH, scratch):
        setattr(s, name, ref)
    b, c, k, big, row8, w = place()
    r = row8 % 4
    band = 2 * big + row8 // 4
    j_own = r * 2 + w
    home = band == b
    up, down, has_up, has_down = neighbours()
    up_bias = jnp.where(has_up, 0.0, -BIG).astype(F32)
    down_bias = jnp.where(has_down, 0.0, -BIG).astype(F32)
    own_rows = pl.ds(0, T)
    eighth = jnp.asarray(0.125, BF)
    away = jnp.logical_not(home)
    windows = [holder(big, 4 * k + j // 2, j % 2) for j in range(G)]
    mine_at = [jnp.logical_and(home, j_own == j) for j in range(G)]
    members = [(band, (c + i) % G) for i in range(G)]

    local = [
        pltpu.make_async_copy(wq, s.w_v.at[c, 0], s.loc.at[0]),
        pltpu.make_async_copy(wk, s.w_v.at[c, 1], s.loc.at[1]),
        pltpu.make_async_copy(wv, s.w_v.at[c, 2], s.loc.at[2]),
        pltpu.make_async_copy(wo, s.o_v.at[c], s.loc.at[3]),
    ]
    for copy in local:
        copy.start()

    @pl.when(jnp.logical_not(has_up))
    def _():
        s.x_v[0] = jnp.zeros((G, T, 128), BF)

    @pl.when(jnp.logical_not(has_down))
    def _():
        s.x_v[2] = jnp.zeros((G, T, 128), BF)

    s.mlh[:, 0] = jnp.full((2, 16, 1, T), BIG, F32)
    s.mlh[:, 1] = jnp.zeros((2, 16, 1, T), F32)
    s.delta_h[...] = jnp.zeros_like(s.delta_h)
    s.gf[...] = jnp.zeros_like(s.gf)
    eye = lax.broadcasted_iota(jnp.int32, (VP, VARS), 0) == lax.broadcasted_iota(jnp.int32, (VP, VARS), 1)
    s.d_v[c] = nt(eye.astype(F32).astype(BF), dec[...]).astype(BF)
    for n in range(16):
        s.i_own[:, n, :] = jnp.broadcast_to(idx[:, n : n + 1], (L, 128))
    s.i_v[b] = s.i_own[b]
    greet()

    sends = []

    def send_state(j, act):
        src = state.at[j // 2, pl.ds((j % 2) * T, T)]

        @pl.when(jnp.logical_not(mine_at[j]))
        def _():
            copy = remote(src, s.x_v.at[1, c], s.s_state.at[j], s.r_state.at[c], windows[j])
            copy.start() if act else copy.wait_send()

        if act:
            @pl.when(mine_at[j])
            def _():
                pltpu.make_async_copy(src, s.x_v.at[1, c], s.loc.at[4]).start()

    for j in range(G):
        send_state(j, True)
    weights = Spread(
        lambda g, at, n: s.w_v.at[g, :, pl.ds(at, n)], 256, (s.w1, s.w2, s.w3, s.w4, s.w5, s.w6, s.w7, s.w8, s.w9, s.w10)
    )
    outs = Spread(
        lambda g, at, n: s.o_v.at[g, pl.ds(at, n)], 32, (s.o1, s.o2, s.o3, s.o4, s.o5, s.o6, s.o7, s.o8, s.o9, s.o10)
    )
    for copy in local[:3]:
        copy.wait()
    weights.first()
    fetch = pltpu.make_async_copy(interp, s.itp, s.loc.at[5])
    fetch.start()
    for i in range(1, L):
        dev = lat_peer(i)
        copy = remote(s.i_own.at[dev[0]], s.i_v.at[b], s.s_i.at[i], s.r_i.at[i], dev)
        copy.start()
        sends.append(copy)

    def halo(g, sem):
        to_up = remote(s.x_v.at[1, g], s.x_v.at[2, g], s.s_h.at[0, sem], s.r_h.at[0, sem], up)
        to_down = remote(s.x_v.at[1, g], s.x_v.at[0, g], s.s_h.at[1, sem], s.r_h.at[1, sem], down)
        return to_up, to_down

    def start_halo(g, sem):
        to_up, to_down = halo(g, sem)
        pl.when(has_up)(lambda: to_up.start())
        pl.when(has_down)(lambda: to_down.start())

    def got_state(g):
        piece = s.x_v.at[1, g]
        remote(piece, piece, s.s_state.at[0], s.r_state.at[g], members[1]).wait_recv()

    @pl.when(home)
    def _():
        pltpu.make_async_copy(state.at[0, pl.ds(0, T)], s.x_v.at[1, c], s.loc.at[4]).wait()

    pl.when(away)(lambda: got_state(c))
    start_halo(c, 0)
    for i in (1, 3, 4, 5, 7, 2, 6):
        g = (c + i) % G
        got_state(g)
        start_halo(g, i)
    weights.relay_z(0)
    for i in (1, 3, 2):
        weights.relay_x(i)
    local[3].wait()
    outs.first()
    for i in range(1, G):
        copy = remote(s.d_v.at[c], s.d_v.at[c], s.s_d.at[i], s.r_d.at[i], (b, (c + i) % G))
        copy.start()
        sends.append(copy)

    def norm(h, at):
        hat, _ = moments(wide(s.x_v, h).astype(F32))
        s.n_v[pl.ds(at * T, T), :] = (hat * gain[...]).astype(BF)

    norm(1, 0)
    weights.relay_y(weights.from_z(0))
    weights.relay_y(weights.from_x(1))
    weights.relay_y(weights.from_x(3))
    for i in range(G):
        to_up, to_down = halo((c + i) % G, i)
        pl.when(has_down)(lambda: to_up.wait_recv())
        pl.when(has_up)(lambda: to_down.wait_recv())
    norm(0, 1)
    norm(2, 2)
    weights.relay_z(1)
    weights.relay_y(weights.from_x(2))
    weights.relay_z(3)

    def attend(i):
        t = (i + 1) % 3
        late = (i >= 2).astype(jnp.int32)
        over = (i >= 5).astype(jnp.int32) + (i == 1).astype(jnp.int32)
        back_by = late * (1 + t * (7 - 3 * t) // 2)
        g = (w + over * (1 - 2 * w)) * 4 + (c % 4 + 4 - back_by) % 4

        def relays(n):
            return pl.when(i == n)

        pl.when(i > 0)(lambda: weights.ready(g))

        @relays(1)
        def _():
            weights.relay_z(2)
            weights.relay_y(weights.from_z(1))

        @relays(2)
        def _():
            weights.relay_y(weights.from_z(3))

        @relays(3)
        def _():
            weights.relay_y(weights.from_z(2))
            outs.relay_z(0)
            for n in (1, 3, 2):
                outs.relay_x(n)

        @relays(5)
        def _():
            for n in (1, 3, 2):
                outs.relay_z(n)
            outs.relay_y(outs.from_z(0))
            for n in (1, 3, 2):
                outs.relay_y(outs.from_x(n))

        @relays(7)
        def _():
            for n in (1, 3, 2):
                outs.relay_y(outs.from_z(n))

        res = nn(s.n_v[...], jnp.concatenate([s.w_v[g, n] for n in range(3)], axis=1))
        for n in range(3):
            s.qkv[n, g] = res[:, n * 128 : (n + 1) * 128].astype(BF)
        vt = jnp.transpose(res[:, 256:]).astype(BF)
        query = s.qkv[0, g, own_rows, :] * eighth
        scores = [nt(s.qkv[1, g], only(query, hh)) for hh in range(2)]
        parts = []
        for hh in range(2):
            n = 2 * g + hh
            sc = scores[hh]
            m0 = jnp.max(sc[:T], axis=0, keepdims=True)
            m1 = jnp.max(sc[T : 2 * T], axis=0, keepdims=True) + up_bias
            m2 = jnp.max(sc[2 * T :], axis=0, keepdims=True) + down_bias
            m = jnp.maximum(jnp.maximum(m0, m1), m2)
            e0 = jnp.exp(sc[:T] - m)
            e1 = jnp.exp(sc[T : 2 * T] - (m - up_bias))
            e2 = jnp.exp(sc[2 * T :] - (m - down_bias))
            l = jnp.sum(e0, axis=0, keepdims=True) + jnp.sum(e1, axis=0, keepdims=True) + jnp.sum(e2, axis=0, keepdims=True)
            inv = 1.0 / l
            s.p_own[n, :T, :] = e0 * inv
            s.p_own[n, T : 2 * T, :] = e1 * inv
            s.p_own[n, 2 * T :, :] = e2 * inv
            p = s.p_own[n].astype(BF)
            parts.append(nn(vt[hh * HD : (hh + 1) * HD], p))
            s.ml[0, n] = m
            s.ml[1, n] = inv
        s.mix[g] = jnp.transpose(jnp.concatenate(parts, axis=0)).astype(BF)

    loop(G, attend)
    start_ml, wait_ml = swap_rows(s.ml, s.mlh.at[0], s.mlh.at[1], s.s_m, s.r_m)
    start_ml()
    for n in range(4):
        if n:
            outs.ready(outs.from_x(n))
        outs.ready(outs.from_z(n))
    for i in range(1, G):
        remote(s.d_v.at[c], s.d_v.at[c], s.s_d.at[i], s.r_d.at[i], members[i]).wait_recv()
    s.acc[...] = jnp.zeros_like(s.acc)

    def out(g):
        s.acc[...] += nn(s.mix[g], s.o_v[g]).astype(BF).astype(F32)

    loop(G, out)
    updated = (wide(s.x_v, 1).astype(F32) + s.acc[...]).astype(BF)
    dec_all = jnp.concatenate([s.d_v[g] for g in range(G)], axis=1)
    s.f_own[...] = nt(dec_all, updated).astype(BF)

    def send_fields(i, act):
        copy = remote(s.f_own, s.fields.at[j_own], s.s_f.at[i], s.r_f.at[j_own], members[i])
        copy.start() if act else copy.wait_send()

    for i in range(1, G):
        send_fields(i, True)
    pl.when(away)(lambda: send_fields(0, True))

    @pl.when(home)
    def _():
        s.fields[j_own] = s.f_own[...]

    for i in range(1, L):
        remote(s.i_own.at[b], s.i_v.at[b], s.s_i.at[i], s.r_i.at[i], lat_peer(i)).wait_recv()
    index = s.i_v[...].reshape(16 * L, 128)
    lanes = lax.broadcasted_iota(jnp.int32, (16 * L, 128), 1) * 16

    total = jnp.zeros((16 * L, 128), F32)
    for j in range(G):
        @pl.when(jnp.logical_not(mine_at[j]))
        def _():
            remote(s.f_own, s.fields.at[j], s.s_f.at[0], s.r_f.at[j], windows[j]).wait_recv()

        for half in range(2):
            hot = (index == lanes + (2 * j + half)).astype(F32).astype(BF)
            total = total + nn(hot[:, :VP], s.fields[j, :, pl.ds(half * 128, 128)])
    s.mine[...] = total.astype(BF).reshape(L, 16, 128)
    for i in range(1, L):
        dev = lat_peer(i)
        copy = remote(s.mine.at[dev[0]], s.picked.at[b], s.s_p.at[i], s.r_p.at[i], dev)
        copy.start()
        sends.append(copy)
    s.picked[b] = s.mine[b]

    wait_ml()

    def near(g):
        s.kt[g] = jnp.transpose(s.qkv[1, g].astype(F32)).astype(BF)
        for side in range(2):
            query = s.qkv[0, g, pl.ds((1 + side) * T, T), :] * eighth
            for hh in range(2):
                n = 2 * g + hh
                sc = nt(s.qkv[1, g, own_rows, :], only(query, hh))
                s.p_nb[side, n] = jnp.exp(sc - s.mlh[side, 0, n]) * s.mlh[side, 1, n]

    loop(4, near)

    fetch.wait()
    row = lax.broadcasted_iota(jnp.int32, (16, 128), 0)

    def observe(i):
        other_b = (b + L - i) % L

        @pl.when(i > 0)
        def _():
            remote(s.mine.at[b], s.picked.at[b], s.s_p.at[i], s.r_p.at[i], (other_b, c)).wait_recv()

        flat = s.itp[other_b].reshape(2048, 128)
        big = nt(s.picked[other_b], flat)
        pred = jnp.zeros((16, 128), F32)
        for n in range(16):
            pred = jnp.where(row == n, big[:, n * 128 : (n + 1) * 128], pred)
        mis = jnp.where(row < count[other_b], pred - obs[other_b].astype(F32), 0.0).astype(BF)
        lhs = jnp.concatenate([jnp.where(row == n, mis, jnp.zeros_like(mis)) for n in range(16)], axis=1)
        s.am[other_b, :16, :] = nn(lhs, flat).astype(BF)
        s.am[other_b, 16:, :] = mis

        @pl.when(i > 0)
        def _():
            remote(s.am.at[other_b], s.came.at[b], s.s_a.at[i], s.r_a.at[i], (other_b, c)).start()

    loop(L, observe)
    s.came[b] = s.am[b]

    loop(4, lambda g: near(g + 4))

    index_t = jnp.transpose(index.astype(F32))[:VP].astype(jnp.int32)
    sub = lax.broadcasted_iota(jnp.int32, (VP, 16 * L), 0) * 16

    def arrived(i):
        other_b = (b + i) % L

        @pl.when(i > 0)
        def _():
            remote(s.am.at[b], s.came.at[b], s.s_a.at[i], s.r_a.at[i], (other_b, c)).wait()

    loop(L, arrived)
    misfit[...] = s.came[:, 16:, :].astype(F32)
    adjoint = s.came[:, :16, :].reshape(16 * L, 128)
    for j in range(G):
        for half in range(2):
            hot = (index_t == sub + (2 * j + half)).astype(F32).astype(BF)
            s.parts[j, :, pl.ds(half * 128, 128)] = nn(hot, adjoint).astype(BF)

        @pl.when(jnp.logical_not(mine_at[j]))
        def _():
            remote(s.parts.at[j], s.got.at[c], s.s_g.at[j], s.r_g.at[c], windows[j]).start()

        @pl.when(mine_at[j])
        def _():
            s.got[c] = s.parts[j]

    def got_part(g):
        remote(s.parts.at[0], s.got.at[g], s.s_g.at[0], s.r_g.at[g], members[1]).wait_recv()

    pl.when(away)(lambda: got_part(c))
    total = s.got[c].astype(F32)
    for i in range(1, G):
        got_part((c + i) % G)
        total = total + s.got[(c + i) % G].astype(F32)
    s.gf[0] = total
    start_gf, wait_gf = swap_rows(s.gf.at[0], s.gf.at[1], s.gf.at[2], s.s_gh, s.r_gh)
    start_gf()

    dec_all = jnp.concatenate([dec_all, jnp.zeros((128 - VP, D), BF)], axis=0)
    dec3 = jnp.concatenate([dec_all, dec_all, dec_all], axis=0)

    def update_of(h):
        field = jnp.transpose(jnp.concatenate([s.gf[h], jnp.zeros((128 - VP, T), F32)], axis=0))
        hi = field.astype(BF)
        rest = field - hi.astype(F32)
        mid = rest.astype(BF)
        lo = (rest - mid.astype(F32)).astype(BF)
        update = nn(jnp.concatenate([hi, mid, lo], axis=1), dec3)
        s.n_v[pl.ds(h * T, T), :] = update.astype(BF)
        return update

    def mixed(rows, n):
        def step(m):
            weight = jnp.concatenate([s.o_v[2 * m], s.o_v[2 * m + 1]], axis=0)
            res = nt(s.n_v[pl.ds(rows, n), :], weight).astype(BF)
            s.do[2 * m, pl.ds(rows, n), :] = res[:, :128]
            s.do[2 * m + 1, pl.ds(rows, n), :] = res[:, 128:]

        return step

    def own(g):
        parts = []
        for hh in range(2):
            n = 2 * g + hh
            dp = nt(s.qkv[2, g], only(s.do[g, own_rows, :], hh))
            p = s.p_own[n]
            along = jnp.sum(p * dp, axis=0, keepdims=True)
            s.delta[n] = along
            ds = (p * (dp - along)).astype(BF)
            parts.append(nn(s.kt[g, pl.ds(hh * HD, HD), :], ds) * 0.125)
            s.dso[g, :, pl.ds(hh * T, T)] = ds[:T]
        s.dq[g] = jnp.transpose(jnp.concatenate(parts, axis=0)).astype(BF)

    def other(g):
        scores, probs, queries, grads = [s.dso[g]], [], [], []
        for hh in range(2):
            probs.append(s.p_own[2 * g + hh, :T, :].astype(BF))
            queries.append(only(s.qkv[0, g, own_rows, :] * eighth, hh))
            grads.append(only(s.do[g, own_rows, :], hh))
        for side in range(2):
            rows = pl.ds((1 + side) * T, T)
            for hh in range(2):
                n = 2 * g + hh
                queries.append(only(s.qkv[0, g, rows, :] * eighth, hh))
                grads.append(only(s.do[g, rows, :], hh))
                dp = nt(s.qkv[2, g, own_rows, :], grads[-1])
                p = s.p_nb[side, n]
                scores.append((p * (dp - s.delta_h[side, n])).astype(BF))
                probs.append(p.astype(BF))
        dk = nn(jnp.concatenate(scores, axis=1), jnp.concatenate(queries, axis=0))
        dv = nn(jnp.concatenate(probs, axis=1), jnp.concatenate(grads, axis=0))
        three = jnp.concatenate([s.dq[g], dk.astype(BF), dv.astype(BF)], axis=1)
        wide_w = jnp.concatenate([s.w_v[g, 0], s.w_v[g, 1], s.w_v[g, 2]], axis=1)
        s.acc[...] += nt(three, wide_w).astype(BF).astype(F32)

    s.gu[...] = update_of(0)
    loop(G // 2, mixed(0, T))
    swaps = []
    for n in range(2):
        loop(4, lambda g: own(g + 4 * n))
        heads = pl.ds(8 * n, 8)
        start, wait = swap_rows(
            s.delta.at[heads], s.delta_h.at[0, heads], s.delta_h.at[1, heads], s.s_dl.at[n], s.r_dl.at[n]
        )
        start()
        swaps.append(wait)
    wait_gf()
    update_of(1)
    update_of(2)
    loop(G // 2, mixed(T, 2 * T))
    s.acc[...] = jnp.zeros_like(s.acc)
    for n in range(2):
        swaps[n]()
        loop(4, lambda g: other(g + 4 * n))

    hat, inv = moments(wide(s.x_v, 1).astype(F32))
    grad_hat = s.acc[...] * gain[...]
    mean = jnp.sum(grad_hat, axis=-1, keepdims=True) * (1.0 / D)
    cross = jnp.sum(grad_hat * hat, axis=-1, keepdims=True) * (1.0 / D)
    total = (s.gu[...] + (grad_hat - mean - hat * cross) * inv).astype(BF)
    for g in range(G):
        s.mix[g] = total[:, g * 128 : (g + 1) * 128]
    def send_back(i, act):
        dev = members[i]
        copy = remote(s.mix.at[dev[1]], back.at[r, pl.ds(w * T, T)], s.s_y.at[i], s.r_y.at[j_own], dev)
        copy.start() if act else copy.wait_send()

    for i in range(1, G):
        send_back(i, True)
    pl.when(away)(lambda: send_back(0, True))

    @pl.when(home)
    def _():
        back[r, pl.ds(w * T, T), :] = s.mix[c]

    weights.finish()
    outs.finish()
    for copy in sends:
        copy.wait_send()
    for i in range(G):
        to_up, to_down = halo((c + i) % G, i)
        pl.when(has_up)(lambda: to_up.wait_send())
        pl.when(has_down)(lambda: to_down.wait_send())
    for i in range(1, G):
        send_fields(i, False)
        send_back(i, False)

    @pl.when(away)
    def _():
        send_fields(0, False)
        send_back(0, False)

    for j in range(G):
        send_state(j, False)

        @pl.when(jnp.logical_not(mine_at[j]))
        def _():
            remote(s.parts.at[j], s.got.at[c], s.s_g.at[j], s.r_g.at[c], windows[j]).wait_send()
            piece = back.at[j // 2, pl.ds((j % 2) * T, T)]
            remote(s.mix.at[0], piece, s.s_y.at[0], s.r_y.at[j], windows[j]).wait_recv()


def body(state, background, gain, w_query, w_key, w_value, w_out, decoder, interp, obs_values, tile_index, block_count):
    smem = pl.BlockSpec(memory_space=pltpu.SMEM)
    misfit, back = call(
        kernel,
        (sds((L, 16, 128), F32), sds((4, 512, 128), BF)),
        [ANY] * 5 + [VM, VM, VM, ANY, VM, smem],
        [VM] * 2,
        list(SCRATCH.values()),
        0,
        "whole",
        (
            state, w_query, w_key, w_value, w_out, decoder, tile_index.reshape(L, 16), gain.reshape(1, D),
            interp.reshape(L, 16, 128, 128), obs_values.reshape(L, 16, 128), block_count.reshape(L),
        ),
    )
    gradient = state.astype(F32) - background.astype(F32) + back.astype(F32)
    return misfit.reshape(L, 1, 1, 16, 128), gradient


def solution(mesh):
    return jax.shard_map(
        body,
        mesh=mesh,
        in_specs=(
            P("lat", None, "chan"),
            P("lat", None, "chan"),
            P(),
            P(None, "chan"),
            P(None, "chan"),
            P(None, "chan"),
            P("chan", None),
            P("chan", None),
            P("lat", "chan", None, None, None, None),
            P("lat", "chan", None, None, None),
            P("lat", "chan", None, None),
            P("lat", "chan", None),
        ),
        out_specs=(P(None, "chan", "lat", None, None), P("lat", None, "chan")),
        check_vma=False,
    )
```

```python
import functools

import jax
import jax.numpy as jnp
from jax import lax
from jax.experimental import pallas as pl
from jax.experimental.pallas import tpu as pltpu
from jax.sharding import PartitionSpec as P

D = 1024
HD = 64
VARS = 69
EPSILON = 1e-05
VP = 80
T = 256
G = 8
L = 16
BIG = 1e30
MESH = pl.DeviceIdType.MESH
BF = jnp.bfloat16
F32 = jnp.float32
VMEM_LIMIT = 62 * 1024 * 1024


def nn(a, b):
    return lax.dot_general(a, b, (((1,), (0,)), ((), ())), preferred_element_type=F32)


def nt(a, b):
    return lax.dot_general(a, b, (((1,), (1,)), ((), ())), preferred_element_type=F32)


def place():
    b = lax.axis_index("lat")
    c = lax.axis_index("chan")
    k = b % 2
    big = b // 2
    q = 2 * (c % 4) + k
    row = q + (big % 2) * (7 - 2 * q)
    return b, c, k, big, row, c // 4


def holder(big, row, w):
    q = row + (big % 2) * (7 - 2 * row)
    return big * 2 + q % 2, w * 4 + q // 2


def neighbours():
    b, c, k, big, row, w = place()
    q = 2 * (c % 4) + k
    step = 1 - 2 * (big % 2)
    inner_up = (row > 0).astype(jnp.int32)
    inner_down = (row < 7).astype(jnp.int32)
    q_up, q_down = q - step * inner_up, q + step * inner_down
    up = ((big - 1 + inner_up) * 2 + q_up % 2, w * 4 + q_up // 2)
    down = ((big + 1 - inner_down) * 2 + q_down % 2, w * 4 + q_down // 2)
    return up, down, big * 8 + row > 0, big * 8 + row < 4 * L - 1


def lat_peer(i):
    b, c = lax.axis_index("lat"), lax.axis_index("chan")
    return ((b + i) % L, c)


def far_flip():
    b, c = lax.axis_index("lat"), lax.axis_index("chan")
    return (b + 2 - 4 * ((b // 2) % 2), (c + 4) % G)


def greeted():
    b, c, k, big, _, _ = place()
    barrier = pltpu.get_barrier_semaphore()
    peers = [(b, (c + i) % G) for i in range(1, G)]
    peers += [(b + 1 - 2 * k, (c + i) % G) for i in range(G)]
    peers += [(2 * ((big + i) % 8) + j, c) for i in range(1, 8) for j in range(2)]
    peers.append(far_flip())
    for dev in peers:
        pl.semaphore_signal(barrier, inc=1, device_id=dev, device_id_type=MESH)
    return lambda: pl.semaphore_wait(barrier, len(peers))


def remote(src, dst, ss, rs, dev):
    return pltpu.make_async_remote_copy(
        src_ref=src, dst_ref=dst, send_sem=ss, recv_sem=rs, device_id=dev, device_id_type=MESH
    )


def call(kernel, out_shape, in_specs, out_specs, scratch, cid, name, args):
    return pl.pallas_call(
        kernel,
        out_shape=out_shape,
        in_specs=in_specs,
        out_specs=out_specs,
        scratch_shapes=scratch,
        compiler_params=pltpu.CompilerParams(
            collective_id=cid, has_side_effects=cid is not None, vmem_limit_bytes=VMEM_LIMIT
        ),
        name=name,
    )(*args)


VM = pl.BlockSpec(memory_space=pltpu.VMEM)
ANY = pl.BlockSpec(memory_space=pl.ANY)
DMA = pltpu.SemaphoreType.DMA


def sds(shape, dtype):
    return jax.ShapeDtypeStruct(shape, dtype)


class Spread:
    def __init__(self, view, size, sems):
        self.view, self.half = view, size // 2
        self.s1, self.r1, self.s2, self.r2, self.s3, self.r3, self.s4, self.r4, self.s5, self.r5 = sems
        b, c, k, _, _, z = place()
        x, y = c % 4, b // 4
        p = y % 2
        self.b, self.c, self.x, self.z = b, c, x, z
        self.start = (p * 2 + k) * size
        self.across = ((1 - p) * 2 + k) * size
        self.turn = (1 - 2 * k) * size
        self.core = (b + 1 - 2 * k, c)
        self.ups = [((b + 4) % L, c), ((b + 12) % L, c)]
        self.flips = [(b, (c + 4) % G), far_flip()]

    def send(self, g, start, size, ss, rs, dev):
        ref = self.view(g, start, size)
        copy = remote(ref, ref, ss, rs, dev)
        copy.start()

    def wait(self, g, start, size, rs):
        ref = self.view(g, start, size)
        remote(ref, ref, self.s1.at[0], rs, self.core).wait_recv()

    def from_x(self, i):
        return self.z * 4 + (self.x + 4 - i) % 4

    def from_z(self, i):
        return (1 - self.z) * 4 + (self.x + 4 - i) % 4

    def along_z(self, g):
        for h in range(2):
            at = self.start + h * self.half
            self.send(g, at, self.half, self.s2.at[h, g], self.r2.at[h, g], self.flips[h])

    def first(self):
        for i in (1, 3, 2):
            dev = (self.b, self.z * 4 + (self.x + i) % 4)
            self.send(self.c, self.start, 2 * self.half, self.s1.at[i], self.r1.at[self.c], dev)
        self.along_z(self.c)

    def fan(self, g, h):
        at = self.start + h * self.half
        self.send(g, at, self.half, self.s4.at[h, g], self.r4.at[h, g], self.ups[h])
        self.send(g, at, self.half, self.s3.at[h, g], self.r3.at[h, g], self.core)

    def relay_x(self, i):
        g = self.from_x(i)
        self.wait(g, self.start, 2 * self.half, self.r1.at[g])
        self.along_z(g)
        self.fan(g, 0)
        self.fan(g, 1)

    def relay_z(self, i):
        g = self.from_z(i)
        for h in range(2):
            self.wait(g, self.start + h * self.half, self.half, self.r2.at[h, g])
            self.fan(g, h)

    def relay_y(self, g):
        for h in range(2):
            at = self.across + h * self.half
            self.wait(g, at, self.half, self.r4.at[h, g])
            self.send(g, at, self.half, self.s5.at[h, g], self.r5.at[h, g], self.core)

    def ready(self, g):
        for h in range(2):
            self.wait(g, self.start + self.turn + h * self.half, self.half, self.r3.at[h, g])
            self.wait(g, self.across + self.turn + h * self.half, self.half, self.r5.at[h, g])

    def finish(self):
        def sent(g, start, size, sem):
            ref = self.view(g, start, size)
            remote(ref, ref, sem, self.r1.at[0], self.core).wait_send()

        half = self.half
        for i in (1, 3, 2):
            sent(self.c, self.start, 2 * half, self.s1.at[i])
        for i in range(4):
            row = self.from_x(i)
            for h in range(2):
                at = self.start + h * half
                sent(row, at, half, self.s2.at[h, row])
                for g in ([row] if i else []) + [self.from_z(i)]:
                    sent(g, at, half, self.s3.at[h, g])
                    sent(g, at, half, self.s4.at[h, g])
                    sent(g, self.across + h * half, half, self.s5.at[h, g])


def wide(ref, h):
    return jnp.concatenate([ref[h, g] for g in range(G)], axis=1)


def moments(x):
    mean = jnp.sum(x, axis=-1, keepdims=True) * (1.0 / D)
    centred = x - mean
    var = jnp.sum(centred * centred, axis=-1, keepdims=True) * (1.0 / D)
    inv = lax.rsqrt(var + EPSILON)
    return centred * inv, inv


def only(value, hh):
    first = lax.broadcasted_iota(jnp.int32, value.shape, 1) < HD
    keep = first if hh == 0 else jnp.logical_not(first)
    return jnp.where(keep, value, jnp.zeros_like(value))


def swap_rows(src, above, below, ss, rs):
    up, down, has_up, has_down = neighbours()
    to_up = remote(src, below, ss.at[0], rs.at[0], up)
    to_down = remote(src, above, ss.at[1], rs.at[1], down)

    def start():
        pl.when(has_up)(lambda: to_up.start())
        pl.when(has_down)(lambda: to_down.start())

    def wait():
        @pl.when(has_up)
        def _():
            to_up.wait_send()
            to_down.wait_recv()

        @pl.when(has_down)
        def _():
            to_down.wait_send()
            to_up.wait_recv()

    return start, wait


def loop(n, step):
    def wrapped(i, carry):
        step(i)
        return carry

    lax.fori_loop(0, n, wrapped, 0)


SCRATCH = dict(
    x_v=pltpu.VMEM((3, G, T, 128), BF),
    w_v=pltpu.VMEM((G, 3, D, 128), BF),
    o_v=pltpu.VMEM((G, 128, D), BF),
    d_v=pltpu.VMEM((G, VP, 128), BF),
    i_v=pltpu.VMEM((L, 16, 128), jnp.int32),
    itp=pltpu.VMEM((L, 16, 128, 128), BF),
    n_v=pltpu.VMEM((3 * T, D), BF),
    qkv=pltpu.VMEM((3, G, 3 * T, 128), BF),
    kt=pltpu.VMEM((G, 128, 3 * T), BF),
    mix=pltpu.VMEM((G, T, 128), BF),
    acc=pltpu.VMEM((T, D), F32),
    ml=pltpu.VMEM((2, 16, 1, T), F32),
    mlh=pltpu.VMEM((2, 2, 16, 1, T), F32),
    fields=pltpu.VMEM((G, VP, T), BF),
    mine=pltpu.VMEM((L, 16, 128), BF),
    picked=pltpu.VMEM((L, 16, 128), BF),
    am=pltpu.VMEM((L, 32, 128), BF),
    came=pltpu.VMEM((L, 32, 128), BF),
    parts=pltpu.VMEM((G, VP, T), BF),
    got=pltpu.VMEM((G, VP, T), BF),
    gf=pltpu.VMEM((3, VP, T), F32),
    gu=pltpu.VMEM((T, D), F32),
    do=pltpu.VMEM((G, 3 * T, 128), BF),
    dq=pltpu.VMEM((G, T, 128), BF),
    dso=pltpu.VMEM((G, T, 2 * T), BF),
    dp=pltpu.VMEM((2, 3 * T, T), F32),
    ds=pltpu.VMEM((2, 3 * T, T), BF),
    p_own=pltpu.VMEM((16, 3 * T, T), F32),
    p_nb=pltpu.VMEM((2, 16, T, T), F32),
    delta=pltpu.VMEM((16, 1, T), F32),
    delta_h=pltpu.VMEM((2, 16, 1, T), F32),
    f_own=pltpu.VMEM((VP, T), BF),
    i_own=pltpu.VMEM((L, 16, 128), jnp.int32),
    loc=DMA((8,)),
    s_state=DMA((G,)), r_state=DMA((G,)),
    s_d=DMA((G,)), r_d=DMA((G,)),
    s_i=DMA((L,)), r_i=DMA((L,)),
    s_h=DMA((2, G)), r_h=DMA((2, G)),
    s_f=DMA((G,)), r_f=DMA((G,)),
    s_p=DMA((L,)), r_p=DMA((L,)),
    s_a=DMA((L,)), r_a=DMA((L,)),
    s_g=DMA((G,)), r_g=DMA((G,)),
    s_y=DMA((G,)), r_y=DMA((G,)),
    s_m=DMA((2,)), r_m=DMA((2,)),
    s_gh=DMA((2,)), r_gh=DMA((2,)),
    s_dl=DMA((2, 2)), r_dl=DMA((2, 2)),
    w1=DMA((4,)), w2=DMA((G,)), w3=DMA((2, G)), w4=DMA((2, G)), w5=DMA((2, G)), w6=DMA((2, G)), w7=DMA((2, G)), w8=DMA((2, G)), w9=DMA((2, G)), w10=DMA((2, G)),
    o1=DMA((4,)), o2=DMA((G,)), o3=DMA((2, G)), o4=DMA((2, G)), o5=DMA((2, G)), o6=DMA((2, G)), o7=DMA((2, G)), o8=DMA((2, G)), o9=DMA((2, G)), o10=DMA((2, G)),
)


class Refs:
    pass


def kernel(state, wq, wk, wv, wo, dec, idx, gain, interp, obs, count, misfit, back, *scratch):
    s = Refs()
    for name, ref in zip(SCRATCH, scratch):
        setattr(s, name, ref)
    b, c, k, big, row8, w = place()
    r = row8 % 4
    band = 2 * big + row8 // 4
    j_own = r * 2 + w
    home = band == b
    up, down, has_up, has_down = neighbours()
    up_bias = jnp.where(has_up, 0.0, -BIG).astype(F32)
    down_bias = jnp.where(has_down, 0.0, -BIG).astype(F32)
    own_rows = pl.ds(0, T)
    eighth = jnp.asarray(0.125, BF)
    away = jnp.logical_not(home)
    windows = [holder(big, 4 * k + j // 2, j % 2) for j in range(G)]
    mine_at = [jnp.logical_and(home, j_own == j) for j in range(G)]
    members = [(band, (c + i) % G) for i in range(G)]

    met = greeted()
    local = [
        pltpu.make_async_copy(wq, s.w_v.at[c, 0], s.loc.at[0]),
        pltpu.make_async_copy(wk, s.w_v.at[c, 1], s.loc.at[1]),
        pltpu.make_async_copy(wv, s.w_v.at[c, 2], s.loc.at[2]),
        pltpu.make_async_copy(wo, s.o_v.at[c], s.loc.at[3]),
    ]
    for copy in local:
        copy.start()

    @pl.when(jnp.logical_not(has_up))
    def _():
        s.x_v[0] = jnp.zeros((G, T, 128), BF)

    @pl.when(jnp.logical_not(has_down))
    def _():
        s.x_v[2] = jnp.zeros((G, T, 128), BF)

    s.mlh[:, 0] = jnp.full((2, 16, 1, T), BIG, F32)
    s.mlh[:, 1] = jnp.zeros((2, 16, 1, T), F32)
    s.delta_h[...] = jnp.zeros_like(s.delta_h)
    s.gf[...] = jnp.zeros_like(s.gf)
    eye = lax.broadcasted_iota(jnp.int32, (VP, VARS), 0) == lax.broadcasted_iota(jnp.int32, (VP, VARS), 1)
    s.d_v[c] = nn(eye.astype(F32).astype(BF), dec[...]).astype(BF)
    for n in range(16):
        s.i_own[:, n, :] = jnp.broadcast_to(idx[:, n : n + 1], (L, 128))
    s.i_v[b] = s.i_own[b]
    met()

    sends = []

    def send_state(j, act):
        src = state.at[j // 2, pl.ds((j % 2) * T, T)]

        @pl.when(jnp.logical_not(mine_at[j]))
        def _():
            copy = remote(src, s.x_v.at[1, c], s.s_state.at[j], s.r_state.at[c], windows[j])
            copy.start() if act else copy.wait_send()

        if act:
            @pl.when(mine_at[j])
            def _():
                pltpu.make_async_copy(src, s.x_v.at[1, c], s.loc.at[4]).start()

    for j in range(G):
        send_state(j, True)
    weights = Spread(
        lambda g, at, n: s.w_v.at[g, :, pl.ds(at, n)], 256, (s.w1, s.w2, s.w3, s.w4, s.w5, s.w6, s.w7, s.w8, s.w9, s.w10)
    )
    outs = Spread(
        lambda g, at, n: s.o_v.at[g, pl.ds(at, n)], 32, (s.o1, s.o2, s.o3, s.o4, s.o5, s.o6, s.o7, s.o8, s.o9, s.o10)
    )
    for copy in local[:3]:
        copy.wait()
    weights.first()
    fetch = pltpu.make_async_copy(interp, s.itp, s.loc.at[5])
    fetch.start()
    for i in range(1, L):
        dev = lat_peer(i)
        copy = remote(s.i_own.at[dev[0]], s.i_v.at[b], s.s_i.at[i], s.r_i.at[i], dev)
        copy.start()
        sends.append(copy)

    def halo(g, sem):
        to_up = remote(s.x_v.at[1, g], s.x_v.at[2, g], s.s_h.at[0, sem], s.r_h.at[0, sem], up)
        to_down = remote(s.x_v.at[1, g], s.x_v.at[0, g], s.s_h.at[1, sem], s.r_h.at[1, sem], down)
        return to_up, to_down

    def start_halo(g, sem):
        to_up, to_down = halo(g, sem)
        pl.when(has_up)(lambda: to_up.start())
        pl.when(has_down)(lambda: to_down.start())

    def got_state(g):
        piece = s.x_v.at[1, g]
        remote(piece, piece, s.s_state.at[0], s.r_state.at[g], members[1]).wait_recv()

    @pl.when(home)
    def _():
        pltpu.make_async_copy(state.at[0, pl.ds(0, T)], s.x_v.at[1, c], s.loc.at[4]).wait()

    pl.when(away)(lambda: got_state(c))
    start_halo(c, 0)
    for i in (1, 3, 4, 5, 7, 2, 6):
        g = (c + i) % G
        got_state(g)
        start_halo(g, i)
    weights.relay_z(0)
    for i in (1, 3, 2):
        weights.relay_x(i)
    local[3].wait()
    outs.first()
    for i in range(1, G):
        copy = remote(s.d_v.at[c], s.d_v.at[c], s.s_d.at[i], s.r_d.at[i], (b, (c + i) % G))
        copy.start()
        sends.append(copy)

    def norm(h, at):
        hat, _ = moments(wide(s.x_v, h).astype(F32))
        s.n_v[pl.ds(at * T, T), :] = (hat * gain[...]).astype(BF)

    norm(1, 0)
    weights.relay_y(weights.from_z(0))
    weights.relay_y(weights.from_x(1))
    weights.relay_y(weights.from_x(3))
    for i in range(G):
        to_up, to_down = halo((c + i) % G, i)
        pl.when(has_down)(lambda: to_up.wait_recv())
        pl.when(has_up)(lambda: to_down.wait_recv())
    norm(0, 1)
    norm(2, 2)
    weights.relay_z(1)
    weights.relay_y(weights.from_x(2))
    weights.relay_z(3)

    def attend(i):
        t = (i + 1) % 3
        late = (i >= 2).astype(jnp.int32)
        over = (i >= 5).astype(jnp.int32) + (i == 1).astype(jnp.int32)
        back_by = late * (1 + t * (7 - 3 * t) // 2)
        g = (w + over * (1 - 2 * w)) * 4 + (c % 4 + 4 - back_by) % 4

        def relays(n):
            return pl.when(i == n)

        pl.when(i > 0)(lambda: weights.ready(g))

        @relays(1)
        def _():
            weights.relay_z(2)
            weights.relay_y(weights.from_z(1))

        @relays(2)
        def _():
            weights.relay_y(weights.from_z(3))

        @relays(3)
        def _():
            weights.relay_y(weights.from_z(2))
            outs.relay_z(0)
            for n in (1, 3, 2):
                outs.relay_x(n)

        @relays(5)
        def _():
            for n in (1, 3, 2):
                outs.relay_z(n)
            outs.relay_y(outs.from_z(0))
            for n in (1, 3, 2):
                outs.relay_y(outs.from_x(n))

        @relays(7)
        def _():
            for n in (1, 3, 2):
                outs.relay_y(outs.from_z(n))

        res = nn(s.n_v[...], jnp.concatenate([s.w_v[g, n] for n in range(3)], axis=1))
        for n in range(3):
            s.qkv[n, g] = res[:, n * 128 : (n + 1) * 128].astype(BF)
        vt = jnp.transpose(res[:, 256:]).astype(BF)
        query = s.qkv[0, g, own_rows, :] * eighth
        scores = [nt(s.qkv[1, g], only(query, hh)) for hh in range(2)]
        parts = []
        for hh in range(2):
            n = 2 * g + hh
            sc = scores[hh]
            m0 = jnp.max(sc[:T], axis=0, keepdims=True)
            m1 = jnp.max(sc[T : 2 * T], axis=0, keepdims=True) + up_bias
            m2 = jnp.max(sc[2 * T :], axis=0, keepdims=True) + down_bias
            m = jnp.maximum(jnp.maximum(m0, m1), m2)
            e0 = jnp.exp(sc[:T] - m)
            e1 = jnp.exp(sc[T : 2 * T] - (m - up_bias))
            e2 = jnp.exp(sc[2 * T :] - (m - down_bias))
            l = jnp.sum(e0, axis=0, keepdims=True) + jnp.sum(e1, axis=0, keepdims=True) + jnp.sum(e2, axis=0, keepdims=True)
            inv = 1.0 / l
            s.p_own[n, :T, :] = e0 * inv
            s.p_own[n, T : 2 * T, :] = e1 * inv
            s.p_own[n, 2 * T :, :] = e2 * inv
            p = s.p_own[n].astype(BF)
            parts.append(nn(vt[hh * HD : (hh + 1) * HD], p))
            s.ml[0, n] = m
            s.ml[1, n] = inv
        s.mix[g] = jnp.transpose(jnp.concatenate(parts, axis=0)).astype(BF)

    loop(G, attend)
    start_ml, wait_ml = swap_rows(s.ml, s.mlh.at[0], s.mlh.at[1], s.s_m, s.r_m)
    start_ml()
    for n in range(4):
        if n:
            outs.ready(outs.from_x(n))
        outs.ready(outs.from_z(n))
    for i in range(1, G):
        remote(s.d_v.at[c], s.d_v.at[c], s.s_d.at[i], s.r_d.at[i], members[i]).wait_recv()
    s.acc[...] = jnp.zeros_like(s.acc)

    def out(g):
        s.acc[...] += nn(s.mix[g], s.o_v[g]).astype(BF).astype(F32)

    loop(G, out)
    updated = (wide(s.x_v, 1).astype(F32) + s.acc[...]).astype(BF)
    dec_all = jnp.concatenate([s.d_v[g] for g in range(G)], axis=1)
    s.f_own[...] = nt(dec_all, updated).astype(BF)

    def send_fields(i, act):
        copy = remote(s.f_own, s.fields.at[j_own], s.s_f.at[i], s.r_f.at[j_own], members[i])
        copy.start() if act else copy.wait_send()

    for i in range(1, G):
        send_fields(i, True)
    pl.when(away)(lambda: send_fields(0, True))

    @pl.when(home)
    def _():
        s.fields[j_own] = s.f_own[...]

    for i in range(1, L):
        remote(s.i_own.at[b], s.i_v.at[b], s.s_i.at[i], s.r_i.at[i], lat_peer(i)).wait_recv()
    index = s.i_v[...].reshape(16 * L, 128)
    lanes = lax.broadcasted_iota(jnp.int32, (16 * L, 128), 1) * 16

    total = jnp.zeros((16 * L, 128), F32)
    for j in range(G):
        @pl.when(jnp.logical_not(mine_at[j]))
        def _():
            remote(s.f_own, s.fields.at[j], s.s_f.at[0], s.r_f.at[j], windows[j]).wait_recv()

        for half in range(2):
            hot = (index == lanes + (2 * j + half)).astype(F32).astype(BF)
            total = total + nn(hot[:, :VP], s.fields[j, :, pl.ds(half * 128, 128)])
    s.mine[...] = total.astype(BF).reshape(L, 16, 128)
    for i in range(1, L):
        dev = lat_peer(i)
        copy = remote(s.mine.at[dev[0]], s.picked.at[b], s.s_p.at[i], s.r_p.at[i], dev)
        copy.start()
        sends.append(copy)
    s.picked[b] = s.mine[b]

    wait_ml()

    def near(g):
        s.kt[g] = jnp.transpose(s.qkv[1, g].astype(F32)).astype(BF)
        for side in range(2):
            query = s.qkv[0, g, pl.ds((1 + side) * T, T), :] * eighth
            for hh in range(2):
                n = 2 * g + hh
                sc = nt(s.qkv[1, g, own_rows, :], only(query, hh))
                s.p_nb[side, n] = jnp.exp(sc - s.mlh[side, 0, n]) * s.mlh[side, 1, n]

    loop(4, near)

    fetch.wait()
    row = lax.broadcasted_iota(jnp.int32, (16, 128), 0)

    def observe(i):
        other_b = (b + L - i) % L

        @pl.when(i > 0)
        def _():
            remote(s.mine.at[b], s.picked.at[b], s.s_p.at[i], s.r_p.at[i], (other_b, c)).wait_recv()

        flat = s.itp[other_b].reshape(2048, 128)
        big = nt(s.picked[other_b], flat)
        pred = jnp.zeros((16, 128), F32)
        for n in range(16):
            pred = jnp.where(row == n, big[:, n * 128 : (n + 1) * 128], pred)
        mis = jnp.where(row < count[other_b], pred - obs[other_b].astype(F32), 0.0).astype(BF)
        lhs = jnp.concatenate([jnp.where(row == n, mis, jnp.zeros_like(mis)) for n in range(16)], axis=1)
        s.am[other_b, :16, :] = nn(lhs, flat).astype(BF)
        s.am[other_b, 16:, :] = mis

        @pl.when(i > 0)
        def _():
            remote(s.am.at[other_b], s.came.at[b], s.s_a.at[i], s.r_a.at[i], (other_b, c)).start()

    loop(L, observe)
    s.came[b] = s.am[b]

    loop(4, lambda g: near(g + 4))

    index_t = jnp.transpose(index.astype(F32))[:VP].astype(jnp.int32)
    sub = lax.broadcasted_iota(jnp.int32, (VP, 16 * L), 0) * 16

    def arrived(i):
        other_b = (b + i) % L

        @pl.when(i > 0)
        def _():
            remote(s.am.at[b], s.came.at[b], s.s_a.at[i], s.r_a.at[i], (other_b, c)).wait()

    loop(L, arrived)
    misfit[...] = s.came[:, 16:, :]
    adjoint = s.came[:, :16, :].reshape(16 * L, 128)
    for j in range(G):
        for half in range(2):
            hot = (index_t == sub + (2 * j + half)).astype(F32).astype(BF)
            s.parts[j, :, pl.ds(half * 128, 128)] = nn(hot, adjoint).astype(BF)

        @pl.when(jnp.logical_not(mine_at[j]))
        def _():
            remote(s.parts.at[j], s.got.at[c], s.s_g.at[j], s.r_g.at[c], windows[j]).start()

        @pl.when(mine_at[j])
        def _():
            s.got[c] = s.parts[j]

    def got_part(g):
        remote(s.parts.at[0], s.got.at[g], s.s_g.at[0], s.r_g.at[g], members[1]).wait_recv()

    pl.when(away)(lambda: got_part(c))
    total = s.got[c].astype(F32)
    for i in range(1, G):
        got_part((c + i) % G)
        total = total + s.got[(c + i) % G].astype(F32)
    s.gf[0] = total
    start_gf, wait_gf = swap_rows(s.gf.at[0], s.gf.at[1], s.gf.at[2], s.s_gh, s.r_gh)
    start_gf()

    dec_all = jnp.concatenate([dec_all, jnp.zeros((128 - VP, D), BF)], axis=0)
    dec3 = jnp.concatenate([dec_all, dec_all, dec_all], axis=0)

    def update_of(h):
        field = jnp.transpose(jnp.concatenate([s.gf[h], jnp.zeros((128 - VP, T), F32)], axis=0))
        hi = field.astype(BF)
        rest = field - hi.astype(F32)
        mid = rest.astype(BF)
        lo = (rest - mid.astype(F32)).astype(BF)
        update = nn(jnp.concatenate([hi, mid, lo], axis=1), dec3)
        s.n_v[pl.ds(h * T, T), :] = update.astype(BF)
        return update

    def mixed(rows, n):
        def step(m):
            weight = jnp.concatenate([s.o_v[2 * m], s.o_v[2 * m + 1]], axis=0)
            res = nt(s.n_v[pl.ds(rows, n), :], weight).astype(BF)
            s.do[2 * m, pl.ds(rows, n), :] = res[:, :128]
            s.do[2 * m + 1, pl.ds(rows, n), :] = res[:, 128:]

        return step

    def own(g):
        for hh in range(2):
            s.dp[hh] = nt(s.qkv[2, g], only(s.do[g, own_rows, :], hh))
        parts = []
        for hh in range(2):
            n = 2 * g + hh
            along = jnp.zeros((8, T), F32)
            for at in range(0, 3 * T, 64):
                product = s.p_own[n, at : at + 64, :] * s.dp[hh, at : at + 64, :]
                along = along + jnp.sum(product.reshape(8, 8, T), axis=0)
            along = jnp.sum(along, axis=0, keepdims=True)
            s.delta[n] = along
            for at in range(0, 3 * T, 64):
                spread = s.p_own[n, at : at + 64, :] * (s.dp[hh, at : at + 64, :] - along)
                s.ds[hh, at : at + 64, :] = spread.astype(BF)
            parts.append(nn(s.kt[g, pl.ds(hh * HD, HD), :], s.ds[hh]) * 0.125)
            s.dso[g, :, pl.ds(hh * T, T)] = s.ds[hh, :T, :]
        s.dq[g] = jnp.transpose(jnp.concatenate(parts, axis=0)).astype(BF)

    def other(g):
        scores, probs, queries, grads = [s.dso[g]], [], [], []
        for hh in range(2):
            probs.append(s.p_own[2 * g + hh, :T, :].astype(BF))
            queries.append(only(s.qkv[0, g, own_rows, :] * eighth, hh))
            grads.append(only(s.do[g, own_rows, :], hh))
        for side in range(2):
            rows = pl.ds((1 + side) * T, T)
            for hh in range(2):
                n = 2 * g + hh
                queries.append(only(s.qkv[0, g, rows, :] * eighth, hh))
                grads.append(only(s.do[g, rows, :], hh))
                dp = nt(s.qkv[2, g, own_rows, :], grads[-1])
                p = s.p_nb[side, n]
                scores.append((p * (dp - s.delta_h[side, n])).astype(BF))
                probs.append(p.astype(BF))
        dk = nn(jnp.concatenate(scores, axis=1), jnp.concatenate(queries, axis=0))
        dv = nn(jnp.concatenate(probs, axis=1), jnp.concatenate(grads, axis=0))
        three = jnp.concatenate([s.dq[g], dk.astype(BF), dv.astype(BF)], axis=1)
        wide_w = jnp.concatenate([s.w_v[g, 0], s.w_v[g, 1], s.w_v[g, 2]], axis=1)
        s.acc[...] += nt(three, wide_w).astype(BF).astype(F32)

    s.gu[...] = update_of(0)
    loop(G // 2, mixed(0, T))
    swaps = []
    for n in range(2):
        loop(4, lambda g: own(g + 4 * n))
        heads = pl.ds(8 * n, 8)
        start, wait = swap_rows(
            s.delta.at[heads], s.delta_h.at[0, heads], s.delta_h.at[1, heads], s.s_dl.at[n], s.r_dl.at[n]
        )
        start()
        swaps.append(wait)
    wait_gf()
    update_of(1)
    update_of(2)
    loop(G // 2, mixed(T, 2 * T))
    s.acc[...] = jnp.zeros_like(s.acc)
    for n in range(2):
        swaps[n]()
        loop(4, lambda g: other(g + 4 * n))

    hat, inv = moments(wide(s.x_v, 1).astype(F32))
    grad_hat = s.acc[...] * gain[...]
    mean = jnp.sum(grad_hat, axis=-1, keepdims=True) * (1.0 / D)
    cross = jnp.sum(grad_hat * hat, axis=-1, keepdims=True) * (1.0 / D)
    total = (s.gu[...] + (grad_hat - mean - hat * cross) * inv).astype(BF)
    for g in range(G):
        s.mix[g] = total[:, g * 128 : (g + 1) * 128]
    def send_back(i, act):
        dev = members[i]
        copy = remote(s.mix.at[dev[1]], back.at[r, pl.ds(w * T, T)], s.s_y.at[i], s.r_y.at[j_own], dev)
        copy.start() if act else copy.wait_send()

    for i in range(1, G):
        send_back(i, True)
    pl.when(away)(lambda: send_back(0, True))

    @pl.when(home)
    def _():
        back[r, pl.ds(w * T, T), :] = s.mix[c]

    weights.finish()
    outs.finish()
    for copy in sends:
        copy.wait_send()
    for i in range(G):
        to_up, to_down = halo((c + i) % G, i)
        pl.when(has_up)(lambda: to_up.wait_send())
        pl.when(has_down)(lambda: to_down.wait_send())
    for i in range(1, G):
        send_fields(i, False)
        send_back(i, False)

    @pl.when(away)
    def _():
        send_fields(0, False)
        send_back(0, False)

    for j in range(G):
        send_state(j, False)

        @pl.when(jnp.logical_not(mine_at[j]))
        def _():
            remote(s.parts.at[j], s.got.at[c], s.s_g.at[j], s.r_g.at[c], windows[j]).wait_send()
            piece = back.at[j // 2, pl.ds((j % 2) * T, T)]
            remote(s.mix.at[0], piece, s.s_y.at[0], s.r_y.at[j], windows[j]).wait_recv()


def finish_kernel(low, back, state, background, misfit, gradient):
    misfit[...] = low[...].astype(F32)
    gradient[...] = state[...].astype(F32) - background[...].astype(F32) + back[...].astype(F32)


def body(state, background, gain, w_query, w_key, w_value, w_out, decoder, interp, obs_values, tile_index, block_count):
    smem = pl.BlockSpec(memory_space=pltpu.SMEM)
    misfit, back = call(
        kernel,
        (sds((L, 16, 128), BF), sds((4, 512, 128), BF)),
        [ANY] * 5 + [VM, VM, VM, ANY, VM, smem],
        [VM] * 2,
        list(SCRATCH.values()),
        0,
        "whole",
        (
            state, w_query, w_key, w_value, w_out, jnp.transpose(decoder), tile_index.reshape(L, 16), gain.reshape(1, D),
            interp.reshape(L, 16, 128, 128), obs_values.reshape(L, 16, 128), block_count.reshape(L),
        ),
    )
    row = pl.BlockSpec((2, 512, 128), lambda i: (i, 0, 0))
    part = pl.BlockSpec((8, 16, 128), lambda i: (i, 0, 0))
    misfit, gradient = pl.pallas_call(
        finish_kernel,
        grid=(2,),
        out_shape=(sds((L, 16, 128), F32), sds((4, 512, 128), F32)),
        in_specs=[part, row, row, row],
        out_specs=(part, row),
        name="finish",
    )(misfit, back, state, background)
    return misfit.reshape(L, 1, 1, 16, 128), gradient


def solution(mesh):
    return jax.shard_map(
        body,
        mesh=mesh,
        in_specs=(
            P("lat", None, "chan"),
            P("lat", None, "chan"),
            P(),
            P(None, "chan"),
            P(None, "chan"),
            P(None, "chan"),
            P("chan", None),
            P("chan", None),
            P("lat", "chan", None, None, None, None),
            P("lat", "chan", None, None, None),
            P("lat", "chan", None, None),
            P("lat", "chan", None),
        ),
        out_specs=(P(None, "chan", "lat", None, None), P("lat", None, "chan")),
        check_vma=False,
    )
```

```python
import functools

import jax
import jax.numpy as jnp
from jax import lax
from jax.experimental import pallas as pl
from jax.experimental.pallas import tpu as pltpu
from jax.sharding import PartitionSpec as P

D = 1024
HD = 64
VARS = 69
EPSILON = 1e-05
VP = 80
T = 256
G = 8
L = 16
BIG = 1e30
MESH = pl.DeviceIdType.MESH
BF = jnp.bfloat16
F32 = jnp.float32
VMEM_LIMIT = 62 * 1024 * 1024


def nn(a, b):
    return lax.dot_general(a, b, (((1,), (0,)), ((), ())), preferred_element_type=F32)


def nt(a, b):
    return lax.dot_general(a, b, (((1,), (1,)), ((), ())), preferred_element_type=F32)


def place():
    b = lax.axis_index("lat")
    c = lax.axis_index("chan")
    k = b % 2
    big = b // 2
    q = 2 * (c % 4) + k
    row = q + (big % 2) * (7 - 2 * q)
    return b, c, k, big, row, c // 4


def holder(big, row, w):
    q = row + (big % 2) * (7 - 2 * row)
    return big * 2 + q % 2, w * 4 + q // 2


def neighbours():
    b, c, k, big, row, w = place()
    q = 2 * (c % 4) + k
    step = 1 - 2 * (big % 2)
    inner_up = (row > 0).astype(jnp.int32)
    inner_down = (row < 7).astype(jnp.int32)
    q_up, q_down = q - step * inner_up, q + step * inner_down
    up = ((big - 1 + inner_up) * 2 + q_up % 2, w * 4 + q_up // 2)
    down = ((big + 1 - inner_down) * 2 + q_down % 2, w * 4 + q_down // 2)
    return up, down, big * 8 + row > 0, big * 8 + row < 4 * L - 1


def lat_peer(i):
    b, c = lax.axis_index("lat"), lax.axis_index("chan")
    return ((b + i) % L, c)


def far_flip():
    b, c = lax.axis_index("lat"), lax.axis_index("chan")
    return (b + 2 - 4 * ((b // 2) % 2), (c + 4) % G)


def greeted():
    b, c, k, big, _, _ = place()
    barrier = pltpu.get_barrier_semaphore()
    peers = [(b, (c + i) % G) for i in range(1, G)]
    peers += [(b + 1 - 2 * k, (c + i) % G) for i in range(G)]
    peers += [(2 * ((big + i) % 8) + j, c) for i in range(1, 8) for j in range(2)]
    peers.append(far_flip())
    for dev in peers:
        pl.semaphore_signal(barrier, inc=1, device_id=dev, device_id_type=MESH)
    return lambda: pl.semaphore_wait(barrier, len(peers))


def remote(src, dst, ss, rs, dev):
    return pltpu.make_async_remote_copy(
        src_ref=src, dst_ref=dst, send_sem=ss, recv_sem=rs, device_id=dev, device_id_type=MESH
    )


def call(kernel, out_shape, in_specs, out_specs, scratch, cid, name, args):
    return pl.pallas_call(
        kernel,
        out_shape=out_shape,
        in_specs=in_specs,
        out_specs=out_specs,
        scratch_shapes=scratch,
        compiler_params=pltpu.CompilerParams(
            collective_id=cid, has_side_effects=cid is not None, vmem_limit_bytes=VMEM_LIMIT
        ),
        name=name,
    )(*args)


VM = pl.BlockSpec(memory_space=pltpu.VMEM)
ANY = pl.BlockSpec(memory_space=pl.ANY)
DMA = pltpu.SemaphoreType.DMA


def sds(shape, dtype):
    return jax.ShapeDtypeStruct(shape, dtype)


class Spread:
    def __init__(self, view, size, sems):
        self.view, self.half = view, size // 2
        self.s1, self.r1, self.s2, self.r2, self.s3, self.r3, self.s4, self.r4, self.s5, self.r5 = sems
        b, c, k, _, _, z = place()
        x, y = c % 4, b // 4
        p = y % 2
        self.b, self.c, self.x, self.z = b, c, x, z
        self.start = (p * 2 + k) * size
        self.across = ((1 - p) * 2 + k) * size
        self.turn = (1 - 2 * k) * size
        self.core = (b + 1 - 2 * k, c)
        self.ups = [((b + 4) % L, c), ((b + 12) % L, c)]
        self.flips = [(b, (c + 4) % G), far_flip()]

    def send(self, g, start, size, ss, rs, dev):
        ref = self.view(g, start, size)
        copy = remote(ref, ref, ss, rs, dev)
        copy.start()

    def wait(self, g, start, size, rs):
        ref = self.view(g, start, size)
        remote(ref, ref, self.s1.at[0], rs, self.core).wait_recv()

    def from_x(self, i):
        return self.z * 4 + (self.x + 4 - i) % 4

    def from_z(self, i):
        return (1 - self.z) * 4 + (self.x + 4 - i) % 4

    def along_z(self, g):
        for h in range(2):
            at = self.start + h * self.half
            self.send(g, at, self.half, self.s2.at[h, g], self.r2.at[h, g], self.flips[h])

    def first(self):
        for i in (1, 3, 2):
            dev = (self.b, self.z * 4 + (self.x + i) % 4)
            self.send(self.c, self.start, 2 * self.half, self.s1.at[i], self.r1.at[self.c], dev)
        self.along_z(self.c)

    def fan(self, g, h):
        at = self.start + h * self.half
        self.send(g, at, self.half, self.s4.at[h, g], self.r4.at[h, g], self.ups[h])
        self.send(g, at, self.half, self.s3.at[h, g], self.r3.at[h, g], self.core)

    def relay_x(self, i):
        g = self.from_x(i)
        self.wait(g, self.start, 2 * self.half, self.r1.at[g])
        self.along_z(g)
        self.fan(g, 0)
        self.fan(g, 1)

    def relay_z(self, i):
        g = self.from_z(i)
        for h in range(2):
            self.wait(g, self.start + h * self.half, self.half, self.r2.at[h, g])
            self.fan(g, h)

    def relay_y(self, g):
        for h in range(2):
            at = self.across + h * self.half
            self.wait(g, at, self.half, self.r4.at[h, g])
            self.send(g, at, self.half, self.s5.at[h, g], self.r5.at[h, g], self.core)

    def ready(self, g):
        for h in range(2):
            self.wait(g, self.start + self.turn + h * self.half, self.half, self.r3.at[h, g])
            self.wait(g, self.across + self.turn + h * self.half, self.half, self.r5.at[h, g])

    def finish(self):
        def sent(g, start, size, sem):
            ref = self.view(g, start, size)
            remote(ref, ref, sem, self.r1.at[0], self.core).wait_send()

        half = self.half
        for i in (1, 3, 2):
            sent(self.c, self.start, 2 * half, self.s1.at[i])
        for i in range(4):
            row = self.from_x(i)
            for h in range(2):
                at = self.start + h * half
                sent(row, at, half, self.s2.at[h, row])
                for g in ([row] if i else []) + [self.from_z(i)]:
                    sent(g, at, half, self.s3.at[h, g])
                    sent(g, at, half, self.s4.at[h, g])
                    sent(g, self.across + h * half, half, self.s5.at[h, g])


def wide(ref, h):
    return jnp.concatenate([ref[h, g] for g in range(G)], axis=1)


def moments(x):
    mean = jnp.sum(x, axis=-1, keepdims=True) * (1.0 / D)
    centred = x - mean
    var = jnp.sum(centred * centred, axis=-1, keepdims=True) * (1.0 / D)
    inv = lax.rsqrt(var + EPSILON)
    return centred * inv, inv


def only(value, hh):
    first = lax.broadcasted_iota(jnp.int32, value.shape, 1) < HD
    keep = first if hh == 0 else jnp.logical_not(first)
    return jnp.where(keep, value, jnp.zeros_like(value))


def swap_rows(src, above, below, ss, rs):
    up, down, has_up, has_down = neighbours()
    to_up = remote(src, below, ss.at[0], rs.at[0], up)
    to_down = remote(src, above, ss.at[1], rs.at[1], down)

    def start():
        pl.when(has_up)(lambda: to_up.start())
        pl.when(has_down)(lambda: to_down.start())

    def wait():
        @pl.when(has_up)
        def _():
            to_up.wait_send()
            to_down.wait_recv()

        @pl.when(has_down)
        def _():
            to_down.wait_send()
            to_up.wait_recv()

    return start, wait


def loop(n, step):
    def wrapped(i, carry):
        step(i)
        return carry

    lax.fori_loop(0, n, wrapped, 0)


SCRATCH = dict(
    x_v=pltpu.VMEM((3, G, T, 128), BF),
    w_v=pltpu.VMEM((G, 3, D, 128), BF),
    o_v=pltpu.VMEM((G, 128, D), BF),
    d_v=pltpu.VMEM((G, VP, 128), BF),
    i_v=pltpu.VMEM((L, 16, 128), jnp.int32),
    itp=pltpu.VMEM((L, 16, 128, 128), BF),
    n_v=pltpu.VMEM((3 * T, D), BF),
    qkv=pltpu.VMEM((3, G, 3 * T, 128), BF),
    kt=pltpu.VMEM((G, 128, 3 * T), BF),
    mix=pltpu.VMEM((G, T, 128), BF),
    acc=pltpu.VMEM((T, D), F32),
    ml=pltpu.VMEM((2, 16, 1, T), F32),
    mlh=pltpu.VMEM((2, 2, 16, 1, T), F32),
    fields=pltpu.VMEM((G, VP, T), BF),
    mine=pltpu.VMEM((L, 16, 128), BF),
    picked=pltpu.VMEM((L, 16, 128), BF),
    am=pltpu.VMEM((L, 32, 128), BF),
    came=pltpu.VMEM((L, 32, 128), BF),
    parts=pltpu.VMEM((G, VP, T), BF),
    got=pltpu.VMEM((G, VP, T), BF),
    gf=pltpu.VMEM((3, VP, T), F32),
    gu=pltpu.VMEM((T, D), F32),
    do=pltpu.VMEM((G, 3 * T, 128), BF),
    dq=pltpu.VMEM((G, T, 128), BF),
    dso=pltpu.VMEM((G, T, 2 * T), BF),
    dp=pltpu.VMEM((2, 3 * T, T), F32),
    ds=pltpu.VMEM((2, 3 * T, T), BF),
    hat=pltpu.VMEM((T, D), F32),
    inv=pltpu.VMEM((T, 128), F32),
    p_own=pltpu.VMEM((16, 3 * T, T), F32),
    p_nb=pltpu.VMEM((2, 16, T, T), F32),
    delta=pltpu.VMEM((16, 1, T), F32),
    delta_h=pltpu.VMEM((2, 16, 1, T), F32),
    f_own=pltpu.VMEM((VP, T), BF),
    i_own=pltpu.VMEM((L, 16, 128), jnp.int32),
    loc=DMA((8,)),
    s_state=DMA((G,)), r_state=DMA((G,)),
    s_d=DMA((G,)), r_d=DMA((G,)),
    s_i=DMA((L,)), r_i=DMA((L,)),
    s_h=DMA((2, G)), r_h=DMA((2, G)),
    s_f=DMA((G,)), r_f=DMA((G,)),
    s_p=DMA((L,)), r_p=DMA((L,)),
    s_a=DMA((L,)), r_a=DMA((L,)),
    s_g=DMA((G,)), r_g=DMA((G,)),
    s_y=DMA((G,)), r_y=DMA((G,)),
    s_m=DMA((2,)), r_m=DMA((2,)),
    s_gh=DMA((2,)), r_gh=DMA((2,)),
    s_dl=DMA((2, 2)), r_dl=DMA((2, 2)),
    w1=DMA((4,)), w2=DMA((G,)), w3=DMA((2, G)), w4=DMA((2, G)), w5=DMA((2, G)), w6=DMA((2, G)), w7=DMA((2, G)), w8=DMA((2, G)), w9=DMA((2, G)), w10=DMA((2, G)),
    o1=DMA((4,)), o2=DMA((G,)), o3=DMA((2, G)), o4=DMA((2, G)), o5=DMA((2, G)), o6=DMA((2, G)), o7=DMA((2, G)), o8=DMA((2, G)), o9=DMA((2, G)), o10=DMA((2, G)),
)


class Refs:
    pass


def kernel(state, wq, wk, wv, wo, dec, idx, gain, interp, obs, count, misfit, back, *scratch):
    s = Refs()
    for name, ref in zip(SCRATCH, scratch):
        setattr(s, name, ref)
    b, c, k, big, row8, w = place()
    r = row8 % 4
    band = 2 * big + row8 // 4
    j_own = r * 2 + w
    home = band == b
    up, down, has_up, has_down = neighbours()
    up_bias = jnp.where(has_up, 0.0, -BIG).astype(F32)
    down_bias = jnp.where(has_down, 0.0, -BIG).astype(F32)
    own_rows = pl.ds(0, T)
    eighth = jnp.asarray(0.125, BF)
    away = jnp.logical_not(home)
    windows = [holder(big, 4 * k + j // 2, j % 2) for j in range(G)]
    mine_at = [jnp.logical_and(home, j_own == j) for j in range(G)]
    members = [(band, (c + i) % G) for i in range(G)]

    met = greeted()
    local = [
        pltpu.make_async_copy(wq, s.w_v.at[c, 0], s.loc.at[0]),
        pltpu.make_async_copy(wk, s.w_v.at[c, 1], s.loc.at[1]),
        pltpu.make_async_copy(wv, s.w_v.at[c, 2], s.loc.at[2]),
        pltpu.make_async_copy(wo, s.o_v.at[c], s.loc.at[3]),
    ]
    for copy in local:
        copy.start()

    @pl.when(jnp.logical_not(has_up))
    def _():
        s.x_v[0] = jnp.zeros((G, T, 128), BF)

    @pl.when(jnp.logical_not(has_down))
    def _():
        s.x_v[2] = jnp.zeros((G, T, 128), BF)

    s.mlh[:, 0] = jnp.full((2, 16, 1, T), BIG, F32)
    s.mlh[:, 1] = jnp.zeros((2, 16, 1, T), F32)
    s.delta_h[...] = jnp.zeros_like(s.delta_h)
    s.gf[...] = jnp.zeros_like(s.gf)
    eye = lax.broadcasted_iota(jnp.int32, (VP, VARS), 0) == lax.broadcasted_iota(jnp.int32, (VP, VARS), 1)
    s.d_v[c] = nn(eye.astype(F32).astype(BF), dec[...]).astype(BF)
    for n in range(16):
        s.i_own[:, n, :] = jnp.broadcast_to(idx[:, n : n + 1], (L, 128))
    s.i_v[b] = s.i_own[b]
    met()

    sends = []

    def send_state(j, act):
        src = state.at[j // 2, pl.ds((j % 2) * T, T)]

        @pl.when(jnp.logical_not(mine_at[j]))
        def _():
            copy = remote(src, s.x_v.at[1, c], s.s_state.at[j], s.r_state.at[c], windows[j])
            copy.start() if act else copy.wait_send()

        if act:
            @pl.when(mine_at[j])
            def _():
                pltpu.make_async_copy(src, s.x_v.at[1, c], s.loc.at[4]).start()

    for j in range(G):
        send_state(j, True)
    weights = Spread(
        lambda g, at, n: s.w_v.at[g, :, pl.ds(at, n)], 256, (s.w1, s.w2, s.w3, s.w4, s.w5, s.w6, s.w7, s.w8, s.w9, s.w10)
    )
    outs = Spread(
        lambda g, at, n: s.o_v.at[g, pl.ds(at, n)], 32, (s.o1, s.o2, s.o3, s.o4, s.o5, s.o6, s.o7, s.o8, s.o9, s.o10)
    )
    for copy in local[:3]:
        copy.wait()
    weights.first()
    fetch = pltpu.make_async_copy(interp, s.itp, s.loc.at[5])
    fetch.start()
    for i in range(1, L):
        dev = lat_peer(i)
        copy = remote(s.i_own.at[dev[0]], s.i_v.at[b], s.s_i.at[i], s.r_i.at[i], dev)
        copy.start()
        sends.append(copy)

    def halo(g, sem):
        to_up = remote(s.x_v.at[1, g], s.x_v.at[2, g], s.s_h.at[0, sem], s.r_h.at[0, sem], up)
        to_down = remote(s.x_v.at[1, g], s.x_v.at[0, g], s.s_h.at[1, sem], s.r_h.at[1, sem], down)
        return to_up, to_down

    def start_halo(g, sem):
        to_up, to_down = halo(g, sem)
        pl.when(has_up)(lambda: to_up.start())
        pl.when(has_down)(lambda: to_down.start())

    def got_state(g):
        piece = s.x_v.at[1, g]
        remote(piece, piece, s.s_state.at[0], s.r_state.at[g], members[1]).wait_recv()

    @pl.when(home)
    def _():
        pltpu.make_async_copy(state.at[0, pl.ds(0, T)], s.x_v.at[1, c], s.loc.at[4]).wait()

    pl.when(away)(lambda: got_state(c))
    start_halo(c, 0)
    for i in (1, 3, 4, 5, 7, 2, 6):
        g = (c + i) % G
        got_state(g)
        start_halo(g, i)
    weights.relay_z(0)
    for i in (1, 3, 2):
        weights.relay_x(i)
    local[3].wait()
    outs.first()
    for i in range(1, G):
        copy = remote(s.d_v.at[c], s.d_v.at[c], s.s_d.at[i], s.r_d.at[i], (b, (c + i) % G))
        copy.start()
        sends.append(copy)

    def norm(h, at):
        hat, inv = moments(wide(s.x_v, h).astype(F32))
        if h == 1:
            s.hat[...] = hat
            s.inv[...] = jnp.broadcast_to(inv, (T, 128))
        s.n_v[pl.ds(at * T, T), :] = (hat * gain[...]).astype(BF)

    norm(1, 0)
    weights.relay_y(weights.from_z(0))
    weights.relay_y(weights.from_x(1))
    weights.relay_y(weights.from_x(3))
    for i in range(G):
        to_up, to_down = halo((c + i) % G, i)
        pl.when(has_down)(lambda: to_up.wait_recv())
        pl.when(has_up)(lambda: to_down.wait_recv())
    norm(0, 1)
    norm(2, 2)
    weights.relay_z(1)
    weights.relay_y(weights.from_x(2))
    weights.relay_z(3)

    def attend(i):
        t = (i + 1) % 3
        late = (i >= 2).astype(jnp.int32)
        over = (i >= 5).astype(jnp.int32) + (i == 1).astype(jnp.int32)
        back_by = late * (1 + t * (7 - 3 * t) // 2)
        g = (w + over * (1 - 2 * w)) * 4 + (c % 4 + 4 - back_by) % 4

        def relays(n):
            return pl.when(i == n)

        pl.when(i > 0)(lambda: weights.ready(g))

        @relays(1)
        def _():
            weights.relay_z(2)
            weights.relay_y(weights.from_z(1))

        @relays(2)
        def _():
            weights.relay_y(weights.from_z(3))

        @relays(3)
        def _():
            weights.relay_y(weights.from_z(2))
            outs.relay_z(0)
            for n in (1, 3, 2):
                outs.relay_x(n)

        @relays(5)
        def _():
            for n in (1, 3, 2):
                outs.relay_z(n)
            outs.relay_y(outs.from_z(0))
            for n in (1, 3, 2):
                outs.relay_y(outs.from_x(n))

        @relays(7)
        def _():
            for n in (1, 3, 2):
                outs.relay_y(outs.from_z(n))

        own_res = nn(s.n_v[:T, :], jnp.concatenate([s.w_v[g, n] for n in range(3)], axis=1))
        near_res = nn(s.n_v[T:, :], jnp.concatenate([s.w_v[g, 1], s.w_v[g, 2]], axis=1))
        for n in range(3):
            s.qkv[n, g, :T, :] = own_res[:, n * 128 : (n + 1) * 128].astype(BF)
        for n in range(2):
            s.qkv[n + 1, g, T:, :] = near_res[:, n * 128 : (n + 1) * 128].astype(BF)
        vt = jnp.transpose(jnp.concatenate([own_res[:, 256:], near_res[:, 128:]], axis=0)).astype(BF)
        query = s.qkv[0, g, own_rows, :] * eighth
        scores = [nt(s.qkv[1, g], only(query, hh)) for hh in range(2)]
        parts = []
        for hh in range(2):
            n = 2 * g + hh
            sc = scores[hh]
            m0 = jnp.max(sc[:T], axis=0, keepdims=True)
            m1 = jnp.max(sc[T : 2 * T], axis=0, keepdims=True) + up_bias
            m2 = jnp.max(sc[2 * T :], axis=0, keepdims=True) + down_bias
            m = jnp.maximum(jnp.maximum(m0, m1), m2)
            e0 = jnp.exp(sc[:T] - m)
            e1 = jnp.exp(sc[T : 2 * T] - (m - up_bias))
            e2 = jnp.exp(sc[2 * T :] - (m - down_bias))
            l = jnp.sum(e0, axis=0, keepdims=True) + jnp.sum(e1, axis=0, keepdims=True) + jnp.sum(e2, axis=0, keepdims=True)
            inv = 1.0 / l
            s.p_own[n, :T, :] = e0 * inv
            s.p_own[n, T : 2 * T, :] = e1 * inv
            s.p_own[n, 2 * T :, :] = e2 * inv
            p = s.p_own[n].astype(BF)
            parts.append(nn(vt[hh * HD : (hh + 1) * HD], p))
            s.ml[0, n] = m
            s.ml[1, n] = inv
        s.mix[g] = jnp.transpose(jnp.concatenate(parts, axis=0)).astype(BF)

    loop(G, attend)
    start_ml, wait_ml = swap_rows(s.ml, s.mlh.at[0], s.mlh.at[1], s.s_m, s.r_m)
    start_ml()
    for n in range(4):
        if n:
            outs.ready(outs.from_x(n))
        outs.ready(outs.from_z(n))
    for i in range(1, G):
        remote(s.d_v.at[c], s.d_v.at[c], s.s_d.at[i], s.r_d.at[i], members[i]).wait_recv()
    def out(m):
        cols = pl.ds(pl.multiple_of(m * 256, 256), 256)
        total = nn(s.mix[0], s.o_v[0, :, cols]).astype(BF).astype(F32)
        for g in range(1, G):
            total = total + nn(s.mix[g], s.o_v[g, :, cols]).astype(BF).astype(F32)
        s.acc[:, cols] = total

    loop(4, out)
    updated = (wide(s.x_v, 1).astype(F32) + s.acc[...]).astype(BF)
    dec_all = jnp.concatenate([s.d_v[g] for g in range(G)], axis=1)
    s.f_own[...] = nt(dec_all, updated).astype(BF)

    def send_fields(i, act):
        copy = remote(s.f_own, s.fields.at[j_own], s.s_f.at[i], s.r_f.at[j_own], members[i])
        copy.start() if act else copy.wait_send()

    for i in range(1, G):
        send_fields(i, True)
    pl.when(away)(lambda: send_fields(0, True))

    @pl.when(home)
    def _():
        s.fields[j_own] = s.f_own[...]

    for i in range(1, L):
        remote(s.i_own.at[b], s.i_v.at[b], s.s_i.at[i], s.r_i.at[i], lat_peer(i)).wait_recv()
    index = s.i_v[...].reshape(16 * L, 128)
    lanes = lax.broadcasted_iota(jnp.int32, (16 * L, 128), 1) * 16

    total = jnp.zeros((16 * L, 128), F32)
    for j in range(G):
        @pl.when(jnp.logical_not(mine_at[j]))
        def _():
            remote(s.f_own, s.fields.at[j], s.s_f.at[0], s.r_f.at[j], windows[j]).wait_recv()

        for half in range(2):
            hot = (index == lanes + (2 * j + half)).astype(F32).astype(BF)
            total = total + nn(hot[:, :VP], s.fields[j, :, pl.ds(half * 128, 128)])
    s.mine[...] = total.astype(BF).reshape(L, 16, 128)
    for i in range(1, L):
        dev = lat_peer(i)
        copy = remote(s.mine.at[dev[0]], s.picked.at[b], s.s_p.at[i], s.r_p.at[i], dev)
        copy.start()
        sends.append(copy)
    s.picked[b] = s.mine[b]

    wait_ml()

    def near(g):
        s.kt[g] = jnp.transpose(s.qkv[1, g].astype(F32)).astype(BF)
        for side in range(2):
            query = s.qkv[0, g, pl.ds((1 + side) * T, T), :] * eighth
            for hh in range(2):
                n = 2 * g + hh
                sc = nt(s.qkv[1, g, own_rows, :], only(query, hh))
                s.p_nb[side, n] = jnp.exp(sc - s.mlh[side, 0, n]) * s.mlh[side, 1, n]

    def near_queries(m):
        both = nn(s.n_v[T:, :], jnp.concatenate([s.w_v[2 * m, 0], s.w_v[2 * m + 1, 0]], axis=1)).astype(BF)
        s.qkv[0, 2 * m, T:, :] = both[:, :128]
        s.qkv[0, 2 * m + 1, T:, :] = both[:, 128:]

    loop(2, near_queries)
    loop(4, near)

    fetch.wait()
    row = lax.broadcasted_iota(jnp.int32, (16, 128), 0)

    def observe(i):
        other_b = (b + L - i) % L

        @pl.when(i > 0)
        def _():
            remote(s.mine.at[b], s.picked.at[b], s.s_p.at[i], s.r_p.at[i], (other_b, c)).wait_recv()

        flat = s.itp[other_b].reshape(2048, 128)
        big = nt(s.picked[other_b], flat)
        pred = jnp.zeros((16, 128), F32)
        for n in range(16):
            pred = jnp.where(row == n, big[:, n * 128 : (n + 1) * 128], pred)
        mis = jnp.where(row < count[other_b], pred - obs[other_b].astype(F32), 0.0).astype(BF)
        lhs = jnp.concatenate([jnp.where(row == n, mis, jnp.zeros_like(mis)) for n in range(16)], axis=1)
        s.am[other_b, :16, :] = nn(lhs, flat).astype(BF)
        s.am[other_b, 16:, :] = mis

        @pl.when(i > 0)
        def _():
            remote(s.am.at[other_b], s.came.at[b], s.s_a.at[i], s.r_a.at[i], (other_b, c)).start()

    loop(L, observe)
    s.came[b] = s.am[b]

    loop(2, lambda m: near_queries(m + 2))
    loop(4, lambda g: near(g + 4))

    index_t = jnp.transpose(index.astype(F32))[:VP].astype(jnp.int32)
    sub = lax.broadcasted_iota(jnp.int32, (VP, 16 * L), 0) * 16

    def arrived(i):
        other_b = (b + i) % L

        @pl.when(i > 0)
        def _():
            remote(s.am.at[b], s.came.at[b], s.s_a.at[i], s.r_a.at[i], (other_b, c)).wait()

    loop(L, arrived)
    misfit[...] = s.came[:, 16:, :]
    adjoint = s.came[:, :16, :].reshape(16 * L, 128)
    for j in range(G):
        for half in range(2):
            hot = (index_t == sub + (2 * j + half)).astype(F32).astype(BF)
            s.parts[j, :, pl.ds(half * 128, 128)] = nn(hot, adjoint).astype(BF)

        @pl.when(jnp.logical_not(mine_at[j]))
        def _():
            remote(s.parts.at[j], s.got.at[c], s.s_g.at[j], s.r_g.at[c], windows[j]).start()

        @pl.when(mine_at[j])
        def _():
            s.got[c] = s.parts[j]

    def got_part(g):
        remote(s.parts.at[0], s.got.at[g], s.s_g.at[0], s.r_g.at[g], members[1]).wait_recv()

    pl.when(away)(lambda: got_part(c))
    total = s.got[c].astype(F32)
    for i in range(1, G):
        got_part((c + i) % G)
        total = total + s.got[(c + i) % G].astype(F32)
    s.gf[0] = total
    start_gf, wait_gf = swap_rows(s.gf.at[0], s.gf.at[1], s.gf.at[2], s.s_gh, s.r_gh)
    start_gf()

    dec_all = jnp.concatenate([dec_all, jnp.zeros((128 - VP, D), BF)], axis=0)
    dec3 = jnp.concatenate([dec_all, dec_all, dec_all], axis=0)

    def update_of(h):
        field = jnp.transpose(jnp.concatenate([s.gf[h], jnp.zeros((128 - VP, T), F32)], axis=0))
        hi = field.astype(BF)
        rest = field - hi.astype(F32)
        mid = rest.astype(BF)
        lo = (rest - mid.astype(F32)).astype(BF)
        update = nn(jnp.concatenate([hi, mid, lo], axis=1), dec3)
        s.n_v[pl.ds(h * T, T), :] = update.astype(BF)
        return update

    def mixed(rows, n):
        def step(m):
            weight = jnp.concatenate([s.o_v[2 * m], s.o_v[2 * m + 1]], axis=0)
            res = nt(s.n_v[pl.ds(rows, n), :], weight).astype(BF)
            s.do[2 * m, pl.ds(rows, n), :] = res[:, :128]
            s.do[2 * m + 1, pl.ds(rows, n), :] = res[:, 128:]

        return step

    def own(g):
        for hh in range(2):
            s.dp[hh] = nt(s.qkv[2, g], only(s.do[g, own_rows, :], hh))
        parts = []
        for hh in range(2):
            n = 2 * g + hh
            along = jnp.zeros((8, T), F32)
            for at in range(0, 3 * T, 64):
                product = s.p_own[n, at : at + 64, :] * s.dp[hh, at : at + 64, :]
                along = along + jnp.sum(product.reshape(8, 8, T), axis=0)
            along = jnp.sum(along, axis=0, keepdims=True)
            s.delta[n] = along
            for at in range(0, 3 * T, 64):
                spread = s.p_own[n, at : at + 64, :] * (s.dp[hh, at : at + 64, :] - along)
                s.ds[hh, at : at + 64, :] = spread.astype(BF)
            parts.append(nn(s.kt[g, pl.ds(hh * HD, HD), :], s.ds[hh]) * 0.125)
            s.dso[g, :, pl.ds(hh * T, T)] = s.ds[hh, :T, :]
        s.dq[g] = jnp.transpose(jnp.concatenate(parts, axis=0)).astype(BF)

    def other(g):
        scores, probs, queries, grads = [s.dso[g]], [], [], []
        for hh in range(2):
            probs.append(s.p_own[2 * g + hh, :T, :].astype(BF))
            queries.append(only(s.qkv[0, g, own_rows, :] * eighth, hh))
            grads.append(only(s.do[g, own_rows, :], hh))
        for side in range(2):
            rows = pl.ds((1 + side) * T, T)
            for hh in range(2):
                n = 2 * g + hh
                queries.append(only(s.qkv[0, g, rows, :] * eighth, hh))
                grads.append(only(s.do[g, rows, :], hh))
                dp = nt(s.qkv[2, g, own_rows, :], grads[-1])
                p = s.p_nb[side, n]
                scores.append((p * (dp - s.delta_h[side, n])).astype(BF))
                probs.append(p.astype(BF))
        dk = nn(jnp.concatenate(scores, axis=1), jnp.concatenate(queries, axis=0))
        dv = nn(jnp.concatenate(probs, axis=1), jnp.concatenate(grads, axis=0))
        three = jnp.concatenate([s.dq[g], dk.astype(BF), dv.astype(BF)], axis=1)
        wide_w = jnp.concatenate([s.w_v[g, 0], s.w_v[g, 1], s.w_v[g, 2]], axis=1)
        s.acc[...] += nt(three, wide_w).astype(BF).astype(F32)

    s.gu[...] = update_of(0)
    loop(G // 2, mixed(0, T))
    swaps = []
    for n in range(2):
        loop(4, lambda g: own(g + 4 * n))
        heads = pl.ds(8 * n, 8)
        start, wait = swap_rows(
            s.delta.at[heads], s.delta_h.at[0, heads], s.delta_h.at[1, heads], s.s_dl.at[n], s.r_dl.at[n]
        )
        start()
        swaps.append(wait)
    wait_gf()
    update_of(1)
    update_of(2)
    loop(G // 2, mixed(T, 2 * T))
    s.acc[...] = jnp.zeros_like(s.acc)
    for n in range(2):
        swaps[n]()
        loop(4, lambda g: other(g + 4 * n))

    hat, inv = s.hat[...], s.inv[:, :1]
    grad_hat = s.acc[...] * gain[...]
    mean = jnp.sum(grad_hat, axis=-1, keepdims=True) * (1.0 / D)
    cross = jnp.sum(grad_hat * hat, axis=-1, keepdims=True) * (1.0 / D)
    total = (s.gu[...] + (grad_hat - mean - hat * cross) * inv).astype(BF)
    for g in range(G):
        s.mix[g] = total[:, g * 128 : (g + 1) * 128]
    def send_back(i, act):
        dev = members[i]
        copy = remote(s.mix.at[dev[1]], back.at[r, pl.ds(w * T, T)], s.s_y.at[i], s.r_y.at[j_own], dev)
        copy.start() if act else copy.wait_send()

    for i in range(1, G):
        send_back(i, True)
    pl.when(away)(lambda: send_back(0, True))

    @pl.when(home)
    def _():
        back[r, pl.ds(w * T, T), :] = s.mix[c]

    weights.finish()
    outs.finish()
    for copy in sends:
        copy.wait_send()
    for i in range(G):
        to_up, to_down = halo((c + i) % G, i)
        pl.when(has_up)(lambda: to_up.wait_send())
        pl.when(has_down)(lambda: to_down.wait_send())
    for i in range(1, G):
        send_fields(i, False)
        send_back(i, False)

    @pl.when(away)
    def _():
        send_fields(0, False)
        send_back(0, False)

    for j in range(G):
        send_state(j, False)

        @pl.when(jnp.logical_not(mine_at[j]))
        def _():
            remote(s.parts.at[j], s.got.at[c], s.s_g.at[j], s.r_g.at[c], windows[j]).wait_send()
            piece = back.at[j // 2, pl.ds((j % 2) * T, T)]
            remote(s.mix.at[0], piece, s.s_y.at[0], s.r_y.at[j], windows[j]).wait_recv()


def finish_kernel(low, back, state, background, misfit, gradient):
    misfit[...] = low[...].astype(F32)
    gradient[...] = state[...].astype(F32) - background[...].astype(F32) + back[...].astype(F32)


def body(state, background, gain, w_query, w_key, w_value, w_out, decoder, interp, obs_values, tile_index, block_count):
    smem = pl.BlockSpec(memory_space=pltpu.SMEM)
    misfit, back = call(
        kernel,
        (sds((L, 16, 128), BF), sds((4, 512, 128), BF)),
        [ANY] * 5 + [VM, VM, VM, ANY, VM, smem],
        [VM] * 2,
        list(SCRATCH.values()),
        0,
        "whole",
        (
            state, w_query, w_key, w_value, w_out, jnp.transpose(decoder), tile_index.reshape(L, 16), gain.reshape(1, D),
            interp.reshape(L, 16, 128, 128), obs_values.reshape(L, 16, 128), block_count.reshape(L),
        ),
    )
    row = pl.BlockSpec((2, 512, 128), lambda i: (i, 0, 0))
    part = pl.BlockSpec((8, 16, 128), lambda i: (i, 0, 0))
    misfit, gradient = pl.pallas_call(
        finish_kernel,
        grid=(2,),
        out_shape=(sds((L, 16, 128), F32), sds((4, 512, 128), F32)),
        in_specs=[part, row, row, row],
        out_specs=(part, row),
        name="finish",
    )(misfit, back, state, background)
    return misfit.reshape(L, 1, 1, 16, 128), gradient


def solution(mesh):
    return jax.shard_map(
        body,
        mesh=mesh,
        in_specs=(
            P("lat", None, "chan"),
            P("lat", None, "chan"),
            P(),
            P(None, "chan"),
            P(None, "chan"),
            P(None, "chan"),
            P("chan", None),
            P("chan", None),
            P("lat", "chan", None, None, None, None),
            P("lat", "chan", None, None, None),
            P("lat", "chan", None, None),
            P("lat", "chan", None),
        ),
        out_specs=(P(None, "chan", "lat", None, None), P("lat", None, "chan")),
        check_vma=False,
    )
```

```python
import functools

import jax
import jax.numpy as jnp
from jax import lax
from jax.experimental import pallas as pl
from jax.experimental.pallas import tpu as pltpu
from jax.sharding import PartitionSpec as P

D = 1024
HD = 64
VARS = 69
EPSILON = 1e-05
VP = 80
T = 256
G = 8
L = 16
BIG = 1e30
MESH = pl.DeviceIdType.MESH
BF = jnp.bfloat16
F32 = jnp.float32
VMEM_LIMIT = 62 * 1024 * 1024


def nn(a, b):
    return lax.dot_general(a, b, (((1,), (0,)), ((), ())), preferred_element_type=F32)


def nt(a, b):
    return lax.dot_general(a, b, (((1,), (1,)), ((), ())), preferred_element_type=F32)


def place():
    b = lax.axis_index("lat")
    c = lax.axis_index("chan")
    k = b % 2
    big = b // 2
    q = 2 * (c % 4) + k
    row = q + (big % 2) * (7 - 2 * q)
    return b, c, k, big, row, c // 4


def holder(big, row, w):
    q = row + (big % 2) * (7 - 2 * row)
    return big * 2 + q % 2, w * 4 + q // 2


def neighbours():
    b, c, k, big, row, w = place()
    q = 2 * (c % 4) + k
    step = 1 - 2 * (big % 2)
    inner_up = (row > 0).astype(jnp.int32)
    inner_down = (row < 7).astype(jnp.int32)
    q_up, q_down = q - step * inner_up, q + step * inner_down
    up = ((big - 1 + inner_up) * 2 + q_up % 2, w * 4 + q_up // 2)
    down = ((big + 1 - inner_down) * 2 + q_down % 2, w * 4 + q_down // 2)
    return up, down, big * 8 + row > 0, big * 8 + row < 4 * L - 1


def lat_peer(i):
    b, c = lax.axis_index("lat"), lax.axis_index("chan")
    return ((b + i) % L, c)


def far_flip():
    b, c = lax.axis_index("lat"), lax.axis_index("chan")
    return (b + 2 - 4 * ((b // 2) % 2), (c + 4) % G)


def greeted():
    b, c, k, big, _, _ = place()
    barrier = pltpu.get_barrier_semaphore()
    peers = [(b, (c + i) % G) for i in range(1, G)]
    peers += [(b + 1 - 2 * k, (c + i) % G) for i in range(G)]
    peers += [(2 * ((big + i) % 8) + j, c) for i in range(1, 8) for j in range(2)]
    peers.append(far_flip())
    for dev in peers:
        pl.semaphore_signal(barrier, inc=1, device_id=dev, device_id_type=MESH)
    return lambda: pl.semaphore_wait(barrier, len(peers))


def remote(src, dst, ss, rs, dev):
    return pltpu.make_async_remote_copy(
        src_ref=src, dst_ref=dst, send_sem=ss, recv_sem=rs, device_id=dev, device_id_type=MESH
    )


def call(kernel, out_shape, in_specs, out_specs, scratch, cid, name, args):
    return pl.pallas_call(
        kernel,
        out_shape=out_shape,
        in_specs=in_specs,
        out_specs=out_specs,
        scratch_shapes=scratch,
        compiler_params=pltpu.CompilerParams(
            collective_id=cid, has_side_effects=cid is not None, vmem_limit_bytes=VMEM_LIMIT
        ),
        name=name,
    )(*args)


VM = pl.BlockSpec(memory_space=pltpu.VMEM)
ANY = pl.BlockSpec(memory_space=pl.ANY)
DMA = pltpu.SemaphoreType.DMA


def sds(shape, dtype):
    return jax.ShapeDtypeStruct(shape, dtype)


class Spread:
    def __init__(self, view, size, sems):
        self.view, self.half = view, size // 2
        self.s1, self.r1, self.s2, self.r2, self.s3, self.r3, self.s4, self.r4, self.s5, self.r5 = sems
        b, c, k, _, _, z = place()
        x, y = c % 4, b // 4
        p = y % 2
        self.b, self.c, self.x, self.z = b, c, x, z
        self.start = (p * 2 + k) * size
        self.across = ((1 - p) * 2 + k) * size
        self.turn = (1 - 2 * k) * size
        self.core = (b + 1 - 2 * k, c)
        self.ups = [((b + 4) % L, c), ((b + 12) % L, c)]
        self.flips = [(b, (c + 4) % G), far_flip()]

    def send(self, g, start, size, ss, rs, dev):
        ref = self.view(g, start, size)
        copy = remote(ref, ref, ss, rs, dev)
        copy.start()

    def wait(self, g, start, size, rs):
        ref = self.view(g, start, size)
        remote(ref, ref, self.s1.at[0], rs, self.core).wait_recv()

    def from_x(self, i):
        return self.z * 4 + (self.x + 4 - i) % 4

    def from_z(self, i):
        return (1 - self.z) * 4 + (self.x + 4 - i) % 4

    def along_z(self, g):
        for h in range(2):
            at = self.start + h * self.half
            self.send(g, at, self.half, self.s2.at[h, g], self.r2.at[h, g], self.flips[h])

    def first(self):
        for i in (1, 3, 2):
            dev = (self.b, self.z * 4 + (self.x + i) % 4)
            self.send(self.c, self.start, 2 * self.half, self.s1.at[i], self.r1.at[self.c], dev)
        self.along_z(self.c)

    def fan(self, g, h):
        at = self.start + h * self.half
        self.send(g, at, self.half, self.s4.at[h, g], self.r4.at[h, g], self.ups[h])
        self.send(g, at, self.half, self.s3.at[h, g], self.r3.at[h, g], self.core)

    def relay_x(self, i):
        g = self.from_x(i)
        self.wait(g, self.start, 2 * self.half, self.r1.at[g])
        self.along_z(g)
        self.fan(g, 0)
        self.fan(g, 1)

    def relay_z(self, i):
        g = self.from_z(i)
        for h in range(2):
            self.wait(g, self.start + h * self.half, self.half, self.r2.at[h, g])
            self.fan(g, h)

    def relay_y(self, g):
        for h in range(2):
            at = self.across + h * self.half
            self.wait(g, at, self.half, self.r4.at[h, g])
            self.send(g, at, self.half, self.s5.at[h, g], self.r5.at[h, g], self.core)

    def ready(self, g):
        for h in range(2):
            self.wait(g, self.start + self.turn + h * self.half, self.half, self.r3.at[h, g])
            self.wait(g, self.across + self.turn + h * self.half, self.half, self.r5.at[h, g])

    def finish(self):
        def sent(g, start, size, sem):
            ref = self.view(g, start, size)
            remote(ref, ref, sem, self.r1.at[0], self.core).wait_send()

        half = self.half
        for i in (1, 3, 2):
            sent(self.c, self.start, 2 * half, self.s1.at[i])
        for i in range(4):
            row = self.from_x(i)
            for h in range(2):
                at = self.start + h * half
                sent(row, at, half, self.s2.at[h, row])
                for g in ([row] if i else []) + [self.from_z(i)]:
                    sent(g, at, half, self.s3.at[h, g])
                    sent(g, at, half, self.s4.at[h, g])
                    sent(g, self.across + h * half, half, self.s5.at[h, g])


def wide(ref, h):
    return jnp.concatenate([ref[h, g] for g in range(G)], axis=1)


def moments(x):
    mean = jnp.sum(x, axis=-1, keepdims=True) * (1.0 / D)
    centred = x - mean
    var = jnp.sum(centred * centred, axis=-1, keepdims=True) * (1.0 / D)
    inv = lax.rsqrt(var + EPSILON)
    return centred * inv, inv


def only(value, hh):
    first = lax.broadcasted_iota(jnp.int32, value.shape, 1) < HD
    keep = first if hh == 0 else jnp.logical_not(first)
    return jnp.where(keep, value, jnp.zeros_like(value))


def swap_rows(src, above, below, ss, rs):
    up, down, has_up, has_down = neighbours()
    to_up = remote(src, below, ss.at[0], rs.at[0], up)
    to_down = remote(src, above, ss.at[1], rs.at[1], down)

    def start():
        pl.when(has_up)(lambda: to_up.start())
        pl.when(has_down)(lambda: to_down.start())

    def wait():
        @pl.when(has_up)
        def _():
            to_up.wait_send()
            to_down.wait_recv()

        @pl.when(has_down)
        def _():
            to_down.wait_send()
            to_up.wait_recv()

    return start, wait


def loop(n, step):
    def wrapped(i, carry):
        step(i)
        return carry

    lax.fori_loop(0, n, wrapped, 0)


SCRATCH = dict(
    x_v=pltpu.VMEM((3, G, T, 128), BF),
    w_v=pltpu.VMEM((G, 3, D, 128), BF),
    o_v=pltpu.VMEM((G, 128, D), BF),
    d_v=pltpu.VMEM((G, VP, 128), BF),
    i_v=pltpu.VMEM((L, 16, 128), jnp.int32),
    itp=pltpu.VMEM((L, 16, 128, 128), BF),
    n_v=pltpu.VMEM((3 * T, D), BF),
    qkv=pltpu.VMEM((3, G, 3 * T, 128), BF),
    kt=pltpu.VMEM((G, 128, 3 * T), BF),
    mix=pltpu.VMEM((G, T, 128), BF),
    acc=pltpu.VMEM((T, D), F32),
    ml=pltpu.VMEM((2, 16, 1, T), F32),
    mlh=pltpu.VMEM((2, 2, 16, 1, T), F32),
    fields=pltpu.VMEM((G, VP, T), BF),
    mine=pltpu.VMEM((L, 16, 128), BF),
    picked=pltpu.VMEM((L, 16, 128), BF),
    am=pltpu.VMEM((L, 32, 128), BF),
    came=pltpu.VMEM((L, 32, 128), BF),
    parts=pltpu.VMEM((G, VP, T), BF),
    got=pltpu.VMEM((G, VP, T), BF),
    gf=pltpu.VMEM((3, VP, T), F32),
    gu=pltpu.VMEM((T, D), F32),
    do=pltpu.VMEM((G, 3 * T, 128), BF),
    dq=pltpu.VMEM((G, T, 128), BF),
    dso=pltpu.VMEM((G, T, 2 * T), BF),
    dp=pltpu.VMEM((2, 3 * T, T), F32),
    ds=pltpu.VMEM((2, 3 * T, T), BF),
    hat=pltpu.VMEM((T, D), F32),
    inv=pltpu.VMEM((T, 128), F32),
    p_own=pltpu.VMEM((16, 3 * T, T), F32),
    p_nb=pltpu.VMEM((2, 16, T, T), F32),
    delta=pltpu.VMEM((16, 1, T), F32),
    delta_h=pltpu.VMEM((2, 16, 1, T), F32),
    f_own=pltpu.VMEM((VP, T), BF),
    i_own=pltpu.VMEM((L, 16, 128), jnp.int32),
    loc=DMA((8,)),
    s_state=DMA((G,)), r_state=DMA((G,)),
    s_d=DMA((G,)), r_d=DMA((G,)),
    s_i=DMA((L,)), r_i=DMA((L,)),
    s_h=DMA((2, G)), r_h=DMA((2, G)),
    s_f=DMA((G,)), r_f=DMA((G,)),
    s_p=DMA((L,)), r_p=DMA((L,)),
    s_a=DMA((L,)), r_a=DMA((L,)),
    s_g=DMA((G,)), r_g=DMA((G,)),
    s_y=DMA((G,)), r_y=DMA((G,)),
    s_m=DMA((2,)), r_m=DMA((2,)),
    s_gh=DMA((2,)), r_gh=DMA((2,)),
    s_dl=DMA((2, 2)), r_dl=DMA((2, 2)),
    w1=DMA((4,)), w2=DMA((G,)), w3=DMA((2, G)), w4=DMA((2, G)), w5=DMA((2, G)), w6=DMA((2, G)), w7=DMA((2, G)), w8=DMA((2, G)), w9=DMA((2, G)), w10=DMA((2, G)),
    o1=DMA((4,)), o2=DMA((G,)), o3=DMA((2, G)), o4=DMA((2, G)), o5=DMA((2, G)), o6=DMA((2, G)), o7=DMA((2, G)), o8=DMA((2, G)), o9=DMA((2, G)), o10=DMA((2, G)),
)


class Refs:
    pass


def kernel(state, wq, wk, wv, wo, dec, idx, gain, interp, obs, count, misfit, back, *scratch):
    s = Refs()
    for name, ref in zip(SCRATCH, scratch):
        setattr(s, name, ref)
    b, c, k, big, row8, w = place()
    r = row8 % 4
    band = 2 * big + row8 // 4
    j_own = r * 2 + w
    home = band == b
    up, down, has_up, has_down = neighbours()
    up_bias = jnp.where(has_up, 0.0, -BIG).astype(F32)
    down_bias = jnp.where(has_down, 0.0, -BIG).astype(F32)
    own_rows = pl.ds(0, T)
    eighth = jnp.asarray(0.125, BF)
    away = jnp.logical_not(home)
    windows = [holder(big, 4 * k + j // 2, j % 2) for j in range(G)]
    mine_at = [jnp.logical_and(home, j_own == j) for j in range(G)]
    members = [(band, (c + i) % G) for i in range(G)]

    met = greeted()
    local = [
        pltpu.make_async_copy(wq, s.w_v.at[c, 0], s.loc.at[0]),
        pltpu.make_async_copy(wk, s.w_v.at[c, 1], s.loc.at[1]),
        pltpu.make_async_copy(wv, s.w_v.at[c, 2], s.loc.at[2]),
        pltpu.make_async_copy(wo, s.o_v.at[c], s.loc.at[3]),
    ]
    for copy in local:
        copy.start()

    @pl.when(jnp.logical_not(has_up))
    def _():
        s.x_v[0] = jnp.zeros((G, T, 128), BF)

    @pl.when(jnp.logical_not(has_down))
    def _():
        s.x_v[2] = jnp.zeros((G, T, 128), BF)

    s.mlh[:, 0] = jnp.full((2, 16, 1, T), BIG, F32)
    s.mlh[:, 1] = jnp.zeros((2, 16, 1, T), F32)
    s.delta_h[...] = jnp.zeros_like(s.delta_h)
    s.gf[...] = jnp.zeros_like(s.gf)
    eye = lax.broadcasted_iota(jnp.int32, (VP, VARS), 0) == lax.broadcasted_iota(jnp.int32, (VP, VARS), 1)
    s.d_v[c] = nn(eye.astype(F32).astype(BF), dec[...]).astype(BF)
    for n in range(16):
        s.i_own[:, n, :] = jnp.broadcast_to(idx[:, n : n + 1], (L, 128))
    s.i_v[b] = s.i_own[b]
    met()

    sends = []

    def send_state(j, act):
        src = state.at[j // 2, pl.ds((j % 2) * T, T)]

        @pl.when(jnp.logical_not(mine_at[j]))
        def _():
            copy = remote(src, s.x_v.at[1, c], s.s_state.at[j], s.r_state.at[c], windows[j])
            copy.start() if act else copy.wait_send()

        if act:
            @pl.when(mine_at[j])
            def _():
                pltpu.make_async_copy(src, s.x_v.at[1, c], s.loc.at[4]).start()

    for j in range(G):
        send_state(j, True)
    weights = Spread(
        lambda g, at, n: s.w_v.at[g, :, pl.ds(at, n)], 256, (s.w1, s.w2, s.w3, s.w4, s.w5, s.w6, s.w7, s.w8, s.w9, s.w10)
    )
    outs = Spread(
        lambda g, at, n: s.o_v.at[g, pl.ds(at, n)], 32, (s.o1, s.o2, s.o3, s.o4, s.o5, s.o6, s.o7, s.o8, s.o9, s.o10)
    )
    for copy in local[:3]:
        copy.wait()
    weights.first()
    fetch = pltpu.make_async_copy(interp, s.itp, s.loc.at[5])
    fetch.start()
    for i in range(1, L):
        dev = lat_peer(i)
        copy = remote(s.i_own.at[dev[0]], s.i_v.at[b], s.s_i.at[i], s.r_i.at[i], dev)
        copy.start()
        sends.append(copy)

    def halo(g, sem):
        to_up = remote(s.x_v.at[1, g], s.x_v.at[2, g], s.s_h.at[0, sem], s.r_h.at[0, sem], up)
        to_down = remote(s.x_v.at[1, g], s.x_v.at[0, g], s.s_h.at[1, sem], s.r_h.at[1, sem], down)
        return to_up, to_down

    def start_halo(g, sem):
        to_up, to_down = halo(g, sem)
        pl.when(has_up)(lambda: to_up.start())
        pl.when(has_down)(lambda: to_down.start())

    def got_state(g):
        piece = s.x_v.at[1, g]
        remote(piece, piece, s.s_state.at[0], s.r_state.at[g], members[1]).wait_recv()

    @pl.when(home)
    def _():
        pltpu.make_async_copy(state.at[0, pl.ds(0, T)], s.x_v.at[1, c], s.loc.at[4]).wait()

    pl.when(away)(lambda: got_state(c))
    start_halo(c, 0)
    for i in (1, 3, 4, 5, 7, 2, 6):
        g = (c + i) % G
        got_state(g)
        start_halo(g, i)
    weights.relay_z(0)
    for i in (1, 3, 2):
        weights.relay_x(i)
    local[3].wait()
    outs.first()
    for i in range(1, G):
        copy = remote(s.d_v.at[c], s.d_v.at[c], s.s_d.at[i], s.r_d.at[i], (b, (c + i) % G))
        copy.start()
        sends.append(copy)

    def norm(h, at):
        hat, inv = moments(wide(s.x_v, h).astype(F32))
        if h == 1:
            s.hat[...] = hat
            s.inv[...] = jnp.broadcast_to(inv, (T, 128))
        s.n_v[pl.ds(at * T, T), :] = (hat * gain[...]).astype(BF)

    norm(1, 0)
    weights.relay_y(weights.from_z(0))
    weights.relay_y(weights.from_x(1))
    weights.relay_y(weights.from_x(3))
    for i in range(G):
        to_up, to_down = halo((c + i) % G, i)
        pl.when(has_down)(lambda: to_up.wait_recv())
        pl.when(has_up)(lambda: to_down.wait_recv())
    norm(0, 1)
    norm(2, 2)
    weights.relay_z(1)
    weights.relay_y(weights.from_x(2))
    weights.relay_z(3)

    def attend(i):
        t = (i + 1) % 3
        late = (i >= 2).astype(jnp.int32)
        over = (i >= 5).astype(jnp.int32) + (i == 1).astype(jnp.int32)
        back_by = late * (1 + t * (7 - 3 * t) // 2)
        g = (w + over * (1 - 2 * w)) * 4 + (c % 4 + 4 - back_by) % 4

        def relays(n):
            return pl.when(i == n)

        pl.when(i > 0)(lambda: weights.ready(g))

        @relays(1)
        def _():
            weights.relay_z(2)
            weights.relay_y(weights.from_z(1))

        @relays(2)
        def _():
            weights.relay_y(weights.from_z(3))

        @relays(3)
        def _():
            weights.relay_y(weights.from_z(2))
            outs.relay_z(0)
            for n in (1, 3, 2):
                outs.relay_x(n)

        @relays(5)
        def _():
            for n in (1, 3, 2):
                outs.relay_z(n)
            outs.relay_y(outs.from_z(0))
            for n in (1, 3, 2):
                outs.relay_y(outs.from_x(n))

        @relays(7)
        def _():
            for n in (1, 3, 2):
                outs.relay_y(outs.from_z(n))

        own_res = nn(s.n_v[:T, :], jnp.concatenate([s.w_v[g, n] for n in range(3)], axis=1))
        near_res = nn(s.n_v[T:, :], jnp.concatenate([s.w_v[g, 1], s.w_v[g, 2]], axis=1))
        for n in range(3):
            s.qkv[n, g, :T, :] = own_res[:, n * 128 : (n + 1) * 128].astype(BF)
        for n in range(2):
            s.qkv[n + 1, g, T:, :] = near_res[:, n * 128 : (n + 1) * 128].astype(BF)
        vt = jnp.transpose(jnp.concatenate([own_res[:, 256:], near_res[:, 128:]], axis=0)).astype(BF)
        query = s.qkv[0, g, own_rows, :] * eighth
        scores = [nt(s.qkv[1, g], only(query, hh)) for hh in range(2)]
        parts = []
        for hh in range(2):
            n = 2 * g + hh
            sc = scores[hh]
            m0 = jnp.max(sc[:T], axis=0, keepdims=True)
            m1 = jnp.max(sc[T : 2 * T], axis=0, keepdims=True) + up_bias
            m2 = jnp.max(sc[2 * T :], axis=0, keepdims=True) + down_bias
            m = jnp.maximum(jnp.maximum(m0, m1), m2)
            e0 = jnp.exp(sc[:T] - m)
            e1 = jnp.exp(sc[T : 2 * T] - (m - up_bias))
            e2 = jnp.exp(sc[2 * T :] - (m - down_bias))
            l = jnp.sum(e0, axis=0, keepdims=True) + jnp.sum(e1, axis=0, keepdims=True) + jnp.sum(e2, axis=0, keepdims=True)
            inv = 1.0 / l
            s.p_own[n, :T, :] = e0 * inv
            s.p_own[n, T : 2 * T, :] = e1 * inv
            s.p_own[n, 2 * T :, :] = e2 * inv
            p = s.p_own[n].astype(BF)
            parts.append(nn(vt[hh * HD : (hh + 1) * HD], p))
            s.ml[0, n] = m
            s.ml[1, n] = inv
        s.mix[g] = jnp.transpose(jnp.concatenate(parts, axis=0)).astype(BF)

    loop(G, attend)
    start_ml, wait_ml = swap_rows(s.ml, s.mlh.at[0], s.mlh.at[1], s.s_m, s.r_m)
    start_ml()
    for n in range(4):
        if n:
            outs.ready(outs.from_x(n))
        outs.ready(outs.from_z(n))
    for i in range(1, G):
        remote(s.d_v.at[c], s.d_v.at[c], s.s_d.at[i], s.r_d.at[i], members[i]).wait_recv()
    def out(m):
        cols = pl.ds(pl.multiple_of(m * 256, 256), 256)
        total = nn(s.mix[0], s.o_v[0, :, cols]).astype(BF).astype(F32)
        for g in range(1, G):
            total = total + nn(s.mix[g], s.o_v[g, :, cols]).astype(BF).astype(F32)
        s.acc[:, cols] = total

    loop(4, out)
    updated = (wide(s.x_v, 1).astype(F32) + s.acc[...]).astype(BF)
    dec_all = jnp.concatenate([s.d_v[g] for g in range(G)], axis=1)
    s.f_own[...] = nt(dec_all, updated).astype(BF)

    def send_fields(i, act):
        copy = remote(s.f_own, s.fields.at[j_own], s.s_f.at[i], s.r_f.at[j_own], members[i])
        copy.start() if act else copy.wait_send()

    for i in (2, 6, 1, 3, 5, 7, 4):
        send_fields(i, True)
    pl.when(away)(lambda: send_fields(0, True))

    @pl.when(home)
    def _():
        s.fields[j_own] = s.f_own[...]

    for i in range(1, L):
        remote(s.i_own.at[b], s.i_v.at[b], s.s_i.at[i], s.r_i.at[i], lat_peer(i)).wait_recv()
    index = s.i_v[...].reshape(16 * L, 128)
    lanes = lax.broadcasted_iota(jnp.int32, (16 * L, 128), 1) * 16

    total = jnp.zeros((16 * L, 128), F32)
    for j in range(G):
        @pl.when(jnp.logical_not(mine_at[j]))
        def _():
            remote(s.f_own, s.fields.at[j], s.s_f.at[0], s.r_f.at[j], windows[j]).wait_recv()

        for half in range(2):
            hot = (index == lanes + (2 * j + half)).astype(F32).astype(BF)
            total = total + nn(hot[:, :VP], s.fields[j, :, pl.ds(half * 128, 128)])
    s.mine[...] = total.astype(BF).reshape(L, 16, 128)
    for i in range(1, L):
        dev = lat_peer(i)
        copy = remote(s.mine.at[dev[0]], s.picked.at[b], s.s_p.at[i], s.r_p.at[i], dev)
        copy.start()
        sends.append(copy)
    s.picked[b] = s.mine[b]

    wait_ml()

    def near(g):
        s.kt[g] = jnp.transpose(s.qkv[1, g].astype(F32)).astype(BF)
        for side in range(2):
            query = s.qkv[0, g, pl.ds((1 + side) * T, T), :] * eighth
            for hh in range(2):
                n = 2 * g + hh
                sc = nt(s.qkv[1, g, own_rows, :], only(query, hh))
                s.p_nb[side, n] = jnp.exp(sc - s.mlh[side, 0, n]) * s.mlh[side, 1, n]

    def near_queries(m):
        both = nn(s.n_v[T:, :], jnp.concatenate([s.w_v[2 * m, 0], s.w_v[2 * m + 1, 0]], axis=1)).astype(BF)
        s.qkv[0, 2 * m, T:, :] = both[:, :128]
        s.qkv[0, 2 * m + 1, T:, :] = both[:, 128:]

    loop(2, near_queries)
    loop(4, near)

    fetch.wait()
    row = lax.broadcasted_iota(jnp.int32, (16, 128), 0)

    def observe(i):
        other_b = (b + L - i) % L

        @pl.when(i > 0)
        def _():
            remote(s.mine.at[b], s.picked.at[b], s.s_p.at[i], s.r_p.at[i], (other_b, c)).wait_recv()

        flat = s.itp[other_b].reshape(2048, 128)
        big = nt(s.picked[other_b], flat)
        pred = jnp.zeros((16, 128), F32)
        for n in range(16):
            pred = jnp.where(row == n, big[:, n * 128 : (n + 1) * 128], pred)
        mis = jnp.where(row < count[other_b], pred - obs[other_b].astype(F32), 0.0).astype(BF)
        lhs = jnp.concatenate([jnp.where(row == n, mis, jnp.zeros_like(mis)) for n in range(16)], axis=1)
        s.am[other_b, :16, :] = nn(lhs, flat).astype(BF)
        s.am[other_b, 16:, :] = mis

        @pl.when(i > 0)
        def _():
            remote(s.am.at[other_b], s.came.at[b], s.s_a.at[i], s.r_a.at[i], (other_b, c)).start()

    loop(L, observe)
    s.came[b] = s.am[b]

    loop(2, lambda m: near_queries(m + 2))
    loop(4, lambda g: near(g + 4))

    index_t = jnp.transpose(index.astype(F32))[:VP].astype(jnp.int32)
    sub = lax.broadcasted_iota(jnp.int32, (VP, 16 * L), 0) * 16

    def arrived(i):
        other_b = (b + i) % L

        @pl.when(i > 0)
        def _():
            remote(s.am.at[b], s.came.at[b], s.s_a.at[i], s.r_a.at[i], (other_b, c)).wait()

    loop(L, arrived)
    misfit[...] = s.came[:, 16:, :]
    adjoint = s.came[:, :16, :].reshape(16 * L, 128)
    for j in range(G):
        for half in range(2):
            hot = (index_t == sub + (2 * j + half)).astype(F32).astype(BF)
            s.parts[j, :, pl.ds(half * 128, 128)] = nn(hot, adjoint).astype(BF)

        @pl.when(jnp.logical_not(mine_at[j]))
        def _():
            remote(s.parts.at[j], s.got.at[c], s.s_g.at[j], s.r_g.at[c], windows[j]).start()

        @pl.when(mine_at[j])
        def _():
            s.got[c] = s.parts[j]

    def got_part(g):
        remote(s.parts.at[0], s.got.at[g], s.s_g.at[0], s.r_g.at[g], members[1]).wait_recv()

    pl.when(away)(lambda: got_part(c))
    total = s.got[c].astype(F32)
    for i in range(1, G):
        got_part((c + i) % G)
        total = total + s.got[(c + i) % G].astype(F32)
    s.gf[0] = total
    start_gf, wait_gf = swap_rows(s.gf.at[0], s.gf.at[1], s.gf.at[2], s.s_gh, s.r_gh)
    start_gf()

    dec_all = jnp.concatenate([dec_all, jnp.zeros((128 - VP, D), BF)], axis=0)
    dec3 = jnp.concatenate([dec_all, dec_all, dec_all], axis=0)

    def update_of(h):
        field = jnp.transpose(jnp.concatenate([s.gf[h], jnp.zeros((128 - VP, T), F32)], axis=0))
        hi = field.astype(BF)
        rest = field - hi.astype(F32)
        mid = rest.astype(BF)
        lo = (rest - mid.astype(F32)).astype(BF)
        update = nn(jnp.concatenate([hi, mid, lo], axis=1), dec3)
        s.n_v[pl.ds(h * T, T), :] = update.astype(BF)
        return update

    def mixed(rows, n):
        def step(m):
            weight = jnp.concatenate([s.o_v[2 * m], s.o_v[2 * m + 1]], axis=0)
            res = nt(s.n_v[pl.ds(rows, n), :], weight).astype(BF)
            s.do[2 * m, pl.ds(rows, n), :] = res[:, :128]
            s.do[2 * m + 1, pl.ds(rows, n), :] = res[:, 128:]

        return step

    def own(g):
        for hh in range(2):
            s.dp[hh] = nt(s.qkv[2, g], only(s.do[g, own_rows, :], hh))
        parts = []
        for hh in range(2):
            n = 2 * g + hh
            along = jnp.zeros((8, T), F32)
            for at in range(0, 3 * T, 64):
                product = s.p_own[n, at : at + 64, :] * s.dp[hh, at : at + 64, :]
                along = along + jnp.sum(product.reshape(8, 8, T), axis=0)
            along = jnp.sum(along, axis=0, keepdims=True)
            s.delta[n] = along
            for at in range(0, 3 * T, 64):
                spread = s.p_own[n, at : at + 64, :] * (s.dp[hh, at : at + 64, :] - along)
                s.ds[hh, at : at + 64, :] = spread.astype(BF)
            parts.append(nn(s.kt[g, pl.ds(hh * HD, HD), :], s.ds[hh]) * 0.125)
            s.dso[g, :, pl.ds(hh * T, T)] = s.ds[hh, :T, :]
        s.dq[g] = jnp.transpose(jnp.concatenate(parts, axis=0)).astype(BF)

    def other(g):
        scores, probs, queries, grads = [s.dso[g]], [], [], []
        for hh in range(2):
            probs.append(s.p_own[2 * g + hh, :T, :].astype(BF))
            queries.append(only(s.qkv[0, g, own_rows, :] * eighth, hh))
            grads.append(only(s.do[g, own_rows, :], hh))
        for side in range(2):
            rows = pl.ds((1 + side) * T, T)
            for hh in range(2):
                n = 2 * g + hh
                queries.append(only(s.qkv[0, g, rows, :] * eighth, hh))
                grads.append(only(s.do[g, rows, :], hh))
                dp = nt(s.qkv[2, g, own_rows, :], grads[-1])
                p = s.p_nb[side, n]
                scores.append((p * (dp - s.delta_h[side, n])).astype(BF))
                probs.append(p.astype(BF))
        dk = nn(jnp.concatenate(scores, axis=1), jnp.concatenate(queries, axis=0))
        dv = nn(jnp.concatenate(probs, axis=1), jnp.concatenate(grads, axis=0))
        three = jnp.concatenate([s.dq[g], dk.astype(BF), dv.astype(BF)], axis=1)
        wide_w = jnp.concatenate([s.w_v[g, 0], s.w_v[g, 1], s.w_v[g, 2]], axis=1)
        s.acc[...] += nt(three, wide_w).astype(BF).astype(F32)

    s.gu[...] = update_of(0)
    loop(G // 2, mixed(0, T))
    swaps = []
    for n in range(2):
        loop(4, lambda g: own(g + 4 * n))
        heads = pl.ds(8 * n, 8)
        start, wait = swap_rows(
            s.delta.at[heads], s.delta_h.at[0, heads], s.delta_h.at[1, heads], s.s_dl.at[n], s.r_dl.at[n]
        )
        start()
        swaps.append(wait)
    wait_gf()
    update_of(1)
    update_of(2)
    loop(G // 2, mixed(T, 2 * T))
    s.acc[...] = jnp.zeros_like(s.acc)
    for n in range(2):
        swaps[n]()
        loop(4, lambda g: other(g + 4 * n))

    hat, inv = s.hat[...], s.inv[:, :1]
    grad_hat = s.acc[...] * gain[...]
    mean = jnp.sum(grad_hat, axis=-1, keepdims=True) * (1.0 / D)
    cross = jnp.sum(grad_hat * hat, axis=-1, keepdims=True) * (1.0 / D)
    total = (s.gu[...] + (grad_hat - mean - hat * cross) * inv).astype(BF)
    for g in range(G):
        s.mix[g] = total[:, g * 128 : (g + 1) * 128]
    def send_back(i, act):
        dev = members[i]
        copy = remote(s.mix.at[dev[1]], back.at[r, pl.ds(w * T, T)], s.s_y.at[i], s.r_y.at[j_own], dev)
        copy.start() if act else copy.wait_send()

    for i in (2, 6, 1, 3, 5, 7, 4):
        send_back(i, True)
    pl.when(away)(lambda: send_back(0, True))

    @pl.when(home)
    def _():
        back[r, pl.ds(w * T, T), :] = s.mix[c]

    weights.finish()
    outs.finish()
    for copy in sends:
        copy.wait_send()
    for i in range(G):
        to_up, to_down = halo((c + i) % G, i)
        pl.when(has_up)(lambda: to_up.wait_send())
        pl.when(has_down)(lambda: to_down.wait_send())
    for i in range(1, G):
        send_fields(i, False)
        send_back(i, False)

    @pl.when(away)
    def _():
        send_fields(0, False)
        send_back(0, False)

    for j in range(G):
        send_state(j, False)

        @pl.when(jnp.logical_not(mine_at[j]))
        def _():
            remote(s.parts.at[j], s.got.at[c], s.s_g.at[j], s.r_g.at[c], windows[j]).wait_send()
            piece = back.at[j // 2, pl.ds((j % 2) * T, T)]
            remote(s.mix.at[0], piece, s.s_y.at[0], s.r_y.at[j], windows[j]).wait_recv()


def finish_kernel(low, back, state, background, misfit, gradient):
    misfit[...] = low[...].astype(F32)
    gradient[...] = state[...].astype(F32) - background[...].astype(F32) + back[...].astype(F32)


def body(state, background, gain, w_query, w_key, w_value, w_out, decoder, interp, obs_values, tile_index, block_count):
    smem = pl.BlockSpec(memory_space=pltpu.SMEM)
    misfit, back = call(
        kernel,
        (sds((L, 16, 128), BF), sds((4, 512, 128), BF)),
        [ANY] * 5 + [VM, VM, VM, ANY, VM, smem],
        [VM] * 2,
        list(SCRATCH.values()),
        0,
        "whole",
        (
            state, w_query, w_key, w_value, w_out, jnp.transpose(decoder), tile_index.reshape(L, 16), gain.reshape(1, D),
            interp.reshape(L, 16, 128, 128), obs_values.reshape(L, 16, 128), block_count.reshape(L),
        ),
    )
    row = pl.BlockSpec((2, 512, 128), lambda i: (i, 0, 0))
    part = pl.BlockSpec((8, 16, 128), lambda i: (i, 0, 0))
    misfit, gradient = pl.pallas_call(
        finish_kernel,
        grid=(2,),
        out_shape=(sds((L, 16, 128), F32), sds((4, 512, 128), F32)),
        in_specs=[part, row, row, row],
        out_specs=(part, row),
        name="finish",
    )(misfit, back, state, background)
    return misfit.reshape(L, 1, 1, 16, 128), gradient


def solution(mesh):
    return jax.shard_map(
        body,
        mesh=mesh,
        in_specs=(
            P("lat", None, "chan"),
            P("lat", None, "chan"),
            P(),
            P(None, "chan"),
            P(None, "chan"),
            P(None, "chan"),
            P("chan", None),
            P("chan", None),
            P("lat", "chan", None, None, None, None),
            P("lat", "chan", None, None, None),
            P("lat", "chan", None, None),
            P("lat", "chan", None),
        ),
        out_specs=(P(None, "chan", "lat", None, None), P("lat", None, "chan")),
        check_vma=False,
    )
```
